32 devices in a mesh: cand: 4 (over x, core), seq: 8 (over z, y).
Axes of the slice: x: 2, y: 2, z: 4, core: 2. Of those that a mesh axis runs over, the one named last changes fastest.
Arguments:
- latent: bfloat16 [4, 384, 3072], P('cand', 'seq'), may hold values from -0.59765625 to 0.59765625
- timesteps: int32 [4], replicated, may hold values from 0 to 999
- positions: int32 [3, 384], replicated, may hold values from 0 to 63
- mod_weight: bfloat16 [3072, 9216], P('cand', 'seq'), may hold values from -0.109375 to 0.109375
- input_weight: bfloat16 [3072, 16, 384], P('cand', 'seq'), may hold values from -0.109375 to 0.109375
- output_weight: bfloat16 [16, 128, 3072], P('seq', None, 'cand'), may hold values from -0.75 to 0.75
- cotangent: bfloat16 [4, 384, 3072], P('cand', 'seq'), may hold values from -6 to 6
Outputs:
- block_out: bfloat16 [4, 384, 3072], P('cand', 'seq')
- latent_grad: float32 [4, 384, 3072], P('cand', 'seq')
The draws below stay inside these ranges and needn't reach their ends.
All inputs are finite; a program needn't handle non-finite values.
Results may differ from the reference program's by a relative error of at most 0.033.
Values may be sent and summed in bfloat16 or wider, within the bound.
A program may use at most 128 MiB of HBM per device.

```python
import jax
import jax.numpy as jnp
import numpy as np
from jax import lax

D = 3072
HEADS = 16
HEAD = 128
LEN = 384
CANDS = 4
GROUP = 2
ATT_WIDTH = 2048
N_SEQ = 8


def with_ends(drawn, stream_key, low, top_value):
    extent = drawn.shape
    place = [jax.random.randint(jax.random.fold_in(stream_key, axis), (), 0, extent[axis]) for axis in range(len(extent))]
    drawn = drawn.at[tuple(place)].set(low)
    longest = extent.index(max(extent))
    place[longest] = (place[longest] + 1) % extent[longest]
    return drawn.at[tuple(place)].set(top_value)


def levels(rng, shape, shards, low, largest):
    def one(axis_at, blocks):
        steps = jax.random.uniform(jax.random.fold_in(jax.random.fold_in(rng, 6), axis_at), (blocks,), jnp.float32, low / len(shards), largest / len(shards))
        return jnp.repeat(jnp.exp(steps), shape[axis_at] // blocks).reshape((-1,) + (1,) * (len(shape) - axis_at - 1))

    loudness = one(*shards[0])
    for cut in shards[1:]:
        loudness = loudness * one(*cut)
    return loudness


def scatter_about(key, extent, spread, bound, cuts=(), kind=jnp.bfloat16):
    loudness = levels(key, extent, cuts, -0.22, 0.18) if cuts else 1.0
    entries = jax.random.normal(key, extent, jnp.float32) * spread * loudness
    return jnp.minimum(jnp.maximum(entries, -bound), bound).astype(kind)


def setup_inputs(seed: int = 0) -> dict:
    arg_keys = jax.random.split(jax.random.key(seed), 8)
    return {
        "latent": scatter_about(arg_keys[0], (CANDS, LEN, D), 0.1, 0.59765625, ((0, 4), (1, 8))),
        "timesteps": with_ends(jax.random.randint(arg_keys[1], (CANDS,), 0, 1000), jax.random.fold_in(arg_keys[1], 1), 0, 999).astype(jnp.int32),
        "positions": with_ends(jax.random.randint(arg_keys[2], (3, LEN), 0, 64), jax.random.fold_in(arg_keys[2], 1), 0, 63).astype(jnp.int32),
        "mod_weight": scatter_about(arg_keys[3], (D, 3 * D), D ** -0.5, 0.109375, ((0, 4), (1, 8))),
        "input_weight": scatter_about(arg_keys[4], (D, HEADS, 3 * HEAD), D ** -0.5, 0.109375, ((0, 4), (1, 8))),
        "output_weight": scatter_about(arg_keys[5], (HEADS, HEAD, D), (ATT_WIDTH // 32) ** -0.5, 0.75, ((0, 8), (2, 4))),
        "cotangent": scatter_about(arg_keys[6], (CANDS, LEN, D), 1.0, 6.0, ((0, 4), (1, 8))),
    }


epsilon = 1e-06

def time_embed(timesteps, feature_width):
    half_size = feature_width // 2
    freq_rate = jnp.exp(-jnp.log(10000.0) * jnp.arange(half_size, dtype=jnp.float32) / half_size)
    angles = timesteps.astype(jnp.float32)[:, None] * freq_rate[None, :]
    return jnp.concatenate([jnp.cos(angles), jnp.sin(angles)], axis=1)

def rope_tables(positions, head_size):
    first_size = head_size // 8
    other_size = (head_size - first_size) // 2
    pieces = []
    swapped = []
    sign_vec = []
    offset = 0
    for axis_id, width_part in enumerate((first_size, other_size, other_size)):
        half_size = width_part // 2
        freq_rate = jnp.exp(-jnp.log(256.0) * 2.0 * jnp.arange(half_size, dtype=jnp.float32) / width_part)
        angle_part = positions[axis_id].astype(jnp.float32)[:, None] * freq_rate[None, :]
        pieces.append(angle_part)
        pieces.append(angle_part)
        swapped += list(range(offset + half_size, offset + width_part)) + list(range(offset, offset + half_size))
        sign_vec += [-1.0] * half_size + [1.0] * half_size
        offset += width_part
    angles = jnp.concatenate(pieces, axis=1)
    return (jnp.cos(angles), jnp.sin(angles), np.array(swapped, np.int32), np.array(sign_vec, np.float32))

def rotate(values, tables):
    cos_tab, sin_tab, swapped, sign_vec = tables
    return values * cos_tab + values[..., swapped] * sign_vec * sin_tab

def unrotate(values, tables):
    cos_tab, sin_tab, swapped, sign_vec = tables
    return values * cos_tab - (values * sin_tab)[..., swapped] * sign_vec

def rms_norm(values):
    inverse = lax.rsqrt(lax.optimization_barrier(jnp.mean(values * values, -1, keepdims=True)) + epsilon)
    return (values * inverse, inverse)

def rms_back(d_normed, normed, inverse):
    return inverse * (d_normed - normed * lax.optimization_barrier(jnp.mean(d_normed * normed, -1, keepdims=True)))

def layer_norm(values):
    centred = values - lax.optimization_barrier(jnp.mean(values, -1, keepdims=True))
    inverse_std = lax.rsqrt(lax.optimization_barrier(jnp.mean(centred * centred, -1, keepdims=True)) + epsilon)
    return (centred * inverse_std, inverse_std)

def layer_norm_back(d_normed, normed, inverse_std):
    return inverse_std * (d_normed - lax.optimization_barrier(jnp.mean(d_normed, -1, keepdims=True)) - normed * lax.optimization_barrier(jnp.mean(d_normed * normed, -1, keepdims=True)))

def attend(projected, tables):
    length, groups, triple = projected.shape
    head_size = triple // 3
    grouped = jnp.transpose(projected.reshape(length, groups, 3, head_size), (2, 1, 0, 3))
    query_n, query_inv = rms_norm(grouped[0])
    key_n, key_inv = rms_norm(grouped[1])
    q_rot = rotate(query_n, tables).astype(jnp.bfloat16)
    k_rot = rotate(key_n, tables).astype(jnp.bfloat16)
    values = grouped[2].astype(jnp.bfloat16)
    score_scale = head_size ** (-0.5)
    scores = jnp.einsum('gld,gmd->glm', q_rot.astype(jnp.float32), k_rot.astype(jnp.float32)) * score_scale
    weights = jnp.exp(scores - head_size ** 0.5)
    probs = weights / lax.optimization_barrier(jnp.sum(weights, -1, keepdims=True))
    probs_low = probs.astype(jnp.bfloat16)
    heads_out = jnp.einsum('glm,gmd->gld', probs_low.astype(jnp.float32), values.astype(jnp.float32))
    attended = jnp.transpose(heads_out, (1, 0, 2)).reshape(length, groups * head_size).astype(jnp.bfloat16)
    saved = (q_rot, k_rot, values, probs, probs_low, query_n, query_inv, key_n, key_inv)
    return (attended, saved)

def attend_back(d_attended, saved, tables):
    q_rot, k_rot, values, probs, probs_low, query_n, query_inv, key_n, key_inv = saved
    groups, length, head_size = q_rot.shape
    score_scale = head_size ** (-0.5)
    d_heads = jnp.transpose(d_attended.reshape(length, groups, head_size), (1, 0, 2)).astype(jnp.float32)
    d_values = jnp.einsum('glm,gld->gmd', probs_low.astype(jnp.float32), d_heads)
    d_probs = jnp.einsum('gld,gmd->glm', d_heads, values.astype(jnp.float32))
    d_scores = (probs * (d_probs - lax.optimization_barrier(jnp.sum(probs * d_probs, -1, keepdims=True)))).astype(jnp.bfloat16)
    d_qrot = jnp.einsum('glm,gmd->gld', d_scores.astype(jnp.float32), k_rot.astype(jnp.float32)) * score_scale
    d_krot = jnp.einsum('glm,gld->gmd', d_scores.astype(jnp.float32), q_rot.astype(jnp.float32)) * score_scale
    d_query = rms_back(unrotate(d_qrot, tables), query_n, query_inv)
    d_key = rms_back(unrotate(d_krot, tables), key_n, key_inv)
    stacked = jnp.stack([d_query, d_key, d_values], 0)
    return jnp.transpose(stacked, (2, 1, 0, 3)).reshape(length, groups * 3 * head_size).astype(jnp.bfloat16)

def reference(latent, timesteps, positions, mod_weight, input_weight, output_weight, cotangent):
    time_act = jax.nn.silu(time_embed(timesteps, D)).astype(jnp.bfloat16)
    modulation = jnp.dot(time_act, mod_weight, preferred_element_type=jnp.float32)
    tables = rope_tables(positions, HEAD)
    flat_in = input_weight.reshape(D, HEADS * 3 * HEAD)
    flat_out = output_weight.reshape(HEADS * HEAD, D)
    group_in = jnp.transpose(input_weight.reshape(D, N_SEQ, GROUP * 3 * HEAD), (1, 0, 2))

    def one_candidate(items):
        latent_one, mod_one, cot_one = items
        shift_vec = mod_one[:D]
        scale_vec = mod_one[D:2 * D]
        gate_vec = mod_one[2 * D:]
        normed, inverse_std = layer_norm(latent_one.astype(jnp.float32))
        modulated = (normed * (1.0 + scale_vec) + shift_vec).astype(jnp.bfloat16)
        projected = jnp.dot(modulated, flat_in, preferred_element_type=jnp.float32)
        attended, saved = attend(projected.reshape(LEN, HEADS, 3 * HEAD), tables)
        mixed = jnp.dot(attended, flat_out, preferred_element_type=jnp.float32)
        block_one = (latent_one.astype(jnp.float32) + gate_vec * mixed).astype(jnp.bfloat16)
        d_mixed = (cot_one.astype(jnp.float32) * gate_vec).astype(jnp.bfloat16)
        d_attended = lax.dot_general(d_mixed, flat_out, (((1,), (1,)), ((), ())), preferred_element_type=jnp.float32).astype(jnp.bfloat16)
        d_projected = attend_back(d_attended, saved, tables)
        d_groups = jnp.transpose(d_projected.reshape(LEN, N_SEQ, GROUP * 3 * HEAD), (1, 0, 2))

        def add_group(total, pieces):
            d_part, w_part = pieces
            partial_sum = lax.dot_general(d_part, w_part, (((1,), (1,)), ((), ())), preferred_element_type=jnp.float32)
            rounded = lax.optimization_barrier(partial_sum.astype(jnp.bfloat16))
            return (total + rounded.astype(jnp.float32), None)
        d_modulated, _unused = lax.scan(add_group, jnp.zeros((LEN, D), jnp.float32), (d_groups, group_in))
        grad_one = cot_one.astype(jnp.float32) + layer_norm_back(d_modulated * (1.0 + scale_vec), normed, inverse_std)
        return (block_one, grad_one)
    block_out, latent_grad = lax.map(one_candidate, (latent, modulation, cotangent))
    return (block_out, latent_grad)
```

```python
import functools
import math

import jax
import jax.numpy as jnp
from jax import lax
from jax.experimental import pallas as pl
from jax.experimental.pallas import tpu as pltpu
from jax.sharding import PartitionSpec as P

HEAD = 128
CHUNKS = 4
PARTS = 3
SLABS = 4
MESH = pl.DeviceIdType.MESH


epsilon = 1e-06


def swap_pairs(values):
    lane = lax.broadcasted_iota(jnp.int32, values.shape, 1)
    small = HEAD // 8
    large = (HEAD - small) // 2
    near = jnp.where(
        lane < small // 2,
        pltpu.roll(values, HEAD - small // 2, 1),
        pltpu.roll(values, small // 2, 1),
    )
    upper = ((lane >= small) & (lane < small + large // 2)) | (
        (lane >= small + large) & (lane < small + large + large // 2)
    )
    far = jnp.where(
        upper, pltpu.roll(values, HEAD - large // 2, 1), pltpu.roll(values, large // 2, 1)
    )
    return jnp.where(lane < small, near, far)


def dot_nt(left, right):
    return lax.dot_general(left, right, (((1,), (1,)), ((), ())), preferred_element_type=jnp.float32)


def dot_tn(left, right):
    return lax.dot_general(left, right, (((0,), (0,)), ((), ())), preferred_element_type=jnp.float32)


def inverse_rms(values):
    return lax.rsqrt(jnp.mean(values * values, -1, keepdims=True) + epsilon)


def layer_norm(values):
    centred = values - jnp.mean(values, -1, keepdims=True)
    inverse_std = lax.rsqrt(jnp.mean(centred * centred, -1, keepdims=True) + epsilon)
    return (centred * inverse_std, inverse_std)


def sections():
    first = HEAD // 8
    other = (HEAD - first) // 2
    return ((0, first), (first, other), (first + other, other))


def step_kernel(
    nc, ns,
    time_ref, pos_ref, mod_w_ref, latent_ref, cot_ref, w_in_ref, w_out_ref,
    block_ref, grad_ref,
    mod_w, pos8, angle, cos_ref, sin_ref, part, part_in, mine, mod_all, vecs,
    lat_all, x_all, w_in_all, w_out_all, cot_all, x_cot, proj, q_all, k_all, v_all, probs,
    att, att_near, d_att, d_away, d_proj, mix_out, mix_in,
    dm_away, dm_here, dm_near, dm_sum, chain_in, total,
    own_sem, lat_s, lat_r, laty_s, laty_r, wi_s, wi_r, wif_s, wif_r, wo_s, wo_r, m1_s, m1_r,
    m2_s, m2_r, cot_s, cot_r, ex_s, ex_r, mx_s, mx_r, dmn_s, dmn_r, ch_s, ch_r,
):
    me_c = lax.axis_index("cand")
    me_s = lax.axis_index("seq")
    rows, width = latent_ref.shape
    length = rows * ns
    slab = w_in_ref.shape[0]
    groups = q_all.shape[0]
    cols = mod_w_ref.shape[1]
    piece = w_out_ref.shape[1]
    chunk = width // CHUNKS
    half = nc // 2
    core = lax.rem(me_c, 2)
    mate = me_c + 1 - 2 * core
    nz = ns // 2
    me_y, me_z = lax.rem(me_s, 2), lax.div(me_s, 2)
    near = me_s + 1 - 2 * me_y
    score_scale = HEAD ** (-0.5)
    size = rows // PARTS
    span = slab // SLABS
    run = nz * rows
    f32, bf16 = jnp.float32, jnp.bfloat16

    def place(index):
        return lax.rem(index, 2) * nz + lax.div(index, 2)

    def rows_of(index, count):
        return pl.ds(pl.multiple_of(index * count, count), count)

    def link(src, dst, send, recv, cand, seq):
        return pltpu.make_async_remote_copy(
            src_ref=src, dst_ref=dst, send_sem=send, recv_sem=recv,
            device_id=(cand, seq), device_id_type=MESH,
        )

    def remote(*args):
        copy = link(*args)
        copy.start()
        return copy

    def c_peer(k):
        return lax.rem(me_c + k, nc)

    def c_from(k):
        return lax.rem(me_c - k + nc, nc)

    def z_seq(z):
        return 2 * z + me_y

    barrier = pltpu.get_barrier_semaphore()
    for k in range(1, nc):
        pl.semaphore_signal(barrier, inc=1, device_id=(c_peer(k), me_s), device_id_type=MESH)
    for k in range(1, ns):
        pl.semaphore_signal(
            barrier, inc=1, device_id=(me_c, lax.rem(me_s + k, ns)), device_id_type=MESH
        )

    def w_in_at(index, q):
        return w_in_all.at[pl.ds(pl.multiple_of(index * slab + q * span, span), span)]

    own = [
        pltpu.make_async_copy(mod_w_ref, mod_w, own_sem.at[0]),
        pltpu.make_async_copy(latent_ref, lat_all.at[rows_of(place(me_s), rows)], own_sem.at[1]),
        pltpu.make_async_copy(cot_ref, cot_all.at[rows_of(me_z, rows)], own_sem.at[2]),
        pltpu.make_async_copy(w_in_ref, w_in_all.at[rows_of(me_c, slab)], own_sem.at[3]),
        pltpu.make_async_copy(w_out_ref, w_out_all.at[me_y, me_c], own_sem.at[4]),
    ]
    for copy in own:
        copy.start()
    pl.semaphore_wait(barrier, nc - 1 + ns - 1)

    def lat_at(z, y, p):
        return lat_all.at[pl.ds(pl.multiple_of((y * nz + z) * rows + p * size, size), size)]

    done = []

    def z_send(dirn, hop, p, src, z):
        to = me_z + 1 - 2 * dirn
        return link(
            src, lat_at(z, me_y, p), lat_s.at[dirn, hop, p], lat_r.at[dirn, hop, p],
            me_c, z_seq(to),
        )

    for p in range(PARTS):
        src = latent_ref.at[pl.ds(p * size, size)]
        for dirn, there in ((0, me_z < nz - 1), (1, me_z > 0)):
            @pl.when(there)
            def _():
                z_send(dirn, 0, p, src, me_z).start()
        done.append(
            remote(src, lat_at(me_z, me_y, p), laty_s.at[0, p], laty_r.at[0, p], me_c, near)
        )

    def slab_part(q):
        src = w_in_ref.at[pl.ds(q * span, span)]
        return [
            remote(src, w_in_at(me_c, q), wi_s.at[j, q], wi_r.at[j, q], c_peer(2 * j), me_s)
            for j in range(1, half)
        ]

    w_in_far = [slab_part(0)]

    count = part.shape[0]
    lead = mod_w_ref.shape[0]
    held_rows = max(16, nc)
    index = me_c * lead + lax.broadcasted_iota(jnp.int32, (held_rows, lead), 1)
    steps = width // 2
    is_cos = index < steps
    order = jnp.where(is_cos, index, index - steps).astype(f32)
    row = lax.broadcasted_iota(jnp.int32, (held_rows, 1), 0)
    times = jnp.zeros((held_rows, 1), f32)
    for c in range(nc):
        times = jnp.where(row == c, time_ref[c].astype(f32), times)
    turns = times * jnp.exp(order * (-math.log(10000.0)) / steps)
    wave = jnp.where(is_cos, jnp.cos(turns), jnp.sin(turns))
    act = (wave / (1.0 + jnp.exp(-wave))).astype(bf16)
    own[0].wait()
    product = jnp.dot(act, mod_w[...], preferred_element_type=f32)
    for c in range(count):
        part[c] = product[c : c + 1]
    m1 = []
    for k in range(1, nc):
        peer = c_peer(k)
        m1.append(remote(part.at[peer], part_in.at[me_c], m1_s.at[k], m1_r.at[k], peer, me_s))
    for q in range(1, SLABS):
        w_in_far.append(slab_part(q))
    w_in_mate = remote(
        w_in_ref, w_in_all.at[rows_of(me_c, slab)], wif_s.at[0, 0], wif_r.at[0, 0], mate, me_s
    )

    def w_out_at(y, c):
        return w_out_all.at[y, c]

    w_out_far = [
        remote(w_out_ref, w_out_at(me_y, me_c), wo_s.at[0, j], wo_r.at[0, j], c_peer(2 * j), me_s)
        for j in range(1, half)
    ]
    w_out_mate = remote(
        w_out_ref, w_out_at(me_y, me_c), wo_s.at[0, 0], wo_r.at[0, 0], mate, me_s
    )

    pos8[...] = jnp.zeros_like(pos8)
    pos8[0 : pos_ref.shape[0]] = pos_ref[...].astype(f32)
    lane = lax.broadcasted_iota(jnp.int32, (8, HEAD), 1)
    axis = lax.broadcasted_iota(jnp.int32, (8, HEAD), 0)
    rate = jnp.zeros((8, HEAD), f32)
    sign = jnp.ones((8, HEAD), f32)
    for a, (start, extent) in enumerate(sections()):
        inside = (lane >= start) & (lane < start + extent)
        late = inside & (lane >= start + extent // 2)
        pair = jnp.where(late, lane - start - extent // 2, lane - start).astype(f32)
        value = jnp.exp(pair * (-math.log(256.0) * 2.0 / extent))
        rate = jnp.where(inside & (axis == a), value, rate)
        sign = jnp.where(inside & ~late, -1.0, sign)
    angle[...] = lax.dot_general(
        pos8[...], rate, (((0,), (0,)), ((), ())), preferred_element_type=f32,
        precision=lax.Precision.HIGHEST,
    )

    def turn_rows(s, _):
        turned = angle[rows_of(s, rows)]
        at = rows_of(place(s), rows)
        cos_ref[at] = jnp.cos(turned)
        sin_ref[at] = jnp.sin(turned) * sign[0:1]
        return 0

    lax.fori_loop(0, ns, turn_rows, 0)

    def exists(dirn, hop):
        return me_z >= hop if dirn == 0 else me_z <= nz - 1 - hop

    def beyond(dirn):
        return me_z < nz - 1 if dirn == 0 else me_z > 0

    def source(dirn, hop):
        return me_z - hop if dirn == 0 else me_z + hop

    def y_slot(dirn, hop):
        return hop if dirn == 0 else nz - 1 + hop

    def y_link(dirn, hop, p):
        held = lat_at(source(dirn, hop), me_y, p)
        slot = y_slot(dirn, hop)
        return link(held, held, laty_s.at[slot, p], laty_r.at[slot, p], me_c, near)

    def relay(hop):
        for p in range(PARTS):
            for dirn in range(2):
                @pl.when(exists(dirn, hop))
                def _():
                    z = source(dirn, hop)
                    held = lat_at(z, me_y, p)
                    z_send(dirn, hop - 1, p, held, z).wait_recv()
                    if hop < nz - 1:
                        @pl.when(beyond(dirn))
                        def _():
                            z_send(dirn, hop, p, held, z).start()
                    y_link(dirn, hop, p).start()

    relay(1)
    for copy in m1:
        copy.wait_recv()
    summed_mod = part[me_c]
    for k in range(1, nc):
        summed_mod = summed_mod + part_in[c_from(k)]
    mine[...] = summed_mod
    mod_all[me_s] = summed_mod
    m2 = [
        remote(
            mine, mod_all.at[me_s], m2_s.at[k], m2_r.at[k], me_c, lax.rem(me_s + k, ns)
        )
        for k in range(1, ns)
    ]
    for hop in range(2, nz - 1):
        relay(hop)
    cot_far = []
    for k in range(1, nz):
        peer = lax.rem(me_z + k, nz)
        cot_far.append(
            remote(
                cot_ref, cot_all.at[rows_of(me_z, rows)], cot_s.at[k], cot_r.at[k],
                me_c, z_seq(peer),
            )
        )
    for copy in m2:
        copy.wait_recv()
    for s in range(ns):
        at = s * cols
        while at < (s + 1) * cols:
            kind = at // width
            stop = min((s + 1) * cols, (kind + 1) * width)
            vecs[kind, :, at - kind * width : stop - kind * width] = mod_all[
                s, :, at - s * cols : stop - s * cols
            ]
            at = stop

    def norm_rows(at):
        normed, _inverse = layer_norm(lat_all[at].astype(f32))
        x_all[at] = (normed * (1.0 + vecs[1]) + vecs[0]).astype(bf16)

    def norm_run(start, count):
        def body(i, _):
            norm_rows(pl.ds(pl.multiple_of(start + i * 16, 16), 16))
            return 0

        lax.fori_loop(0, count // 16, body, 0)

    own[1].wait()
    norm_run(place(me_s) * rows, rows)
    for dirn in range(2):
        for hop in range(1, nz - 1):
            @pl.when(exists(dirn, hop))
            def _():
                norm_run((me_y * nz + source(dirn, hop)) * rows, rows)

    if nz > 1:
        relay(nz - 1)
        for dirn in range(2):
            @pl.when(exists(dirn, nz - 1))
            def _():
                norm_run((me_y * nz + source(dirn, nz - 1)) * rows, rows)

    w_out_near = remote(
        w_out_ref, w_out_at(me_y, me_c), wo_s.at[1, 0], wo_r.at[1, 0], me_c, near
    )

    w_in_second = []

    def slab_forward(q):
        for j in range(1, half):
            w_in_far[q][j - 1].wait_recv()
            held = w_in_at(c_from(2 * j), q)
            w_in_second.append(
                remote(held, held, wif_s.at[j, q], wif_r.at[j, q], mate, me_s)
            )

    for q in range(SLABS - 1):
        slab_forward(q)
    for copy in done:
        copy.wait_recv()
    norm_run(((1 - me_y) * nz + me_z) * rows, rows)
    for hop in range(1, nz):
        for dirn in range(2):
            @pl.when(exists(dirn, hop))
            def _():
                for p in range(PARTS):
                    y_link(dirn, hop, p).wait_recv()
                norm_run(((1 - me_y) * nz + source(dirn, hop)) * rows, rows)
    slab_forward(SLABS - 1)
    own[3].wait()
    w_in_mate.wait_recv()
    for copy in w_in_second:
        copy.wait_recv()

    tile = 3 * HEAD

    def project(index, _):
        at = pl.ds(pl.multiple_of(index * tile, tile), tile)
        proj[index] = jnp.dot(x_all[...], w_in_all[:, at], preferred_element_type=f32)
        return 0

    lax.fori_loop(0, groups, project, 0)

    def head_at(h):
        return pl.ds(pl.multiple_of(h * HEAD, HEAD), HEAD)

    def head_forward(h, _):
        query = proj[h, :, 0:HEAD]
        key = proj[h, :, HEAD : 2 * HEAD]
        query_n = query * inverse_rms(query)
        key_n = key * inverse_rms(key)
        q_rot = (query_n * cos_ref[...] + swap_pairs(query_n) * sin_ref[...]).astype(bf16)
        k_rot = (key_n * cos_ref[...] + swap_pairs(key_n) * sin_ref[...]).astype(bf16)
        values = proj[h, :, 2 * HEAD :].astype(bf16)
        q_all[h] = q_rot
        k_all[h] = k_rot
        v_all[h] = values
        weights = jnp.exp(dot_nt(q_rot, k_rot) * score_scale - HEAD**0.5)
        share = weights * (1.0 / jnp.sum(weights, -1, keepdims=True))
        probs[h] = share
        att[:, head_at(h)] = jnp.dot(
            share.astype(bf16), values, preferred_element_type=f32
        ).astype(bf16)
        return 0

    lax.fori_loop(0, groups, head_forward, 0)
    att_move = remote(
        att.at[rows_of(1 - me_y, run)], att_near, ex_s.at[0], ex_r.at[0], me_c, near
    )

    w_out_second = []
    for j in range(1, half):
        w_out_far[j - 1].wait_recv()
        held = w_out_at(me_y, c_from(2 * j))
        w_out_second.append(
            remote(held, held, wo_s.at[2, j], wo_r.at[2, j], mate, me_s)
        )
    w_out_near.wait_recv()
    held = w_out_at(1 - me_y, me_c)
    w_out_second.append(remote(held, held, wo_s.at[2, 0], wo_r.at[2, 0], mate, me_s))
    w_out_cross = []
    for j in range(1, half):
        held = w_out_all.at[
            jnp.where(core == 0, me_y, 1 - me_y), jnp.where(core == 0, c_from(2 * j), me_c)
        ]
        w_out_cross.append(
            remote(
                held, held, wo_s.at[3, j], wo_r.at[3, j],
                jnp.where(core == 0, me_c, c_peer(2 * j)), jnp.where(core == 0, near, me_s),
            )
        )

    own[2].wait()
    for copy in cot_far:
        copy.wait_recv()

    def gate_rows(index, _):
        at = rows_of(index, 16)
        x_cot[at] = (cot_all[at].astype(f32) * vecs[2]).astype(bf16)
        return 0

    lax.fori_loop(0, run // 16, gate_rows, 0)

    for j in range(1, half):
        held = w_out_at(1 - me_y, c_from(2 * j))
        link(held, held, wo_s.at[3, j], wo_r.at[3, j], me_c, near).wait_recv()
        w_out_second.append(
            remote(held, held, wo_s.at[4, j], wo_r.at[4, j], mate, me_s)
        )
    own[4].wait()
    w_out_mate.wait_recv()
    for copy in w_out_second:
        copy.wait_recv()

    def d_attended(y):
        block = jnp.zeros((run, groups * HEAD), f32)
        for c in range(nc):
            block = block + dot_nt(x_cot[:, c * piece : (c + 1) * piece], w_out_all[y, c])
        return block.astype(bf16)

    d_away[...] = d_attended(1 - me_y)
    d_move = remote(
        d_away, d_att.at[rows_of(me_y, run)], ex_s.at[1], ex_r.at[1], me_c, near
    )
    d_att[rows_of(me_y, run)] = d_attended(me_y)

    att_move.wait_recv()
    att_own = att[rows_of(me_y, run)]
    for c in range(nc):
        mix_out[:, c * piece : (c + 1) * piece] = (
            jnp.dot(att_own, w_out_all[me_y, c], preferred_element_type=f32)
            + jnp.dot(att_near[...], w_out_all[1 - me_y, c], preferred_element_type=f32)
        ).astype(bf16)
    mixed = []
    for k in range(1, nz):
        peer = lax.rem(me_z + k, nz)
        mixed.append(
            remote(
                mix_out.at[rows_of(peer, rows)], mix_in.at[rows_of(me_z, rows)],
                mx_s.at[k], mx_r.at[k], me_c, z_seq(peer),
            )
        )
    d_move.wait_recv()

    def back_norm(d_rot, raw):
        inverse = inverse_rms(raw)
        normed = raw * inverse
        d_normed = d_rot * cos_ref[...] - swap_pairs(d_rot) * sin_ref[...]
        return inverse * (d_normed - normed * jnp.mean(d_normed * normed, -1, keepdims=True))

    def head_backward(h, _):
        d_heads = d_att[:, head_at(h)]
        share = probs[h]
        d_values = dot_tn(share.astype(bf16), d_heads)
        d_probs = dot_nt(d_heads, v_all[h])
        d_scores = (share * (d_probs - jnp.sum(share * d_probs, -1, keepdims=True))).astype(bf16)
        d_qrot = jnp.dot(d_scores, k_all[h], preferred_element_type=f32) * score_scale
        d_krot = dot_tn(d_scores, q_all[h]) * score_scale
        d_query = back_norm(d_qrot, proj[h, :, 0:HEAD])
        d_key = back_norm(d_krot, proj[h, :, HEAD : 2 * HEAD])
        d_proj[:, head_at(3 * h)] = d_query.astype(bf16)
        d_proj[:, head_at(3 * h + 1)] = d_key.astype(bf16)
        d_proj[:, head_at(3 * h + 2)] = d_values.astype(bf16)
        return 0

    lax.fori_loop(0, groups, head_backward, 0)

    order = []
    low, high = 0, nz - 1
    for i in range(nz):
        take = (me_z - low >= high - me_z).astype(jnp.int32)
        order.append(take * low + (1 - take) * high)
        low, high = low + take, high - (1 - take)

    d_near = [[None] * CHUNKS for _ in range(nz)]

    def away(i, j):
        at = (rows_of(order[i], rows), pl.ds(j * chunk, chunk))
        d_near[i][j] = remote(
            dm_away.at[at], dm_near.at[at], dmn_s.at[i, j], dmn_r.at[i, j], me_c, near
        )

    for j in range(CHUNKS):
        part_cols = slice(j * chunk, (j + 1) * chunk)
        dm_away[:, part_cols] = dot_nt(
            d_proj[rows_of(1 - me_y, run)], w_in_all[part_cols]
        ).astype(bf16)
        away(0, j)
    for i in range(1, nz):
        for j in range(CHUNKS):
            away(i, j)
    for j in range(CHUNKS):
        part_cols = slice(j * chunk, (j + 1) * chunk)
        dm_here[:, part_cols] = dot_nt(
            d_proj[rows_of(me_y, run)], w_in_all[part_cols]
        ).astype(bf16)

    chain = []
    for i in range(nz - 1):
        to = order[i]
        up = to > me_z
        dirn = 1 - up.astype(jnp.int32)
        fed = (up & (me_z > 0)) | (~up & (me_z < nz - 1))
        beside = z_seq(me_z + 1 - 2 * dirn)
        for j in range(CHUNKS):
            at = (rows_of(to, rows), pl.ds(j * chunk, chunk))
            d_near[i][j].wait_recv()
            hop = link(
                dm_sum.at[at], chain_in.at[(dirn,) + at], ch_s.at[dirn, to, j],
                ch_r.at[dirn, to, j], me_c, beside,
            )
            value = dm_here[at].astype(f32) + dm_near[at].astype(f32)

            @pl.when(fed)
            def _():
                hop.wait_recv()
                dm_sum[at] = (value + chain_in[(dirn,) + at].astype(f32)).astype(bf16)

            @pl.when(~fed)
            def _():
                dm_sum[at] = value.astype(bf16)

            hop.start()
            chain.append(hop)

    for copy in mixed:
        copy.wait_recv()
    for start in range(0, rows, 16):
        mine_at = pl.ds(pl.multiple_of(me_z * rows + start, 16), 16)
        lat_rows = pl.ds(pl.multiple_of(place(me_s) * rows + start, 16), 16)
        value = mix_out[mine_at].astype(f32)
        for k in range(1, nz):
            from_z = lax.rem(me_z + k, nz)
            value = value + mix_in[
                pl.ds(pl.multiple_of(from_z * rows + start, 16), 16)
            ].astype(f32)
        block_ref[start : start + 16] = (
            lat_all[lat_rows].astype(f32) + vecs[2] * value
        ).astype(bf16)

    for j in range(CHUNKS):
        part_cols = pl.ds(j * chunk, chunk)
        at = (rows_of(me_z, rows), part_cols)
        d_near[nz - 1][j].wait_recv()
        total[:, part_cols] = dm_here[at].astype(f32) + dm_near[at].astype(f32)
        for dirn, fed in ((0, me_z > 0), (1, me_z < nz - 1)):
            @pl.when(fed)
            def _():
                landed = chain_in.at[(dirn,) + at]
                link(
                    landed, landed, ch_s.at[dirn, me_z, j], ch_r.at[dirn, me_z, j], me_c, near
                ).wait_recv()
                total[:, part_cols] += landed[...].astype(f32)

    for start in range(0, rows, 16):
        lat_rows = pl.ds(pl.multiple_of(place(me_s) * rows + start, 16), 16)
        cot_rows = pl.ds(pl.multiple_of(me_z * rows + start, 16), 16)
        normed, inverse_std = layer_norm(lat_all[lat_rows].astype(f32))
        d_normed = total[start : start + 16] * (1.0 + vecs[1])
        grad_ref[start : start + 16] = cot_all[cot_rows].astype(f32) + inverse_std * (
            d_normed
            - jnp.mean(d_normed, -1, keepdims=True)
            - normed * jnp.mean(d_normed * normed, -1, keepdims=True)
        )

    for p in range(PARTS):
        for dirn in range(2):
            for hop in range(nz - 1):
                @pl.when(exists(dirn, hop) & beyond(dirn))
                def _():
                    held = lat_at(source(dirn, hop), me_y, p)
                    z_send(dirn, hop, p, held, source(dirn, hop)).wait_send()
            for hop in range(1, nz):
                @pl.when(exists(dirn, hop))
                def _():
                    y_link(dirn, hop, p).wait_send()
    for copy in (
        done + m1 + m2 + sum(w_in_far, []) + [w_in_mate] + w_in_second + w_out_far
        + [w_out_mate, w_out_near] + w_out_second + w_out_cross + cot_far
        + [att_move, d_move] + mixed + sum(d_near, []) + chain
    ):
        copy.wait_send()


def on_device(latent, timesteps, positions, mod_weight, input_weight, output_weight, cotangent):
    nc = lax.axis_size("cand")
    ns = lax.axis_size("seq")
    rows, width = latent.shape[1:]
    length = rows * ns
    slab = input_weight.shape[0]
    groups = input_weight.shape[1]
    cols = mod_weight.shape[1]
    piece = output_weight.shape[2]
    half = nc // 2
    nz = ns // 2
    run = nz * rows
    vmem = pl.BlockSpec(memory_space=pltpu.VMEM)
    smem = pl.BlockSpec(memory_space=pltpu.SMEM)
    anywhere = pl.BlockSpec(memory_space=pl.ANY)
    f32, bf16 = jnp.float32, jnp.bfloat16
    dma = pltpu.SemaphoreType.DMA
    block_out, latent_grad = pl.pallas_call(
        functools.partial(step_kernel, nc, ns),
        out_shape=(
            jax.ShapeDtypeStruct((rows, width), bf16),
            jax.ShapeDtypeStruct((rows, width), f32),
        ),
        in_specs=[smem, vmem] + [anywhere] * 5,
        out_specs=(vmem, vmem),
        scratch_shapes=[
            pltpu.VMEM(mod_weight.shape, bf16),
            pltpu.VMEM((8, length), f32),
            pltpu.VMEM((length, HEAD), f32),
            pltpu.VMEM((length, HEAD), f32),
            pltpu.VMEM((length, HEAD), f32),
            pltpu.VMEM((nc, 1, cols), f32),
            pltpu.VMEM((nc, 1, cols), f32),
            pltpu.VMEM((1, cols), f32),
            pltpu.VMEM((ns, 1, cols), f32),
            pltpu.VMEM((3, 1, width), f32),
            pltpu.VMEM((length, width), bf16),
            pltpu.VMEM((length, width), bf16),
            pltpu.VMEM((slab * nc, groups * 3 * HEAD), bf16),
            pltpu.VMEM((2, nc, groups * HEAD, piece), bf16),
            pltpu.VMEM((run, width), bf16),
            pltpu.VMEM((run, width), bf16),
            pltpu.VMEM((groups, length, 3 * HEAD), f32),
            pltpu.VMEM((groups, length, HEAD), bf16),
            pltpu.VMEM((groups, length, HEAD), bf16),
            pltpu.VMEM((groups, length, HEAD), bf16),
            pltpu.VMEM((groups, length, length), f32),
            pltpu.VMEM((length, groups * HEAD), bf16),
            pltpu.VMEM((run, groups * HEAD), bf16),
            pltpu.VMEM((length, groups * HEAD), bf16),
            pltpu.VMEM((run, groups * HEAD), bf16),
            pltpu.VMEM((length, groups * 3 * HEAD), bf16),
            pltpu.VMEM((run, width), bf16),
            pltpu.VMEM((run, width), bf16),
            pltpu.VMEM((run, width), bf16),
            pltpu.VMEM((run, width), bf16),
            pltpu.VMEM((run, width), bf16),
            pltpu.VMEM((run, width), bf16),
            pltpu.VMEM((2, run, width), bf16),
            pltpu.VMEM((rows, width), f32),
            dma((5,)),
            dma((2, nz, PARTS)), dma((2, nz, PARTS)),
            dma((2 * nz, PARTS)), dma((2 * nz, PARTS)),
            dma((half, SLABS)), dma((half, SLABS)), dma((half, SLABS)), dma((half, SLABS)),
            dma((5, half)), dma((5, half)), dma((nc,)), dma((nc,)), dma((ns,)), dma((ns,)),
            dma((nz,)), dma((nz,)), dma((2,)), dma((2,)), dma((nz,)), dma((nz,)),
            dma((nz, CHUNKS)), dma((nz, CHUNKS)), dma((2, nz, CHUNKS)), dma((2, nz, CHUNKS)),
        ],
        compiler_params=pltpu.CompilerParams(
            collective_id=0, has_side_effects=True, vmem_limit_bytes=66000000
        ),
    )(
        timesteps, positions, mod_weight, latent[0], cotangent[0],
        input_weight.reshape(slab, groups * 3 * HEAD),
        output_weight.reshape(groups * HEAD, piece),
    )
    return (block_out[None], latent_grad[None])


def solution(mesh):
    placed = (
        P("cand", "seq", None),
        P(),
        P(),
        P("cand", "seq"),
        P("cand", "seq", None),
        P("seq", None, "cand"),
        P("cand", "seq", None),
    )
    return jax.shard_map(
        on_device,
        mesh=mesh,
        in_specs=placed,
        out_specs=(P("cand", "seq", None), P("cand", "seq", None)),
        check_vma=False,
    )
```

```python
import functools
import math

import jax
import jax.numpy as jnp
from jax import lax
from jax.experimental import pallas as pl
from jax.experimental.pallas import tpu as pltpu
from jax.sharding import PartitionSpec as P

HEAD = 128
CHUNKS = 4
PARTS = 3
SLABS = 4
MESH = pl.DeviceIdType.MESH


epsilon = 1e-06


def swap_pairs(values):
    lane = lax.broadcasted_iota(jnp.int32, values.shape, 1)
    small = HEAD // 8
    large = (HEAD - small) // 2
    near = jnp.where(
        lane < small // 2,
        pltpu.roll(values, HEAD - small // 2, 1),
        pltpu.roll(values, small // 2, 1),
    )
    upper = ((lane >= small) & (lane < small + large // 2)) | (
        (lane >= small + large) & (lane < small + large + large // 2)
    )
    far = jnp.where(
        upper, pltpu.roll(values, HEAD - large // 2, 1), pltpu.roll(values, large // 2, 1)
    )
    return jnp.where(lane < small, near, far)


def dot_nt(left, right):
    return lax.dot_general(left, right, (((1,), (1,)), ((), ())), preferred_element_type=jnp.float32)


def dot_tn(left, right):
    return lax.dot_general(left, right, (((0,), (0,)), ((), ())), preferred_element_type=jnp.float32)


def inverse_rms(values):
    return lax.rsqrt(jnp.mean(values * values, -1, keepdims=True) + epsilon)


def layer_norm(values):
    centred = values - jnp.mean(values, -1, keepdims=True)
    inverse_std = lax.rsqrt(jnp.mean(centred * centred, -1, keepdims=True) + epsilon)
    return (centred * inverse_std, inverse_std)


def sections():
    first = HEAD // 8
    other = (HEAD - first) // 2
    return ((0, first), (first, other), (first + other, other))


def step_kernel(
    nc, ns,
    time_ref, pos_ref, mod_w_ref, latent_ref, cot_ref, w_in_ref, w_out_ref,
    block_ref, grad_ref,
    mod_w, pos8, angle, cos_ref, sin_ref, part, part_in, mine, mod_all, vecs,
    lat_all, x_all, w_in_all, w_out_all, cot_all, x_cot, proj, q_all, k_all, v_all, probs,
    att, att_near, d_att, d_away, d_proj, key_sum, value_sum, mix_out, mix_in,
    dm_away, dm_here, dm_near, dm_sum, chain_in, total,
    own_sem, lat_s, lat_r, laty_s, laty_r, wi_s, wi_r, wif_s, wif_r, wo_s, wo_r, m1_s, m1_r,
    m2_s, m2_r, cot_s, cot_r, ex_s, ex_r, mx_s, mx_r, dmn_s, dmn_r, ch_s, ch_r,
):
    me_c = lax.axis_index("cand")
    me_s = lax.axis_index("seq")
    rows, width = latent_ref.shape
    length = rows * ns
    slab = w_in_ref.shape[0]
    groups = q_all.shape[0]
    cols = mod_w_ref.shape[1]
    piece = w_out_ref.shape[1]
    chunk = width // CHUNKS
    half = nc // 2
    core = lax.rem(me_c, 2)
    mate = me_c + 1 - 2 * core
    nz = ns // 2
    me_y, me_z = lax.rem(me_s, 2), lax.div(me_s, 2)
    near = me_s + 1 - 2 * me_y
    score_scale = HEAD ** (-0.5)
    size = rows // PARTS
    span = slab // SLABS
    run = nz * rows
    f32, bf16 = jnp.float32, jnp.bfloat16

    def place(index):
        return lax.rem(index, 2) * nz + lax.div(index, 2)

    def rows_of(index, count):
        return pl.ds(pl.multiple_of(index * count, count), count)

    def link(src, dst, send, recv, cand, seq):
        return pltpu.make_async_remote_copy(
            src_ref=src, dst_ref=dst, send_sem=send, recv_sem=recv,
            device_id=(cand, seq), device_id_type=MESH,
        )

    def remote(*args):
        copy = link(*args)
        copy.start()
        return copy

    def c_peer(k):
        return lax.rem(me_c + k, nc)

    def c_from(k):
        return lax.rem(me_c - k + nc, nc)

    def z_seq(z):
        return 2 * z + me_y

    barrier = pltpu.get_barrier_semaphore()
    for k in range(1, nc):
        pl.semaphore_signal(barrier, inc=1, device_id=(c_peer(k), me_s), device_id_type=MESH)
    for k in range(1, ns):
        pl.semaphore_signal(
            barrier, inc=1, device_id=(me_c, lax.rem(me_s + k, ns)), device_id_type=MESH
        )

    def w_in_at(index, q):
        return w_in_all.at[pl.ds(pl.multiple_of(index * slab + q * span, span), span)]

    own = [
        pltpu.make_async_copy(mod_w_ref, mod_w, own_sem.at[0]),
        pltpu.make_async_copy(latent_ref, lat_all.at[rows_of(place(me_s), rows)], own_sem.at[1]),
        pltpu.make_async_copy(cot_ref, cot_all.at[rows_of(me_z, rows)], own_sem.at[2]),
        pltpu.make_async_copy(w_in_ref, w_in_all.at[rows_of(me_c, slab)], own_sem.at[3]),
        pltpu.make_async_copy(w_out_ref, w_out_all.at[me_y, me_c], own_sem.at[4]),
    ]
    for copy in own:
        copy.start()
    pl.semaphore_wait(barrier, nc - 1 + ns - 1)

    def lat_at(z, y, p):
        return lat_all.at[pl.ds(pl.multiple_of((y * nz + z) * rows + p * size, size), size)]

    done = []

    def z_send(dirn, hop, p, src, z):
        to = me_z + 1 - 2 * dirn
        return link(
            src, lat_at(z, me_y, p), lat_s.at[dirn, hop, p], lat_r.at[dirn, hop, p],
            me_c, z_seq(to),
        )

    for p in range(PARTS):
        src = latent_ref.at[pl.ds(p * size, size)]
        for dirn, there in ((0, me_z < nz - 1), (1, me_z > 0)):
            @pl.when(there)
            def _():
                z_send(dirn, 0, p, src, me_z).start()
        done.append(
            remote(src, lat_at(me_z, me_y, p), laty_s.at[0, p], laty_r.at[0, p], me_c, near)
        )

    def slab_part(q):
        src = w_in_ref.at[pl.ds(q * span, span)]
        return [
            remote(src, w_in_at(me_c, q), wi_s.at[j, q], wi_r.at[j, q], c_peer(2 * j), me_s)
            for j in range(1, half)
        ]

    w_in_far = [slab_part(0)]

    count = part.shape[0]
    lead = mod_w_ref.shape[0]
    held_rows = max(16, nc)
    index = me_c * lead + lax.broadcasted_iota(jnp.int32, (held_rows, lead), 1)
    steps = width // 2
    is_cos = index < steps
    order = jnp.where(is_cos, index, index - steps).astype(f32)
    row = lax.broadcasted_iota(jnp.int32, (held_rows, 1), 0)
    times = jnp.zeros((held_rows, 1), f32)
    for c in range(nc):
        times = jnp.where(row == c, time_ref[c].astype(f32), times)
    turns = times * jnp.exp(order * (-math.log(10000.0)) / steps)
    wave = jnp.where(is_cos, jnp.cos(turns), jnp.sin(turns))
    act = (wave / (1.0 + jnp.exp(-wave))).astype(bf16)
    own[0].wait()
    product = jnp.dot(act, mod_w[...], preferred_element_type=f32)
    for c in range(count):
        part[c] = product[c : c + 1]
    m1 = []
    for k in range(1, nc):
        peer = c_peer(k)
        m1.append(remote(part.at[peer], part_in.at[me_c], m1_s.at[k], m1_r.at[k], peer, me_s))
    for q in range(1, SLABS):
        w_in_far.append(slab_part(q))
    w_in_mate = remote(
        w_in_ref, w_in_all.at[rows_of(me_c, slab)], wif_s.at[0, 0], wif_r.at[0, 0], mate, me_s
    )

    def w_out_at(y, c):
        return w_out_all.at[y, c]

    w_out_far = [
        remote(w_out_ref, w_out_at(me_y, me_c), wo_s.at[0, j], wo_r.at[0, j], c_peer(2 * j), me_s)
        for j in range(1, half)
    ]
    w_out_mate = remote(
        w_out_ref, w_out_at(me_y, me_c), wo_s.at[0, 0], wo_r.at[0, 0], mate, me_s
    )

    pos8[...] = jnp.zeros_like(pos8)
    pos8[0 : pos_ref.shape[0]] = pos_ref[...].astype(f32)
    lane = lax.broadcasted_iota(jnp.int32, (8, HEAD), 1)
    axis = lax.broadcasted_iota(jnp.int32, (8, HEAD), 0)
    rate = jnp.zeros((8, HEAD), f32)
    sign = jnp.ones((8, HEAD), f32)
    for a, (start, extent) in enumerate(sections()):
        inside = (lane >= start) & (lane < start + extent)
        late = inside & (lane >= start + extent // 2)
        pair = jnp.where(late, lane - start - extent // 2, lane - start).astype(f32)
        value = jnp.exp(pair * (-math.log(256.0) * 2.0 / extent))
        rate = jnp.where(inside & (axis == a), value, rate)
        sign = jnp.where(inside & ~late, -1.0, sign)
    angle[...] = lax.dot_general(
        pos8[...], rate, (((0,), (0,)), ((), ())), preferred_element_type=f32,
        precision=lax.Precision.HIGHEST,
    )

    def turn_rows(s, _):
        turned = angle[rows_of(s, rows)]
        at = rows_of(place(s), rows)
        cos_ref[at] = jnp.cos(turned)
        sin_ref[at] = jnp.sin(turned) * sign[0:1]
        return 0

    lax.fori_loop(0, ns, turn_rows, 0)

    def exists(dirn, hop):
        return me_z >= hop if dirn == 0 else me_z <= nz - 1 - hop

    def beyond(dirn):
        return me_z < nz - 1 if dirn == 0 else me_z > 0

    def source(dirn, hop):
        return me_z - hop if dirn == 0 else me_z + hop

    def y_slot(dirn, hop):
        return hop if dirn == 0 else nz - 1 + hop

    def y_link(dirn, hop, p):
        held = lat_at(source(dirn, hop), me_y, p)
        slot = y_slot(dirn, hop)
        return link(held, held, laty_s.at[slot, p], laty_r.at[slot, p], me_c, near)

    def relay(hop):
        for p in range(PARTS):
            for dirn in range(2):
                @pl.when(exists(dirn, hop))
                def _():
                    z = source(dirn, hop)
                    held = lat_at(z, me_y, p)
                    z_send(dirn, hop - 1, p, held, z).wait_recv()
                    if hop < nz - 1:
                        @pl.when(beyond(dirn))
                        def _():
                            z_send(dirn, hop, p, held, z).start()
                    y_link(dirn, hop, p).start()

    relay(1)
    for copy in m1:
        copy.wait_recv()
    summed_mod = part[me_c]
    for k in range(1, nc):
        summed_mod = summed_mod + part_in[c_from(k)]
    mine[...] = summed_mod
    mod_all[me_s] = summed_mod
    m2 = [
        remote(
            mine, mod_all.at[me_s], m2_s.at[k], m2_r.at[k], me_c, lax.rem(me_s + k, ns)
        )
        for k in range(1, ns)
    ]
    for hop in range(2, nz - 1):
        relay(hop)
    cot_far = []
    for k in range(1, nz):
        peer = lax.rem(me_z + k, nz)
        cot_far.append(
            remote(
                cot_ref, cot_all.at[rows_of(me_z, rows)], cot_s.at[k], cot_r.at[k],
                me_c, z_seq(peer),
            )
        )
    for copy in m2:
        copy.wait_recv()
    for s in range(ns):
        at = s * cols
        while at < (s + 1) * cols:
            kind = at // width
            stop = min((s + 1) * cols, (kind + 1) * width)
            vecs[kind, :, at - kind * width : stop - kind * width] = mod_all[
                s, :, at - s * cols : stop - s * cols
            ]
            at = stop

    def norm_rows(at):
        normed, _inverse = layer_norm(lat_all[at].astype(f32))
        x_all[at] = (normed * (1.0 + vecs[1]) + vecs[0]).astype(bf16)

    def norm_run(start, count):
        def body(i, _):
            norm_rows(pl.ds(pl.multiple_of(start + i * 16, 16), 16))
            return 0

        lax.fori_loop(0, count // 16, body, 0)

    own[1].wait()
    norm_run(place(me_s) * rows, rows)
    for dirn in range(2):
        for hop in range(1, nz - 1):
            @pl.when(exists(dirn, hop))
            def _():
                norm_run((me_y * nz + source(dirn, hop)) * rows, rows)

    if nz > 1:
        relay(nz - 1)
        for dirn in range(2):
            @pl.when(exists(dirn, nz - 1))
            def _():
                norm_run((me_y * nz + source(dirn, nz - 1)) * rows, rows)

    w_out_near = remote(
        w_out_ref, w_out_at(me_y, me_c), wo_s.at[1, 0], wo_r.at[1, 0], me_c, near
    )

    w_in_second = []

    def slab_forward(q):
        for j in range(1, half):
            w_in_far[q][j - 1].wait_recv()
            held = w_in_at(c_from(2 * j), q)
            w_in_second.append(
                remote(held, held, wif_s.at[j, q], wif_r.at[j, q], mate, me_s)
            )

    for q in range(SLABS - 1):
        slab_forward(q)
    for copy in done:
        copy.wait_recv()
    norm_run(((1 - me_y) * nz + me_z) * rows, rows)
    for hop in range(1, nz):
        for dirn in range(2):
            @pl.when(exists(dirn, hop))
            def _():
                for p in range(PARTS):
                    y_link(dirn, hop, p).wait_recv()
                norm_run(((1 - me_y) * nz + source(dirn, hop)) * rows, rows)
    slab_forward(SLABS - 1)
    own[3].wait()
    w_in_mate.wait_recv()
    for copy in w_in_second:
        copy.wait_recv()

    tile = 3 * HEAD

    def project(index, _):
        at = pl.ds(pl.multiple_of(index * tile, tile), tile)
        proj[index] = jnp.dot(x_all[...], w_in_all[:, at], preferred_element_type=f32)
        return 0

    lax.fori_loop(0, groups, project, 0)

    def head_at(h):
        return pl.ds(pl.multiple_of(h * HEAD, HEAD), HEAD)

    def head_forward(h, _):
        query = proj[h, :, 0:HEAD]
        key = proj[h, :, HEAD : 2 * HEAD]
        query_n = query * inverse_rms(query)
        key_n = key * inverse_rms(key)
        q_rot = (query_n * cos_ref[...] + swap_pairs(query_n) * sin_ref[...]).astype(bf16)
        k_rot = (key_n * cos_ref[...] + swap_pairs(key_n) * sin_ref[...]).astype(bf16)
        values = proj[h, :, 2 * HEAD :].astype(bf16)
        q_all[h] = q_rot
        k_all[h] = k_rot
        v_all[h] = values
        weights = jnp.exp(dot_nt(q_rot, k_rot) * score_scale - HEAD**0.5)
        share = weights * (1.0 / jnp.sum(weights, -1, keepdims=True))
        probs[h] = share
        att[:, head_at(h)] = jnp.dot(
            share.astype(bf16), values, preferred_element_type=f32
        ).astype(bf16)
        return 0

    lax.fori_loop(0, groups, head_forward, 0)
    att_move = remote(
        att.at[rows_of(1 - me_y, run)], att_near, ex_s.at[0], ex_r.at[0], me_c, near
    )

    def att_rows(which):
        return att[rows_of(me_y, run)] if which == 0 else att_near[...]

    mixed = []

    def mix_chip(j):
        first = 2 * lax.rem(lax.div(me_c, 2) + j, half)
        for b in range(2):
            mix_out[first + b] = (
                jnp.dot(att_rows(0), w_out_all[me_y, first + b], preferred_element_type=f32)
                + jnp.dot(att_rows(1), w_out_all[1 - me_y, first + b], preferred_element_type=f32)
            ).astype(bf16)
        for k in range(1, nz):
            peer = lax.rem(me_z + k, nz)
            mixed.append(
                remote(
                    mix_out.at[pl.ds(first, 2), rows_of(peer, rows)],
                    mix_in.at[me_z, pl.ds(first, 2)],
                    mx_s.at[k, j], mx_r.at[k, j], me_c, z_seq(peer),
                )
            )

    w_out_near.wait_recv()
    held = w_out_at(1 - me_y, me_c)
    w_out_near_mate = remote(held, held, wo_s.at[2, 0], wo_r.at[2, 0], mate, me_s)
    own[4].wait()
    w_out_mate.wait_recv()
    att_move.wait_recv()
    w_out_near_mate.wait_recv()
    mix_chip(0)

    w_out_second = []
    w_out_cross = []
    for j in range(1, half):
        w_out_far[j - 1].wait_recv()
        held = w_out_all.at[
            jnp.where(core == 0, me_y, 1 - me_y), jnp.where(core == 0, c_from(2 * j), me_c)
        ]
        w_out_cross.append(
            remote(
                held, held, wo_s.at[3, j], wo_r.at[3, j],
                jnp.where(core == 0, me_c, c_peer(2 * j)), jnp.where(core == 0, near, me_s),
            )
        )
        held = w_out_at(me_y, c_from(2 * j))
        w_out_second.append(
            remote(held, held, wo_s.at[2, j], wo_r.at[2, j], mate, me_s)
        )

    own[2].wait()
    for copy in cot_far:
        copy.wait_recv()

    def gate_rows(index, _):
        at = rows_of(index, 16)
        x_cot[at] = (cot_all[at].astype(f32) * vecs[2]).astype(bf16)
        return 0

    lax.fori_loop(0, run // 16, gate_rows, 0)

    for j in range(1, half):
        held = w_out_at(1 - me_y, c_from(2 * j))
        link(held, held, wo_s.at[3, j], wo_r.at[3, j], me_c, near).wait_recv()
        w_out_second.append(
            remote(held, held, wo_s.at[4, j], wo_r.at[4, j], mate, me_s)
        )
    for copy in w_out_second:
        copy.wait_recv()

    def d_attended(y):
        block = jnp.zeros((run, groups * HEAD), f32)
        for c in range(nc):
            block = block + dot_nt(x_cot[:, c * piece : (c + 1) * piece], w_out_all[y, c])
        return block.astype(bf16)

    d_away[...] = d_attended(1 - me_y)
    d_move = remote(
        d_away, d_att.at[rows_of(me_y, run)], ex_s.at[1], ex_r.at[1], me_c, near
    )
    d_att[rows_of(me_y, run)] = d_attended(me_y)
    for j in range(1, half):
        mix_chip(j)

    def back_norm(d_rot, raw, cos, sin):
        inverse = inverse_rms(raw)
        normed = raw * inverse
        d_normed = d_rot * cos - swap_pairs(d_rot) * sin
        return inverse * (d_normed - normed * jnp.mean(d_normed * normed, -1, keepdims=True))

    def query_part(h, y):
        at = rows_of(y, run)
        d_heads = d_att[at, head_at(h)]
        share = probs[h, at]
        d_values = dot_tn(share.astype(bf16), d_heads)
        d_probs = dot_nt(d_heads, v_all[h])
        d_scores = (share * (d_probs - jnp.sum(share * d_probs, -1, keepdims=True))).astype(bf16)
        d_qrot = jnp.dot(d_scores, k_all[h], preferred_element_type=f32) * score_scale
        d_krot = dot_tn(d_scores, q_all[h, at])
        d_query = back_norm(d_qrot, proj[h, at, 0:HEAD], cos_ref[at], sin_ref[at])
        d_proj[at, head_at(3 * h)] = d_query.astype(bf16)
        return d_values, d_krot

    def first_half(h, _):
        d_values, d_krot = query_part(h, me_y)
        value_sum[h] = d_values
        key_sum[h] = d_krot
        return 0

    lax.fori_loop(0, groups, first_half, 0)
    d_move.wait_recv()

    def second_half(h, _):
        d_values, d_krot = query_part(h, 1 - me_y)
        d_key = back_norm(
            (key_sum[h] + d_krot) * score_scale, proj[h, :, HEAD : 2 * HEAD],
            cos_ref[...], sin_ref[...],
        )
        d_proj[:, head_at(3 * h + 1)] = d_key.astype(bf16)
        d_proj[:, head_at(3 * h + 2)] = (value_sum[h] + d_values).astype(bf16)
        return 0

    lax.fori_loop(0, groups, second_half, 0)

    order = []
    low, high = 0, nz - 1
    for i in range(nz):
        take = (me_z - low >= high - me_z).astype(jnp.int32)
        order.append(take * low + (1 - take) * high)
        low, high = low + take, high - (1 - take)

    d_near = [[None] * CHUNKS for _ in range(nz)]

    def away(i, j):
        at = (rows_of(order[i], rows), pl.ds(j * chunk, chunk))
        d_near[i][j] = remote(
            dm_away.at[at], dm_near.at[at], dmn_s.at[i, j], dmn_r.at[i, j], me_c, near
        )

    for j in range(CHUNKS):
        part_cols = slice(j * chunk, (j + 1) * chunk)
        dm_away[:, part_cols] = dot_nt(
            d_proj[rows_of(1 - me_y, run)], w_in_all[part_cols]
        ).astype(bf16)
        away(0, j)
    for i in range(1, nz):
        for j in range(CHUNKS):
            away(i, j)
    for j in range(CHUNKS):
        part_cols = slice(j * chunk, (j + 1) * chunk)
        dm_here[:, part_cols] = dot_nt(
            d_proj[rows_of(me_y, run)], w_in_all[part_cols]
        ).astype(bf16)

    chain = []
    for i in range(nz - 1):
        to = order[i]
        up = to > me_z
        dirn = 1 - up.astype(jnp.int32)
        fed = (up & (me_z > 0)) | (~up & (me_z < nz - 1))
        beside = z_seq(me_z + 1 - 2 * dirn)
        for j in range(CHUNKS):
            at = (rows_of(to, rows), pl.ds(j * chunk, chunk))
            d_near[i][j].wait_recv()
            hop = link(
                dm_sum.at[at], chain_in.at[(dirn,) + at], ch_s.at[dirn, to, j],
                ch_r.at[dirn, to, j], me_c, beside,
            )
            value = dm_here[at].astype(f32) + dm_near[at].astype(f32)

            @pl.when(fed)
            def _():
                hop.wait_recv()
                dm_sum[at] = (value + chain_in[(dirn,) + at].astype(f32)).astype(bf16)

            @pl.when(~fed)
            def _():
                dm_sum[at] = value.astype(bf16)

            hop.start()
            chain.append(hop)

    for copy in mixed:
        copy.wait_recv()
    for start in range(0, rows, 16):
        mine_at = pl.ds(pl.multiple_of(me_z * rows + start, 16), 16)
        lat_rows = pl.ds(pl.multiple_of(place(me_s) * rows + start, 16), 16)
        for c in range(nc):
            value = mix_out[c, mine_at].astype(f32)
            for k in range(1, nz):
                value = value + mix_in[lax.rem(me_z + k, nz), c, start : start + 16].astype(f32)
            part_cols = slice(c * piece, (c + 1) * piece)
            block_ref[start : start + 16, part_cols] = (
                lat_all[lat_rows, part_cols].astype(f32) + vecs[2, :, part_cols] * value
            ).astype(bf16)

    for j in range(CHUNKS):
        part_cols = pl.ds(j * chunk, chunk)
        at = (rows_of(me_z, rows), part_cols)
        d_near[nz - 1][j].wait_recv()
        total[:, part_cols] = dm_here[at].astype(f32) + dm_near[at].astype(f32)
        for dirn, fed in ((0, me_z > 0), (1, me_z < nz - 1)):
            @pl.when(fed)
            def _():
                landed = chain_in.at[(dirn,) + at]
                link(
                    landed, landed, ch_s.at[dirn, me_z, j], ch_r.at[dirn, me_z, j], me_c, near
                ).wait_recv()
                total[:, part_cols] += landed[...].astype(f32)

    for start in range(0, rows, 16):
        lat_rows = pl.ds(pl.multiple_of(place(me_s) * rows + start, 16), 16)
        cot_rows = pl.ds(pl.multiple_of(me_z * rows + start, 16), 16)
        normed, inverse_std = layer_norm(lat_all[lat_rows].astype(f32))
        d_normed = total[start : start + 16] * (1.0 + vecs[1])
        grad_ref[start : start + 16] = cot_all[cot_rows].astype(f32) + inverse_std * (
            d_normed
            - jnp.mean(d_normed, -1, keepdims=True)
            - normed * jnp.mean(d_normed * normed, -1, keepdims=True)
        )

    for p in range(PARTS):
        for dirn in range(2):
            for hop in range(nz - 1):
                @pl.when(exists(dirn, hop) & beyond(dirn))
                def _():
                    held = lat_at(source(dirn, hop), me_y, p)
                    z_send(dirn, hop, p, held, source(dirn, hop)).wait_send()
            for hop in range(1, nz):
                @pl.when(exists(dirn, hop))
                def _():
                    y_link(dirn, hop, p).wait_send()
    for copy in (
        done + m1 + m2 + sum(w_in_far, []) + [w_in_mate] + w_in_second + w_out_far
        + [w_out_mate, w_out_near, w_out_near_mate] + w_out_second + w_out_cross + cot_far
        + [att_move, d_move] + mixed + sum(d_near, []) + chain
    ):
        copy.wait_send()


def on_device(latent, timesteps, positions, mod_weight, input_weight, output_weight, cotangent):
    nc = lax.axis_size("cand")
    ns = lax.axis_size("seq")
    rows, width = latent.shape[1:]
    length = rows * ns
    slab = input_weight.shape[0]
    groups = input_weight.shape[1]
    cols = mod_weight.shape[1]
    piece = output_weight.shape[2]
    half = nc // 2
    nz = ns // 2
    run = nz * rows
    vmem = pl.BlockSpec(memory_space=pltpu.VMEM)
    smem = pl.BlockSpec(memory_space=pltpu.SMEM)
    anywhere = pl.BlockSpec(memory_space=pl.ANY)
    f32, bf16 = jnp.float32, jnp.bfloat16
    dma = pltpu.SemaphoreType.DMA
    block_out, latent_grad = pl.pallas_call(
        functools.partial(step_kernel, nc, ns),
        out_shape=(
            jax.ShapeDtypeStruct((rows, width), bf16),
            jax.ShapeDtypeStruct((rows, width), f32),
        ),
        in_specs=[smem, vmem] + [anywhere] * 5,
        out_specs=(vmem, vmem),
        scratch_shapes=[
            pltpu.VMEM(mod_weight.shape, bf16),
            pltpu.VMEM((8, length), f32),
            pltpu.VMEM((length, HEAD), f32),
            pltpu.VMEM((length, HEAD), f32),
            pltpu.VMEM((length, HEAD), f32),
            pltpu.VMEM((nc, 1, cols), f32),
            pltpu.VMEM((nc, 1, cols), f32),
            pltpu.VMEM((1, cols), f32),
            pltpu.VMEM((ns, 1, cols), f32),
            pltpu.VMEM((3, 1, width), f32),
            pltpu.VMEM((length, width), bf16),
            pltpu.VMEM((length, width), bf16),
            pltpu.VMEM((slab * nc, groups * 3 * HEAD), bf16),
            pltpu.VMEM((2, nc, groups * HEAD, piece), bf16),
            pltpu.VMEM((run, width), bf16),
            pltpu.VMEM((run, width), bf16),
            pltpu.VMEM((groups, length, 3 * HEAD), f32),
            pltpu.VMEM((groups, length, HEAD), bf16),
            pltpu.VMEM((groups, length, HEAD), bf16),
            pltpu.VMEM((groups, length, HEAD), bf16),
            pltpu.VMEM((groups, length, length), f32),
            pltpu.VMEM((length, groups * HEAD), bf16),
            pltpu.VMEM((run, groups * HEAD), bf16),
            pltpu.VMEM((length, groups * HEAD), bf16),
            pltpu.VMEM((run, groups * HEAD), bf16),
            pltpu.VMEM((length, groups * 3 * HEAD), bf16),
            pltpu.VMEM((groups, length, HEAD), f32),
            pltpu.VMEM((groups, length, HEAD), f32),
            pltpu.VMEM((nc, run, piece), bf16),
            pltpu.VMEM((nz, nc, rows, piece), bf16),
            pltpu.VMEM((run, width), bf16),
            pltpu.VMEM((run, width), bf16),
            pltpu.VMEM((run, width), bf16),
            pltpu.VMEM((run, width), bf16),
            pltpu.VMEM((2, run, width), bf16),
            pltpu.VMEM((rows, width), f32),
            dma((5,)),
            dma((2, nz, PARTS)), dma((2, nz, PARTS)),
            dma((2 * nz, PARTS)), dma((2 * nz, PARTS)),
            dma((half, SLABS)), dma((half, SLABS)), dma((half, SLABS)), dma((half, SLABS)),
            dma((5, half)), dma((5, half)), dma((nc,)), dma((nc,)), dma((ns,)), dma((ns,)),
            dma((nz,)), dma((nz,)), dma((2,)), dma((2,)), dma((nz, half)), dma((nz, half)),
            dma((nz, CHUNKS)), dma((nz, CHUNKS)), dma((2, nz, CHUNKS)), dma((2, nz, CHUNKS)),
        ],
        compiler_params=pltpu.CompilerParams(
            collective_id=0, has_side_effects=True, vmem_limit_bytes=66000000
        ),
    )(
        timesteps, positions, mod_weight, latent[0], cotangent[0],
        input_weight.reshape(slab, groups * 3 * HEAD),
        output_weight.reshape(groups * HEAD, piece),
    )
    return (block_out[None], latent_grad[None])


def solution(mesh):
    placed = (
        P("cand", "seq", None),
        P(),
        P(),
        P("cand", "seq"),
        P("cand", "seq", None),
        P("seq", None, "cand"),
        P("cand", "seq", None),
    )
    return jax.shard_map(
        on_device,
        mesh=mesh,
        in_specs=placed,
        out_specs=(P("cand", "seq", None), P("cand", "seq", None)),
        check_vma=False,
    )
```

```python
import functools
import math

import jax
import jax.numpy as jnp
from jax import lax
from jax.experimental import pallas as pl
from jax.experimental.pallas import tpu as pltpu
from jax.sharding import PartitionSpec as P

HEAD = 128
CHUNKS = 4
PARTS = 3
SLABS = 4
MESH = pl.DeviceIdType.MESH


epsilon = 1e-06


def swap_pairs(values):
    lane = lax.broadcasted_iota(jnp.int32, values.shape, 1)
    small = HEAD // 8
    large = (HEAD - small) // 2
    near = jnp.where(
        lane < small // 2,
        pltpu.roll(values, HEAD - small // 2, 1),
        pltpu.roll(values, small // 2, 1),
    )
    upper = ((lane >= small) & (lane < small + large // 2)) | (
        (lane >= small + large) & (lane < small + large + large // 2)
    )
    far = jnp.where(
        upper, pltpu.roll(values, HEAD - large // 2, 1), pltpu.roll(values, large // 2, 1)
    )
    return jnp.where(lane < small, near, far)


def dot_nt(left, right):
    return lax.dot_general(left, right, (((1,), (1,)), ((), ())), preferred_element_type=jnp.float32)


def dot_tn(left, right):
    return lax.dot_general(left, right, (((0,), (0,)), ((), ())), preferred_element_type=jnp.float32)


def inverse_rms(values):
    return lax.rsqrt(jnp.mean(values * values, -1, keepdims=True) + epsilon)


def layer_norm(values):
    centred = values - jnp.mean(values, -1, keepdims=True)
    inverse_std = lax.rsqrt(jnp.mean(centred * centred, -1, keepdims=True) + epsilon)
    return (centred * inverse_std, inverse_std)


def sections():
    first = HEAD // 8
    other = (HEAD - first) // 2
    return ((0, first), (first, other), (first + other, other))


def step_kernel(
    nc, ns,
    time_ref, pos_ref, mod_w_ref, latent_ref, cot_ref, w_in_ref, w_out_ref,
    block_ref, grad_ref,
    mod_w, pos8, angle, cos_ref, sin_ref, part, part_in, mine, mod_all, vecs,
    lat_all, x_all, w_in_all, w_out_all, cot_all, x_cot, proj, q_all, k_all, v_all, probs,
    att, att_near, d_att, d_away, d_proj, key_sum, value_sum, mix_out, mix_in,
    dm_away, dm_here, dm_near, dm_sum, chain_in, total,
    own_sem, lat_s, lat_r, laty_s, laty_r, wi_s, wi_r, wif_s, wif_r, wo_s, wo_r, m1_s, m1_r,
    m2_s, m2_r, cot_s, cot_r, ex_s, ex_r, mx_s, mx_r, dmn_s, dmn_r, ch_s, ch_r,
):
    me_c = lax.axis_index("cand")
    me_s = lax.axis_index("seq")
    rows, width = latent_ref.shape
    length = rows * ns
    slab = w_in_ref.shape[0]
    groups = q_all.shape[0]
    cols = mod_w_ref.shape[1]
    piece = w_out_ref.shape[1]
    chunk = width // CHUNKS
    half = nc // 2
    core = lax.rem(me_c, 2)
    mate = me_c + 1 - 2 * core
    nz = ns // 2
    me_y, me_z = lax.rem(me_s, 2), lax.div(me_s, 2)
    near = me_s + 1 - 2 * me_y
    score_scale = HEAD ** (-0.5)
    size = rows // PARTS
    span = slab // SLABS
    run = nz * rows
    f32, bf16 = jnp.float32, jnp.bfloat16

    def place(index):
        return lax.rem(index, 2) * nz + lax.div(index, 2)

    def rows_of(index, count):
        return pl.ds(pl.multiple_of(index * count, count), count)

    def link(src, dst, send, recv, cand, seq):
        return pltpu.make_async_remote_copy(
            src_ref=src, dst_ref=dst, send_sem=send, recv_sem=recv,
            device_id=(cand, seq), device_id_type=MESH,
        )

    def remote(*args):
        copy = link(*args)
        copy.start()
        return copy

    def c_peer(k):
        return lax.rem(me_c + k, nc)

    def c_from(k):
        return lax.rem(me_c - k + nc, nc)

    def z_seq(z):
        return 2 * z + me_y

    barrier = pltpu.get_barrier_semaphore()
    for k in range(1, nc):
        pl.semaphore_signal(barrier, inc=1, device_id=(c_peer(k), me_s), device_id_type=MESH)
    for k in range(1, ns):
        pl.semaphore_signal(
            barrier, inc=1, device_id=(me_c, lax.rem(me_s + k, ns)), device_id_type=MESH
        )

    def w_in_at(index, q):
        return w_in_all.at[pl.ds(pl.multiple_of(index * slab + q * span, span), span)]

    own = [
        pltpu.make_async_copy(mod_w_ref, mod_w, own_sem.at[0]),
        pltpu.make_async_copy(latent_ref, lat_all.at[rows_of(place(me_s), rows)], own_sem.at[1]),
        pltpu.make_async_copy(cot_ref, cot_all.at[rows_of(me_z, rows)], own_sem.at[2]),
        pltpu.make_async_copy(w_in_ref, w_in_all.at[rows_of(me_c, slab)], own_sem.at[3]),
        pltpu.make_async_copy(w_out_ref, w_out_all.at[me_y, me_c], own_sem.at[4]),
    ]
    for copy in own:
        copy.start()
    pl.semaphore_wait(barrier, nc - 1 + ns - 1)

    def lat_at(z, y, p):
        return lat_all.at[pl.ds(pl.multiple_of((y * nz + z) * rows + p * size, size), size)]

    done = []

    def z_send(dirn, hop, p, src, z):
        to = me_z + 1 - 2 * dirn
        return link(
            src, lat_at(z, me_y, p), lat_s.at[dirn, hop, p], lat_r.at[dirn, hop, p],
            me_c, z_seq(to),
        )

    for p in range(PARTS):
        src = latent_ref.at[pl.ds(p * size, size)]
        for dirn, there in ((0, me_z < nz - 1), (1, me_z > 0)):
            @pl.when(there)
            def _():
                z_send(dirn, 0, p, src, me_z).start()
        done.append(
            remote(src, lat_at(me_z, me_y, p), laty_s.at[0, p], laty_r.at[0, p], me_c, near)
        )

    def slab_part(q):
        src = w_in_ref.at[pl.ds(q * span, span)]
        return [
            remote(src, w_in_at(me_c, q), wi_s.at[j, q], wi_r.at[j, q], c_peer(2 * j), me_s)
            for j in range(1, half)
        ]

    w_in_far = [slab_part(0)]

    count = part.shape[0]
    lead = mod_w_ref.shape[0]
    held_rows = max(16, nc)
    index = me_c * lead + lax.broadcasted_iota(jnp.int32, (held_rows, lead), 1)
    steps = width // 2
    is_cos = index < steps
    order = jnp.where(is_cos, index, index - steps).astype(f32)
    row = lax.broadcasted_iota(jnp.int32, (held_rows, 1), 0)
    times = jnp.zeros((held_rows, 1), f32)
    for c in range(nc):
        times = jnp.where(row == c, time_ref[c].astype(f32), times)
    turns = times * jnp.exp(order * (-math.log(10000.0)) / steps)
    wave = jnp.where(is_cos, jnp.cos(turns), jnp.sin(turns))
    act = (wave / (1.0 + jnp.exp(-wave))).astype(bf16)
    own[0].wait()
    product = jnp.dot(act, mod_w[...], preferred_element_type=f32)
    for c in range(count):
        part[c] = product[c : c + 1]
    m1 = []
    for k in range(1, nc):
        peer = c_peer(k)
        m1.append(remote(part.at[peer], part_in.at[me_c], m1_s.at[k], m1_r.at[k], peer, me_s))
    for q in range(1, SLABS):
        w_in_far.append(slab_part(q))
    w_in_mate = remote(
        w_in_ref, w_in_all.at[rows_of(me_c, slab)], wif_s.at[0, 0], wif_r.at[0, 0], mate, me_s
    )

    def w_out_at(y, c):
        return w_out_all.at[y, c]

    w_out_far = [
        remote(w_out_ref, w_out_at(me_y, me_c), wo_s.at[0, j], wo_r.at[0, j], c_peer(2 * j), me_s)
        for j in range(1, half)
    ]
    w_out_mate = remote(
        w_out_ref, w_out_at(me_y, me_c), wo_s.at[0, 0], wo_r.at[0, 0], mate, me_s
    )

    pos8[...] = jnp.zeros_like(pos8)
    pos8[0 : pos_ref.shape[0]] = pos_ref[...].astype(f32)
    lane = lax.broadcasted_iota(jnp.int32, (8, HEAD), 1)
    axis = lax.broadcasted_iota(jnp.int32, (8, HEAD), 0)
    rate = jnp.zeros((8, HEAD), f32)
    sign = jnp.ones((8, HEAD), f32)
    for a, (start, extent) in enumerate(sections()):
        inside = (lane >= start) & (lane < start + extent)
        late = inside & (lane >= start + extent // 2)
        pair = jnp.where(late, lane - start - extent // 2, lane - start).astype(f32)
        value = jnp.exp(pair * (-math.log(256.0) * 2.0 / extent))
        rate = jnp.where(inside & (axis == a), value, rate)
        sign = jnp.where(inside & ~late, -1.0, sign)
    angle[...] = lax.dot_general(
        pos8[...], rate, (((0,), (0,)), ((), ())), preferred_element_type=f32,
        precision=lax.Precision.HIGHEST,
    )

    def turn_rows(s, _):
        turned = angle[rows_of(s, rows)]
        at = rows_of(place(s), rows)
        cos_ref[at] = jnp.cos(turned)
        sin_ref[at] = jnp.sin(turned) * sign[0:1]
        return 0

    lax.fori_loop(0, ns, turn_rows, 0)

    def exists(dirn, hop):
        return me_z >= hop if dirn == 0 else me_z <= nz - 1 - hop

    def beyond(dirn):
        return me_z < nz - 1 if dirn == 0 else me_z > 0

    def source(dirn, hop):
        return me_z - hop if dirn == 0 else me_z + hop

    def y_slot(dirn, hop):
        return hop if dirn == 0 else nz - 1 + hop

    def y_link(dirn, hop, p):
        held = lat_at(source(dirn, hop), me_y, p)
        slot = y_slot(dirn, hop)
        return link(held, held, laty_s.at[slot, p], laty_r.at[slot, p], me_c, near)

    def relay(hop):
        for p in range(PARTS):
            for dirn in range(2):
                @pl.when(exists(dirn, hop))
                def _():
                    z = source(dirn, hop)
                    held = lat_at(z, me_y, p)
                    z_send(dirn, hop - 1, p, held, z).wait_recv()
                    if hop < nz - 1:
                        @pl.when(beyond(dirn))
                        def _():
                            z_send(dirn, hop, p, held, z).start()
                    y_link(dirn, hop, p).start()

    relay(1)
    for copy in m1:
        copy.wait_recv()
    summed_mod = part[me_c]
    for k in range(1, nc):
        summed_mod = summed_mod + part_in[c_from(k)]
    mine[...] = summed_mod
    mod_all[me_s] = summed_mod
    m2 = [
        remote(
            mine, mod_all.at[me_s], m2_s.at[k], m2_r.at[k], me_c, lax.rem(me_s + k, ns)
        )
        for k in range(1, ns)
    ]
    for hop in range(2, nz - 1):
        relay(hop)

    def cot_at(z, p):
        return cot_all.at[pl.ds(pl.multiple_of(z * rows + p * size, size), size)]

    def cot_send(dirn, hop, p, src, z):
        return link(
            src, cot_at(z, p), cot_s.at[dirn, hop, p], cot_r.at[dirn, hop, p],
            me_c, z_seq(me_z + 1 - 2 * dirn),
        )

    for p in range(PARTS):
        for dirn in range(2):
            @pl.when(beyond(dirn))
            def _():
                cot_send(dirn, 0, p, cot_ref.at[pl.ds(p * size, size)], me_z).start()

    def cot_relay(hop):
        for p in range(PARTS):
            for dirn in range(2):
                @pl.when(exists(dirn, hop))
                def _():
                    z = source(dirn, hop)
                    cot_send(dirn, hop - 1, p, cot_at(z, p), z).wait_recv()
                    if hop < nz - 1:
                        @pl.when(beyond(dirn))
                        def _():
                            cot_send(dirn, hop, p, cot_at(z, p), z).start()

    def gate_rows(z):
        def body(index, _):
            at = pl.ds(pl.multiple_of(z * rows + index * 16, 16), 16)
            x_cot[at] = (cot_all[at].astype(f32) * vecs[2]).astype(bf16)
            return 0

        lax.fori_loop(0, rows // 16, body, 0)

    def gate_hop(hop):
        for dirn in range(2):
            @pl.when(exists(dirn, hop))
            def _():
                gate_rows(source(dirn, hop))

    for copy in m2:
        copy.wait_recv()
    for s in range(ns):
        at = s * cols
        while at < (s + 1) * cols:
            kind = at // width
            stop = min((s + 1) * cols, (kind + 1) * width)
            vecs[kind, :, at - kind * width : stop - kind * width] = mod_all[
                s, :, at - s * cols : stop - s * cols
            ]
            at = stop

    def norm_rows(at):
        normed, _inverse = layer_norm(lat_all[at].astype(f32))
        x_all[at] = (normed * (1.0 + vecs[1]) + vecs[0]).astype(bf16)

    def norm_run(start, count):
        def body(i, _):
            norm_rows(pl.ds(pl.multiple_of(start + i * 16, 16), 16))
            return 0

        lax.fori_loop(0, count // 16, body, 0)

    own[1].wait()
    norm_run(place(me_s) * rows, rows)
    for dirn in range(2):
        for hop in range(1, nz - 1):
            @pl.when(exists(dirn, hop))
            def _():
                norm_run((me_y * nz + source(dirn, hop)) * rows, rows)

    if nz > 1:
        relay(nz - 1)
        for dirn in range(2):
            @pl.when(exists(dirn, nz - 1))
            def _():
                norm_run((me_y * nz + source(dirn, nz - 1)) * rows, rows)

    w_out_near = remote(
        w_out_ref, w_out_at(me_y, me_c), wo_s.at[1, 0], wo_r.at[1, 0], me_c, near
    )

    w_in_second = []

    def slab_forward(q):
        for j in range(1, half):
            w_in_far[q][j - 1].wait_recv()
            held = w_in_at(c_from(2 * j), q)
            w_in_second.append(
                remote(held, held, wif_s.at[j, q], wif_r.at[j, q], mate, me_s)
            )

    for q in range(SLABS - 1):
        slab_forward(q)
    for copy in done:
        copy.wait_recv()
    norm_run(((1 - me_y) * nz + me_z) * rows, rows)
    for hop in range(1, nz):
        if hop == nz - 1 and nz > 2:
            cot_relay(1)
        for dirn in range(2):
            @pl.when(exists(dirn, hop))
            def _():
                for p in range(PARTS):
                    y_link(dirn, hop, p).wait_recv()
                norm_run(((1 - me_y) * nz + source(dirn, hop)) * rows, rows)
    slab_forward(SLABS - 1)
    own[3].wait()
    w_in_mate.wait_recv()
    for copy in w_in_second:
        copy.wait_recv()

    tile = 3 * HEAD

    def project(index, _):
        at = pl.ds(pl.multiple_of(index * tile, tile), tile)
        proj[index] = jnp.dot(x_all[...], w_in_all[:, at], preferred_element_type=f32)
        return 0

    lax.fori_loop(0, groups, project, 0)
    for hop in range(2, nz - 1):
        cot_relay(hop)

    def head_at(h):
        return pl.ds(pl.multiple_of(h * HEAD, HEAD), HEAD)

    def head_forward(h, _):
        query = proj[h, :, 0:HEAD]
        key = proj[h, :, HEAD : 2 * HEAD]
        query_n = query * inverse_rms(query)
        key_n = key * inverse_rms(key)
        q_rot = (query_n * cos_ref[...] + swap_pairs(query_n) * sin_ref[...]).astype(bf16)
        k_rot = (key_n * cos_ref[...] + swap_pairs(key_n) * sin_ref[...]).astype(bf16)
        values = proj[h, :, 2 * HEAD :].astype(bf16)
        q_all[h] = q_rot
        k_all[h] = k_rot
        v_all[h] = values
        weights = jnp.exp(dot_nt(q_rot, k_rot) * score_scale - HEAD**0.5)
        share = weights * (1.0 / jnp.sum(weights, -1, keepdims=True))
        probs[h] = share
        att[:, head_at(h)] = jnp.dot(
            share.astype(bf16), values, preferred_element_type=f32
        ).astype(bf16)
        return 0

    lax.fori_loop(0, groups, head_forward, 0)
    att_move = remote(
        att.at[rows_of(1 - me_y, run)], att_near, ex_s.at[0], ex_r.at[0], me_c, near
    )

    def att_rows(which):
        return att[rows_of(me_y, run)] if which == 0 else att_near[...]

    mixed = []

    def mix_chip(j):
        first = 2 * lax.rem(lax.div(me_c, 2) + j, half)
        for b in range(2):
            mix_out[first + b] = (
                jnp.dot(att_rows(0), w_out_all[me_y, first + b], preferred_element_type=f32)
                + jnp.dot(att_rows(1), w_out_all[1 - me_y, first + b], preferred_element_type=f32)
            ).astype(bf16)
        for k in range(1, nz):
            peer = lax.rem(me_z + k, nz)
            mixed.append(
                remote(
                    mix_out.at[pl.ds(first, 2), rows_of(peer, rows)],
                    mix_in.at[me_z, pl.ds(first, 2)],
                    mx_s.at[k, j], mx_r.at[k, j], me_c, z_seq(peer),
                )
            )

    w_out_near.wait_recv()
    held = w_out_at(1 - me_y, me_c)
    w_out_near_mate = remote(held, held, wo_s.at[2, 0], wo_r.at[2, 0], mate, me_s)
    w_out_second = []
    w_out_cross = []
    for j in range(1, half):
        w_out_far[j - 1].wait_recv()
        held = w_out_all.at[
            jnp.where(core == 0, me_y, 1 - me_y), jnp.where(core == 0, c_from(2 * j), me_c)
        ]
        w_out_cross.append(
            remote(
                held, held, wo_s.at[3, j], wo_r.at[3, j],
                jnp.where(core == 0, me_c, c_peer(2 * j)), jnp.where(core == 0, near, me_s),
            )
        )
        held = w_out_at(me_y, c_from(2 * j))
        w_out_second.append(
            remote(held, held, wo_s.at[2, j], wo_r.at[2, j], mate, me_s)
        )

    own[4].wait()
    w_out_mate.wait_recv()
    att_move.wait_recv()
    w_out_near_mate.wait_recv()
    mix_chip(0)

    own[2].wait()
    gate_rows(me_z)
    for hop in range(1, nz - 1):
        gate_hop(hop)
    cot_relay(nz - 1)
    gate_hop(nz - 1)

    for j in range(1, half):
        held = w_out_at(1 - me_y, c_from(2 * j))
        link(held, held, wo_s.at[3, j], wo_r.at[3, j], me_c, near).wait_recv()
        w_out_second.append(
            remote(held, held, wo_s.at[4, j], wo_r.at[4, j], mate, me_s)
        )
    for copy in w_out_second:
        copy.wait_recv()

    def d_attended(y):
        block = jnp.zeros((run, groups * HEAD), f32)
        for c in range(nc):
            block = block + dot_nt(x_cot[:, c * piece : (c + 1) * piece], w_out_all[y, c])
        return block.astype(bf16)

    d_away[...] = d_attended(1 - me_y)
    d_move = remote(
        d_away, d_att.at[rows_of(me_y, run)], ex_s.at[1], ex_r.at[1], me_c, near
    )
    d_att[rows_of(me_y, run)] = d_attended(me_y)
    for j in range(1, half):
        mix_chip(j)

    def back_norm(d_rot, raw, cos, sin):
        inverse = inverse_rms(raw)
        normed = raw * inverse
        d_normed = d_rot * cos - swap_pairs(d_rot) * sin
        return inverse * (d_normed - normed * jnp.mean(d_normed * normed, -1, keepdims=True))

    def query_part(h, y):
        at = rows_of(y, run)
        d_heads = d_att[at, head_at(h)]
        share = probs[h, at]
        d_values = dot_tn(share.astype(bf16), d_heads)
        d_probs = dot_nt(d_heads, v_all[h])
        d_scores = (share * (d_probs - jnp.sum(share * d_probs, -1, keepdims=True))).astype(bf16)
        d_qrot = jnp.dot(d_scores, k_all[h], preferred_element_type=f32) * score_scale
        d_krot = dot_tn(d_scores, q_all[h, at])
        d_query = back_norm(d_qrot, proj[h, at, 0:HEAD], cos_ref[at], sin_ref[at])
        d_proj[at, head_at(3 * h)] = d_query.astype(bf16)
        return d_values, d_krot

    def first_half(h, _):
        d_values, d_krot = query_part(h, me_y)
        value_sum[h] = d_values
        key_sum[h] = d_krot
        return 0

    lax.fori_loop(0, groups, first_half, 0)
    d_move.wait_recv()

    def second_half(h, _):
        d_values, d_krot = query_part(h, 1 - me_y)
        d_key = back_norm(
            (key_sum[h] + d_krot) * score_scale, proj[h, :, HEAD : 2 * HEAD],
            cos_ref[...], sin_ref[...],
        )
        d_proj[:, head_at(3 * h + 1)] = d_key.astype(bf16)
        d_proj[:, head_at(3 * h + 2)] = (value_sum[h] + d_values).astype(bf16)
        return 0

    lax.fori_loop(0, groups, second_half, 0)

    order = []
    low, high = 0, nz - 1
    for i in range(nz):
        take = (me_z - low >= high - me_z).astype(jnp.int32)
        order.append(take * low + (1 - take) * high)
        low, high = low + take, high - (1 - take)

    d_near = [[None] * CHUNKS for _ in range(nz)]

    def away(i, j):
        at = (rows_of(order[i], rows), pl.ds(j * chunk, chunk))
        d_near[i][j] = remote(
            dm_away.at[at], dm_near.at[at], dmn_s.at[i, j], dmn_r.at[i, j], me_c, near
        )

    for j in range(CHUNKS):
        part_cols = slice(j * chunk, (j + 1) * chunk)
        dm_away[:, part_cols] = dot_nt(
            d_proj[rows_of(1 - me_y, run)], w_in_all[part_cols]
        ).astype(bf16)
        away(0, j)
    for i in range(1, nz):
        for j in range(CHUNKS):
            away(i, j)
    for j in range(CHUNKS):
        part_cols = slice(j * chunk, (j + 1) * chunk)
        dm_here[:, part_cols] = dot_nt(
            d_proj[rows_of(me_y, run)], w_in_all[part_cols]
        ).astype(bf16)

    chain = []
    for i in range(nz - 1):
        to = order[i]
        up = to > me_z
        dirn = 1 - up.astype(jnp.int32)
        fed = (up & (me_z > 0)) | (~up & (me_z < nz - 1))
        beside = z_seq(me_z + 1 - 2 * dirn)
        for j in range(CHUNKS):
            at = (rows_of(to, rows), pl.ds(j * chunk, chunk))
            d_near[i][j].wait_recv()
            hop = link(
                dm_sum.at[at], chain_in.at[(dirn,) + at], ch_s.at[dirn, to, j],
                ch_r.at[dirn, to, j], me_c, beside,
            )
            value = dm_here[at].astype(f32) + dm_near[at].astype(f32)

            @pl.when(fed)
            def _():
                hop.wait_recv()
                dm_sum[at] = (value + chain_in[(dirn,) + at].astype(f32)).astype(bf16)

            @pl.when(~fed)
            def _():
                dm_sum[at] = value.astype(bf16)

            hop.start()
            chain.append(hop)

    for copy in mixed:
        copy.wait_recv()
    for start in range(0, rows, 16):
        mine_at = pl.ds(pl.multiple_of(me_z * rows + start, 16), 16)
        lat_rows = pl.ds(pl.multiple_of(place(me_s) * rows + start, 16), 16)
        for c in range(nc):
            value = mix_out[c, mine_at].astype(f32)
            for k in range(1, nz):
                value = value + mix_in[lax.rem(me_z + k, nz), c, start : start + 16].astype(f32)
            part_cols = slice(c * piece, (c + 1) * piece)
            block_ref[start : start + 16, part_cols] = (
                lat_all[lat_rows, part_cols].astype(f32) + vecs[2, :, part_cols] * value
            ).astype(bf16)

    for j in range(CHUNKS):
        part_cols = pl.ds(j * chunk, chunk)
        at = (rows_of(me_z, rows), part_cols)
        d_near[nz - 1][j].wait_recv()
        total[:, part_cols] = dm_here[at].astype(f32) + dm_near[at].astype(f32)
        for dirn, fed in ((0, me_z > 0), (1, me_z < nz - 1)):
            @pl.when(fed)
            def _():
                landed = chain_in.at[(dirn,) + at]
                link(
                    landed, landed, ch_s.at[dirn, me_z, j], ch_r.at[dirn, me_z, j], me_c, near
                ).wait_recv()
                total[:, part_cols] += landed[...].astype(f32)

    for start in range(0, rows, 16):
        lat_rows = pl.ds(pl.multiple_of(place(me_s) * rows + start, 16), 16)
        cot_rows = pl.ds(pl.multiple_of(me_z * rows + start, 16), 16)
        normed, inverse_std = layer_norm(lat_all[lat_rows].astype(f32))
        d_normed = total[start : start + 16] * (1.0 + vecs[1])
        grad_ref[start : start + 16] = cot_all[cot_rows].astype(f32) + inverse_std * (
            d_normed
            - jnp.mean(d_normed, -1, keepdims=True)
            - normed * jnp.mean(d_normed * normed, -1, keepdims=True)
        )

    for p in range(PARTS):
        for dirn in range(2):
            for hop in range(nz - 1):
                @pl.when(exists(dirn, hop) & beyond(dirn))
                def _():
                    held = lat_at(source(dirn, hop), me_y, p)
                    z_send(dirn, hop, p, held, source(dirn, hop)).wait_send()
                    held = cot_at(source(dirn, hop), p)
                    cot_send(dirn, hop, p, held, source(dirn, hop)).wait_send()
            for hop in range(1, nz):
                @pl.when(exists(dirn, hop))
                def _():
                    y_link(dirn, hop, p).wait_send()
    for copy in (
        done + m1 + m2 + sum(w_in_far, []) + [w_in_mate] + w_in_second + w_out_far
        + [w_out_mate, w_out_near, w_out_near_mate] + w_out_second + w_out_cross
        + [att_move, d_move] + mixed + sum(d_near, []) + chain
    ):
        copy.wait_send()


def on_device(latent, timesteps, positions, mod_weight, input_weight, output_weight, cotangent):
    nc = lax.axis_size("cand")
    ns = lax.axis_size("seq")
    rows, width = latent.shape[1:]
    length = rows * ns
    slab = input_weight.shape[0]
    groups = input_weight.shape[1]
    cols = mod_weight.shape[1]
    piece = output_weight.shape[2]
    half = nc // 2
    nz = ns // 2
    run = nz * rows
    vmem = pl.BlockSpec(memory_space=pltpu.VMEM)
    smem = pl.BlockSpec(memory_space=pltpu.SMEM)
    anywhere = pl.BlockSpec(memory_space=pl.ANY)
    f32, bf16 = jnp.float32, jnp.bfloat16
    dma = pltpu.SemaphoreType.DMA
    block_out, latent_grad = pl.pallas_call(
        functools.partial(step_kernel, nc, ns),
        out_shape=(
            jax.ShapeDtypeStruct((rows, width), bf16),
            jax.ShapeDtypeStruct((rows, width), f32),
        ),
        in_specs=[smem, vmem] + [anywhere] * 5,
        out_specs=(vmem, vmem),
        scratch_shapes=[
            pltpu.VMEM(mod_weight.shape, bf16),
            pltpu.VMEM((8, length), f32),
            pltpu.VMEM((length, HEAD), f32),
            pltpu.VMEM((length, HEAD), f32),
            pltpu.VMEM((length, HEAD), f32),
            pltpu.VMEM((nc, 1, cols), f32),
            pltpu.VMEM((nc, 1, cols), f32),
            pltpu.VMEM((1, cols), f32),
            pltpu.VMEM((ns, 1, cols), f32),
            pltpu.VMEM((3, 1, width), f32),
            pltpu.VMEM((length, width), bf16),
            pltpu.VMEM((length, width), bf16),
            pltpu.VMEM((slab * nc, groups * 3 * HEAD), bf16),
            pltpu.VMEM((2, nc, groups * HEAD, piece), bf16),
            pltpu.VMEM((run, width), bf16),
            pltpu.VMEM((run, width), bf16),
            pltpu.VMEM((groups, length, 3 * HEAD), f32),
            pltpu.VMEM((groups, length, HEAD), bf16),
            pltpu.VMEM((groups, length, HEAD), bf16),
            pltpu.VMEM((groups, length, HEAD), bf16),
            pltpu.VMEM((groups, length, length), f32),
            pltpu.VMEM((length, groups * HEAD), bf16),
            pltpu.VMEM((run, groups * HEAD), bf16),
            pltpu.VMEM((length, groups * HEAD), bf16),
            pltpu.VMEM((run, groups * HEAD), bf16),
            pltpu.VMEM((length, groups * 3 * HEAD), bf16),
            pltpu.VMEM((groups, length, HEAD), f32),
            pltpu.VMEM((groups, length, HEAD), f32),
            pltpu.VMEM((nc, run, piece), bf16),
            pltpu.VMEM((nz, nc, rows, piece), bf16),
            pltpu.VMEM((run, width), bf16),
            pltpu.VMEM((run, width), bf16),
            pltpu.VMEM((run, width), bf16),
            pltpu.VMEM((run, width), bf16),
            pltpu.VMEM((2, run, width), bf16),
            pltpu.VMEM((rows, width), f32),
            dma((5,)),
            dma((2, nz, PARTS)), dma((2, nz, PARTS)),
            dma((2 * nz, PARTS)), dma((2 * nz, PARTS)),
            dma((half, SLABS)), dma((half, SLABS)), dma((half, SLABS)), dma((half, SLABS)),
            dma((5, half)), dma((5, half)), dma((nc,)), dma((nc,)), dma((ns,)), dma((ns,)),
            dma((2, nz, PARTS)), dma((2, nz, PARTS)), dma((2,)), dma((2,)), dma((nz, half)), dma((nz, half)),
            dma((nz, CHUNKS)), dma((nz, CHUNKS)), dma((2, nz, CHUNKS)), dma((2, nz, CHUNKS)),
        ],
        compiler_params=pltpu.CompilerParams(
            collective_id=0, has_side_effects=True, vmem_limit_bytes=66000000
        ),
    )(
        timesteps, positions, mod_weight, latent[0], cotangent[0],
        input_weight.reshape(slab, groups * 3 * HEAD),
        output_weight.reshape(groups * HEAD, piece),
    )
    return (block_out[None], latent_grad[None])


def solution(mesh):
    placed = (
        P("cand", "seq", None),
        P(),
        P(),
        P("cand", "seq"),
        P("cand", "seq", None),
        P("seq", None, "cand"),
        P("cand", "seq", None),
    )
    return jax.shard_map(
        on_device,
        mesh=mesh,
        in_specs=placed,
        out_specs=(P("cand", "seq", None), P("cand", "seq", None)),
        check_vma=False,
    )
```

```python
import functools
import math

import jax
import jax.numpy as jnp
from jax import lax
from jax.experimental import pallas as pl
from jax.experimental.pallas import tpu as pltpu
from jax.sharding import PartitionSpec as P

HEAD = 128
CHUNKS = 4
PARTS = 3
SLABS = 4
MESH = pl.DeviceIdType.MESH


epsilon = 1e-06


def swap_pairs(values):
    lane = lax.broadcasted_iota(jnp.int32, values.shape, 1)
    small = HEAD // 8
    large = (HEAD - small) // 2
    near = jnp.where(
        lane < small // 2,
        pltpu.roll(values, HEAD - small // 2, 1),
        pltpu.roll(values, small // 2, 1),
    )
    upper = ((lane >= small) & (lane < small + large // 2)) | (
        (lane >= small + large) & (lane < small + large + large // 2)
    )
    far = jnp.where(
        upper, pltpu.roll(values, HEAD - large // 2, 1), pltpu.roll(values, large // 2, 1)
    )
    return jnp.where(lane < small, near, far)


def dot_nt(left, right):
    return lax.dot_general(left, right, (((1,), (1,)), ((), ())), preferred_element_type=jnp.float32)


def dot_tn(left, right):
    return lax.dot_general(left, right, (((0,), (0,)), ((), ())), preferred_element_type=jnp.float32)


def inverse_rms(values):
    return lax.rsqrt(jnp.mean(values * values, -1, keepdims=True) + epsilon)


def layer_norm(values):
    centred = values - jnp.mean(values, -1, keepdims=True)
    inverse_std = lax.rsqrt(jnp.mean(centred * centred, -1, keepdims=True) + epsilon)
    return (centred * inverse_std, inverse_std)


def sections():
    first = HEAD // 8
    other = (HEAD - first) // 2
    return ((0, first), (first, other), (first + other, other))


def step_kernel(
    nc, ns,
    time_ref, pos_ref, mod_w_ref, latent_ref, cot_ref, w_in_ref, w_out_ref,
    block_ref, grad_ref,
    w_raw, mod_w, pos8, angle, cos_ref, sin_ref, part, part_in, mine, mod_all, vecs,
    lat_all, x_all, w_in_all, w_out_all, cot_all, x_cot, proj, q_all, k_all, v_all, probs,
    att, att_near, d_att, d_away, d_proj, key_sum, value_sum, mix_out, mix_in,
    dm_away, dm_here, dm_near, dm_sum, chain_in, total,
    own_sem, lat_s, lat_r, laty_s, laty_r, wi_s, wi_r, wif_s, wif_r, wo_s, wo_r, m1_s, m1_r,
    m2_s, m2_r, cot_s, cot_r, ex_s, ex_r, mx_s, mx_r, dmn_s, dmn_r, ch_s, ch_r,
):
    me_c = lax.axis_index("cand")
    me_s = lax.axis_index("seq")
    rows, width = latent_ref.shape
    length = rows * ns
    slab = w_in_ref.shape[0]
    groups = q_all.shape[0]
    cols = mod_w_ref.shape[1]
    piece = w_out_ref.shape[1]
    chunk = width // CHUNKS
    half = nc // 2
    core = lax.rem(me_c, 2)
    mate = me_c + 1 - 2 * core
    nz = ns // 2
    me_y, me_z = lax.rem(me_s, 2), lax.div(me_s, 2)
    near = me_s + 1 - 2 * me_y
    score_scale = HEAD ** (-0.5)
    size = rows // PARTS
    span = slab // SLABS
    run = nz * rows
    f32, bf16 = jnp.float32, jnp.bfloat16

    def place(index):
        return lax.rem(index, 2) * nz + lax.div(index, 2)

    def rows_of(index, count):
        return pl.ds(pl.multiple_of(index * count, count), count)

    def link(src, dst, send, recv, cand, seq):
        return pltpu.make_async_remote_copy(
            src_ref=src, dst_ref=dst, send_sem=send, recv_sem=recv,
            device_id=(cand, seq), device_id_type=MESH,
        )

    def remote(*args):
        copy = link(*args)
        copy.start()
        return copy

    def c_peer(k):
        return lax.rem(me_c + k, nc)

    def c_from(k):
        return lax.rem(me_c - k + nc, nc)

    def z_seq(z):
        return 2 * z + me_y

    barrier = pltpu.get_barrier_semaphore()
    for k in range(1, nc):
        pl.semaphore_signal(barrier, inc=1, device_id=(c_peer(k), me_s), device_id_type=MESH)
    for k in range(1, ns):
        pl.semaphore_signal(
            barrier, inc=1, device_id=(me_c, lax.rem(me_s + k, ns)), device_id_type=MESH
        )

    def w_in_at(index, q):
        return w_in_all.at[pl.ds(pl.multiple_of(index * slab + q * span, span), span)]

    own = [
        pltpu.make_async_copy(mod_w_ref, mod_w, own_sem.at[0]),
        pltpu.make_async_copy(latent_ref, lat_all.at[rows_of(place(me_s), rows)], own_sem.at[1]),
        pltpu.make_async_copy(cot_ref, cot_all.at[rows_of(me_z, rows)], own_sem.at[2]),
        pltpu.make_async_copy(w_in_ref, w_raw, own_sem.at[3]),
        pltpu.make_async_copy(w_out_ref, w_out_all.at[me_y, me_c], own_sem.at[4]),
    ]
    for copy in own:
        copy.start()
    tile = 3 * HEAD

    def flatten(i, _):
        at = pl.ds(pl.multiple_of(me_c * slab + i * 16, 16), 16)
        for h in range(groups):
            w_in_all[at, h * tile : (h + 1) * tile] = w_raw[
                pl.ds(pl.multiple_of(i * 16, 16), 16), h
            ]
        return 0

    pl.semaphore_wait(barrier, nc - 1 + ns - 1)

    def lat_at(z, y, p):
        return lat_all.at[pl.ds(pl.multiple_of((y * nz + z) * rows + p * size, size), size)]

    done = []

    def z_send(dirn, hop, p, src, z):
        to = me_z + 1 - 2 * dirn
        return link(
            src, lat_at(z, me_y, p), lat_s.at[dirn, hop, p], lat_r.at[dirn, hop, p],
            me_c, z_seq(to),
        )

    for p in range(PARTS):
        src = latent_ref.at[pl.ds(p * size, size)]
        for dirn, there in ((0, me_z < nz - 1), (1, me_z > 0)):
            @pl.when(there)
            def _():
                z_send(dirn, 0, p, src, me_z).start()
        done.append(
            remote(src, lat_at(me_z, me_y, p), laty_s.at[0, p], laty_r.at[0, p], me_c, near)
        )

    def slab_part(q):
        src = w_in_at(me_c, q)
        return [
            remote(src, w_in_at(me_c, q), wi_s.at[j, q], wi_r.at[j, q], c_peer(2 * j), me_s)
            for j in range(1, half)
        ]

    def flatten_part(q):
        lax.fori_loop(q * span // 16, (q + 1) * span // 16, flatten, 0)

    own[3].wait()
    flatten_part(0)
    w_in_far = [slab_part(0)]

    count = part.shape[0]
    lead = mod_w_ref.shape[0]
    held_rows = max(16, nc)
    index = me_c * lead + lax.broadcasted_iota(jnp.int32, (held_rows, lead), 1)
    steps = width // 2
    is_cos = index < steps
    order = jnp.where(is_cos, index, index - steps).astype(f32)
    row = lax.broadcasted_iota(jnp.int32, (held_rows, 1), 0)
    times = jnp.zeros((held_rows, 1), f32)
    for c in range(nc):
        times = jnp.where(row == c, time_ref[c].astype(f32), times)
    turns = times * jnp.exp(order * (-math.log(10000.0)) / steps)
    wave = jnp.where(is_cos, jnp.cos(turns), jnp.sin(turns))
    act = (wave / (1.0 + jnp.exp(-wave))).astype(bf16)
    own[0].wait()
    product = jnp.dot(act, mod_w[...], preferred_element_type=f32)
    for c in range(count):
        part[c] = product[c : c + 1]
    m1 = []
    for k in range(1, nc):
        peer = c_peer(k)
        m1.append(remote(part.at[peer], part_in.at[me_c], m1_s.at[k], m1_r.at[k], peer, me_s))
    for q in range(1, SLABS):
        flatten_part(q)
        w_in_far.append(slab_part(q))
    w_in_mate = remote(
        w_in_all.at[rows_of(me_c, slab)], w_in_all.at[rows_of(me_c, slab)], wif_s.at[0, 0],
        wif_r.at[0, 0], mate, me_s
    )

    def w_out_at(y, c):
        return w_out_all.at[y, c]

    w_out_far = [
        remote(w_out_ref, w_out_at(me_y, me_c), wo_s.at[0, j], wo_r.at[0, j], c_peer(2 * j), me_s)
        for j in range(1, half)
    ]
    w_out_mate = remote(
        w_out_ref, w_out_at(me_y, me_c), wo_s.at[0, 0], wo_r.at[0, 0], mate, me_s
    )

    pos8[...] = jnp.zeros_like(pos8)
    pos8[0 : pos_ref.shape[0]] = pos_ref[...].astype(f32)
    lane = lax.broadcasted_iota(jnp.int32, (8, HEAD), 1)
    axis = lax.broadcasted_iota(jnp.int32, (8, HEAD), 0)
    rate = jnp.zeros((8, HEAD), f32)
    sign = jnp.ones((8, HEAD), f32)
    for a, (start, extent) in enumerate(sections()):
        inside = (lane >= start) & (lane < start + extent)
        late = inside & (lane >= start + extent // 2)
        pair = jnp.where(late, lane - start - extent // 2, lane - start).astype(f32)
        value = jnp.exp(pair * (-math.log(256.0) * 2.0 / extent))
        rate = jnp.where(inside & (axis == a), value, rate)
        sign = jnp.where(inside & ~late, -1.0, sign)
    angle[...] = lax.dot_general(
        pos8[...], rate, (((0,), (0,)), ((), ())), preferred_element_type=f32,
        precision=lax.Precision.HIGHEST,
    )

    def turn_rows(s, _):
        turned = angle[rows_of(s, rows)]
        at = rows_of(place(s), rows)
        cos_ref[at] = jnp.cos(turned)
        sin_ref[at] = jnp.sin(turned) * sign[0:1]
        return 0

    lax.fori_loop(0, ns, turn_rows, 0)

    def exists(dirn, hop):
        return me_z >= hop if dirn == 0 else me_z <= nz - 1 - hop

    def beyond(dirn):
        return me_z < nz - 1 if dirn == 0 else me_z > 0

    def source(dirn, hop):
        return me_z - hop if dirn == 0 else me_z + hop

    def y_slot(dirn, hop):
        return hop if dirn == 0 else nz - 1 + hop

    def y_link(dirn, hop, p):
        held = lat_at(source(dirn, hop), me_y, p)
        slot = y_slot(dirn, hop)
        return link(held, held, laty_s.at[slot, p], laty_r.at[slot, p], me_c, near)

    def relay(hop):
        for p in range(PARTS):
            for dirn in range(2):
                @pl.when(exists(dirn, hop))
                def _():
                    z = source(dirn, hop)
                    held = lat_at(z, me_y, p)
                    z_send(dirn, hop - 1, p, held, z).wait_recv()
                    if hop < nz - 1:
                        @pl.when(beyond(dirn))
                        def _():
                            z_send(dirn, hop, p, held, z).start()
                    y_link(dirn, hop, p).start()

    relay(1)
    for copy in m1:
        copy.wait_recv()
    summed_mod = part[me_c]
    for k in range(1, nc):
        summed_mod = summed_mod + part_in[c_from(k)]
    mine[...] = summed_mod
    mod_all[me_s] = summed_mod
    m2 = [
        remote(
            mine, mod_all.at[me_s], m2_s.at[k], m2_r.at[k], me_c, lax.rem(me_s + k, ns)
        )
        for k in range(1, ns)
    ]
    for hop in range(2, nz - 1):
        relay(hop)

    def cot_at(z, p):
        return cot_all.at[pl.ds(pl.multiple_of(z * rows + p * size, size), size)]

    def cot_send(dirn, hop, p, src, z):
        return link(
            src, cot_at(z, p), cot_s.at[dirn, hop, p], cot_r.at[dirn, hop, p],
            me_c, z_seq(me_z + 1 - 2 * dirn),
        )

    for p in range(PARTS):
        for dirn in range(2):
            @pl.when(beyond(dirn))
            def _():
                cot_send(dirn, 0, p, cot_ref.at[pl.ds(p * size, size)], me_z).start()

    def cot_relay(hop):
        for p in range(PARTS):
            for dirn in range(2):
                @pl.when(exists(dirn, hop))
                def _():
                    z = source(dirn, hop)
                    cot_send(dirn, hop - 1, p, cot_at(z, p), z).wait_recv()
                    if hop < nz - 1:
                        @pl.when(beyond(dirn))
                        def _():
                            cot_send(dirn, hop, p, cot_at(z, p), z).start()

    def gate_rows(z):
        def body(index, _):
            at = pl.ds(pl.multiple_of(z * rows + index * 16, 16), 16)
            x_cot[at] = (cot_all[at].astype(f32) * vecs[2]).astype(bf16)
            return 0

        lax.fori_loop(0, rows // 16, body, 0)

    def gate_hop(hop):
        for dirn in range(2):
            @pl.when(exists(dirn, hop))
            def _():
                gate_rows(source(dirn, hop))

    for copy in m2:
        copy.wait_recv()
    for s in range(ns):
        at = s * cols
        while at < (s + 1) * cols:
            kind = at // width
            stop = min((s + 1) * cols, (kind + 1) * width)
            vecs[kind, :, at - kind * width : stop - kind * width] = mod_all[
                s, :, at - s * cols : stop - s * cols
            ]
            at = stop

    def norm_rows(at):
        normed, _inverse = layer_norm(lat_all[at].astype(f32))
        x_all[at] = (normed * (1.0 + vecs[1]) + vecs[0]).astype(bf16)

    def norm_run(start, count):
        def body(i, _):
            norm_rows(pl.ds(pl.multiple_of(start + i * 16, 16), 16))
            return 0

        lax.fori_loop(0, count // 16, body, 0)

    own[1].wait()
    norm_run(place(me_s) * rows, rows)
    for dirn in range(2):
        for hop in range(1, nz - 1):
            @pl.when(exists(dirn, hop))
            def _():
                norm_run((me_y * nz + source(dirn, hop)) * rows, rows)

    if nz > 1:
        relay(nz - 1)
        for dirn in range(2):
            @pl.when(exists(dirn, nz - 1))
            def _():
                norm_run((me_y * nz + source(dirn, nz - 1)) * rows, rows)

    w_out_near = remote(
        w_out_ref, w_out_at(me_y, me_c), wo_s.at[1, 0], wo_r.at[1, 0], me_c, near
    )

    w_in_second = []

    def slab_forward(q):
        for j in range(1, half):
            w_in_far[q][j - 1].wait_recv()
            held = w_in_at(c_from(2 * j), q)
            w_in_second.append(
                remote(held, held, wif_s.at[j, q], wif_r.at[j, q], mate, me_s)
            )

    for q in range(SLABS - 1):
        slab_forward(q)
    for copy in done:
        copy.wait_recv()
    norm_run(((1 - me_y) * nz + me_z) * rows, rows)
    for hop in range(1, nz):
        if hop == nz - 1 and nz > 2:
            cot_relay(1)
        for dirn in range(2):
            @pl.when(exists(dirn, hop))
            def _():
                for p in range(PARTS):
                    y_link(dirn, hop, p).wait_recv()
                norm_run(((1 - me_y) * nz + source(dirn, hop)) * rows, rows)
    slab_forward(SLABS - 1)
    w_in_mate.wait_recv()
    for copy in w_in_second:
        copy.wait_recv()

    def project(index, _):
        at = pl.ds(pl.multiple_of(index * tile, tile), tile)
        proj[index] = jnp.dot(x_all[...], w_in_all[:, at], preferred_element_type=f32)
        return 0

    lax.fori_loop(0, groups, project, 0)
    for hop in range(2, nz - 1):
        cot_relay(hop)

    def head_at(h):
        return pl.ds(pl.multiple_of(h * HEAD, HEAD), HEAD)

    def head_forward(h, _):
        query = proj[h, :, 0:HEAD]
        key = proj[h, :, HEAD : 2 * HEAD]
        query_n = query * inverse_rms(query)
        key_n = key * inverse_rms(key)
        q_rot = (query_n * cos_ref[...] + swap_pairs(query_n) * sin_ref[...]).astype(bf16)
        k_rot = (key_n * cos_ref[...] + swap_pairs(key_n) * sin_ref[...]).astype(bf16)
        values = proj[h, :, 2 * HEAD :].astype(bf16)
        q_all[h] = q_rot
        k_all[h] = k_rot
        v_all[h] = values
        weights = jnp.exp(dot_nt(q_rot, k_rot) * score_scale - HEAD**0.5)
        share = weights * (1.0 / jnp.sum(weights, -1, keepdims=True))
        probs[h] = share
        att[:, head_at(h)] = jnp.dot(
            share.astype(bf16), values, preferred_element_type=f32
        ).astype(bf16)
        return 0

    lax.fori_loop(0, groups, head_forward, 0)
    att_move = remote(
        att.at[rows_of(1 - me_y, run)], att_near, ex_s.at[0], ex_r.at[0], me_c, near
    )

    def att_rows(which):
        return att[rows_of(me_y, run)] if which == 0 else att_near[...]

    mixed = []

    def mix_chip(j):
        first = 2 * lax.rem(lax.div(me_c, 2) + j, half)
        for b in range(2):
            mix_out[first + b] = (
                jnp.dot(att_rows(0), w_out_all[me_y, first + b], preferred_element_type=f32)
                + jnp.dot(att_rows(1), w_out_all[1 - me_y, first + b], preferred_element_type=f32)
            ).astype(bf16)
        for k in range(1, nz):
            peer = lax.rem(me_z + k, nz)
            mixed.append(
                remote(
                    mix_out.at[pl.ds(first, 2), rows_of(peer, rows)],
                    mix_in.at[me_z, pl.ds(first, 2)],
                    mx_s.at[k, j], mx_r.at[k, j], me_c, z_seq(peer),
                )
            )

    w_out_near.wait_recv()
    held = w_out_at(1 - me_y, me_c)
    w_out_near_mate = remote(held, held, wo_s.at[2, 0], wo_r.at[2, 0], mate, me_s)
    w_out_second = []
    w_out_cross = []
    for j in range(1, half):
        w_out_far[j - 1].wait_recv()
        held = w_out_all.at[
            jnp.where(core == 0, me_y, 1 - me_y), jnp.where(core == 0, c_from(2 * j), me_c)
        ]
        w_out_cross.append(
            remote(
                held, held, wo_s.at[3, j], wo_r.at[3, j],
                jnp.where(core == 0, me_c, c_peer(2 * j)), jnp.where(core == 0, near, me_s),
            )
        )
        held = w_out_at(me_y, c_from(2 * j))
        w_out_second.append(
            remote(held, held, wo_s.at[2, j], wo_r.at[2, j], mate, me_s)
        )

    own[4].wait()
    w_out_mate.wait_recv()
    att_move.wait_recv()
    w_out_near_mate.wait_recv()
    mix_chip(0)

    own[2].wait()
    gate_rows(me_z)
    for hop in range(1, nz - 1):
        gate_hop(hop)
    cot_relay(nz - 1)
    gate_hop(nz - 1)

    for j in range(1, half):
        held = w_out_at(1 - me_y, c_from(2 * j))
        link(held, held, wo_s.at[3, j], wo_r.at[3, j], me_c, near).wait_recv()
        w_out_second.append(
            remote(held, held, wo_s.at[4, j], wo_r.at[4, j], mate, me_s)
        )
    for copy in w_out_second:
        copy.wait_recv()

    def d_attended(y):
        block = jnp.zeros((run, groups * HEAD), f32)
        for c in range(nc):
            block = block + dot_nt(x_cot[:, c * piece : (c + 1) * piece], w_out_all[y, c])
        return block.astype(bf16)

    d_away[...] = d_attended(1 - me_y)
    d_move = remote(
        d_away, d_att.at[rows_of(me_y, run)], ex_s.at[1], ex_r.at[1], me_c, near
    )
    d_att[rows_of(me_y, run)] = d_attended(me_y)
    for j in range(1, half):
        mix_chip(j)

    def back_norm(d_rot, raw, cos, sin):
        inverse = inverse_rms(raw)
        normed = raw * inverse
        d_normed = d_rot * cos - swap_pairs(d_rot) * sin
        return inverse * (d_normed - normed * jnp.mean(d_normed * normed, -1, keepdims=True))

    def query_part(h, y):
        at = rows_of(y, run)
        d_heads = d_att[at, head_at(h)]
        share = probs[h, at]
        d_values = dot_tn(share.astype(bf16), d_heads)
        d_probs = dot_nt(d_heads, v_all[h])
        d_scores = (share * (d_probs - jnp.sum(share * d_probs, -1, keepdims=True))).astype(bf16)
        d_qrot = jnp.dot(d_scores, k_all[h], preferred_element_type=f32) * score_scale
        d_krot = dot_tn(d_scores, q_all[h, at])
        d_query = back_norm(d_qrot, proj[h, at, 0:HEAD], cos_ref[at], sin_ref[at])
        d_proj[at, head_at(3 * h)] = d_query.astype(bf16)
        return d_values, d_krot

    def first_half(h, _):
        d_values, d_krot = query_part(h, me_y)
        value_sum[h] = d_values
        key_sum[h] = d_krot
        return 0

    lax.fori_loop(0, groups, first_half, 0)
    d_move.wait_recv()

    def second_half(h, _):
        d_values, d_krot = query_part(h, 1 - me_y)
        d_key = back_norm(
            (key_sum[h] + d_krot) * score_scale, proj[h, :, HEAD : 2 * HEAD],
            cos_ref[...], sin_ref[...],
        )
        d_proj[:, head_at(3 * h + 1)] = d_key.astype(bf16)
        d_proj[:, head_at(3 * h + 2)] = (value_sum[h] + d_values).astype(bf16)
        return 0

    lax.fori_loop(0, groups, second_half, 0)

    order = []
    low, high = 0, nz - 1
    for i in range(nz):
        take = (me_z - low >= high - me_z).astype(jnp.int32)
        order.append(take * low + (1 - take) * high)
        low, high = low + take, high - (1 - take)

    d_near = [[None] * CHUNKS for _ in range(nz)]

    def away(i, j):
        at = (rows_of(order[i], rows), pl.ds(j * chunk, chunk))
        d_near[i][j] = remote(
            dm_away.at[at], dm_near.at[at], dmn_s.at[i, j], dmn_r.at[i, j], me_c, near
        )

    for j in range(CHUNKS):
        part_cols = slice(j * chunk, (j + 1) * chunk)
        dm_away[:, part_cols] = dot_nt(
            d_proj[rows_of(1 - me_y, run)], w_in_all[part_cols]
        ).astype(bf16)
        away(0, j)
    for i in range(1, nz):
        for j in range(CHUNKS):
            away(i, j)
    for j in range(CHUNKS):
        part_cols = slice(j * chunk, (j + 1) * chunk)
        dm_here[:, part_cols] = dot_nt(
            d_proj[rows_of(me_y, run)], w_in_all[part_cols]
        ).astype(bf16)

    chain = []
    for i in range(nz - 1):
        to = order[i]
        up = to > me_z
        dirn = 1 - up.astype(jnp.int32)
        fed = (up & (me_z > 0)) | (~up & (me_z < nz - 1))
        beside = z_seq(me_z + 1 - 2 * dirn)
        for j in range(CHUNKS):
            at = (rows_of(to, rows), pl.ds(j * chunk, chunk))
            d_near[i][j].wait_recv()
            hop = link(
                dm_sum.at[at], chain_in.at[(dirn,) + at], ch_s.at[dirn, to, j],
                ch_r.at[dirn, to, j], me_c, beside,
            )
            value = dm_here[at].astype(f32) + dm_near[at].astype(f32)

            @pl.when(fed)
            def _():
                hop.wait_recv()
                dm_sum[at] = (value + chain_in[(dirn,) + at].astype(f32)).astype(bf16)

            @pl.when(~fed)
            def _():
                dm_sum[at] = value.astype(bf16)

            hop.start()
            chain.append(hop)

    for copy in mixed:
        copy.wait_recv()
    for start in range(0, rows, 16):
        mine_at = pl.ds(pl.multiple_of(me_z * rows + start, 16), 16)
        lat_rows = pl.ds(pl.multiple_of(place(me_s) * rows + start, 16), 16)
        for c in range(nc):
            value = mix_out[c, mine_at].astype(f32)
            for k in range(1, nz):
                value = value + mix_in[lax.rem(me_z + k, nz), c, start : start + 16].astype(f32)
            part_cols = slice(c * piece, (c + 1) * piece)
            block_ref[start : start + 16, part_cols] = (
                lat_all[lat_rows, part_cols].astype(f32) + vecs[2, :, part_cols] * value
            ).astype(bf16)

    for j in range(CHUNKS):
        part_cols = pl.ds(j * chunk, chunk)
        at = (rows_of(me_z, rows), part_cols)
        d_near[nz - 1][j].wait_recv()
        total[:, part_cols] = dm_here[at].astype(f32) + dm_near[at].astype(f32)
        for dirn, fed in ((0, me_z > 0), (1, me_z < nz - 1)):
            @pl.when(fed)
            def _():
                landed = chain_in.at[(dirn,) + at]
                link(
                    landed, landed, ch_s.at[dirn, me_z, j], ch_r.at[dirn, me_z, j], me_c, near
                ).wait_recv()
                total[:, part_cols] += landed[...].astype(f32)

    for start in range(0, rows, 16):
        lat_rows = pl.ds(pl.multiple_of(place(me_s) * rows + start, 16), 16)
        cot_rows = pl.ds(pl.multiple_of(me_z * rows + start, 16), 16)
        normed, inverse_std = layer_norm(lat_all[lat_rows].astype(f32))
        d_normed = total[start : start + 16] * (1.0 + vecs[1])
        grad_ref[start : start + 16] = cot_all[cot_rows].astype(f32) + inverse_std * (
            d_normed
            - jnp.mean(d_normed, -1, keepdims=True)
            - normed * jnp.mean(d_normed * normed, -1, keepdims=True)
        )

    for p in range(PARTS):
        for dirn in range(2):
            for hop in range(nz - 1):
                @pl.when(exists(dirn, hop) & beyond(dirn))
                def _():
                    held = lat_at(source(dirn, hop), me_y, p)
                    z_send(dirn, hop, p, held, source(dirn, hop)).wait_send()
                    held = cot_at(source(dirn, hop), p)
                    cot_send(dirn, hop, p, held, source(dirn, hop)).wait_send()
            for hop in range(1, nz):
                @pl.when(exists(dirn, hop))
                def _():
                    y_link(dirn, hop, p).wait_send()
    for copy in (
        done + m1 + m2 + sum(w_in_far, []) + [w_in_mate] + w_in_second + w_out_far
        + [w_out_mate, w_out_near, w_out_near_mate] + w_out_second + w_out_cross
        + [att_move, d_move] + mixed + sum(d_near, []) + chain
    ):
        copy.wait_send()


def hand_over(block_ref, grad_ref, block_out, grad_out):
    block_out[...] = block_ref[...]
    grad_out[...] = grad_ref[...]


def on_device(latent, timesteps, positions, mod_weight, input_weight, output_weight, cotangent):
    nc = lax.axis_size("cand")
    ns = lax.axis_size("seq")
    rows, width = latent.shape[1:]
    length = rows * ns
    slab = input_weight.shape[0]
    groups = input_weight.shape[1]
    cols = mod_weight.shape[1]
    piece = output_weight.shape[2]
    half = nc // 2
    nz = ns // 2
    run = nz * rows
    vmem = pl.BlockSpec(memory_space=pltpu.VMEM)
    smem = pl.BlockSpec(memory_space=pltpu.SMEM)
    anywhere = pl.BlockSpec(memory_space=pl.ANY)
    f32, bf16 = jnp.float32, jnp.bfloat16
    dma = pltpu.SemaphoreType.DMA
    block_out, latent_grad = pl.pallas_call(
        functools.partial(step_kernel, nc, ns),
        out_shape=(
            jax.ShapeDtypeStruct((rows, width), bf16),
            jax.ShapeDtypeStruct((rows, width), f32),
        ),
        in_specs=[smem, vmem] + [anywhere] * 5,
        out_specs=(vmem, vmem),
        scratch_shapes=[
            pltpu.VMEM(input_weight.shape, bf16),
            pltpu.VMEM(mod_weight.shape, bf16),
            pltpu.VMEM((8, length), f32),
            pltpu.VMEM((length, HEAD), f32),
            pltpu.VMEM((length, HEAD), f32),
            pltpu.VMEM((length, HEAD), f32),
            pltpu.VMEM((nc, 1, cols), f32),
            pltpu.VMEM((nc, 1, cols), f32),
            pltpu.VMEM((1, cols), f32),
            pltpu.VMEM((ns, 1, cols), f32),
            pltpu.VMEM((3, 1, width), f32),
            pltpu.VMEM((length, width), bf16),
            pltpu.VMEM((length, width), bf16),
            pltpu.VMEM((slab * nc, groups * 3 * HEAD), bf16),
            pltpu.VMEM((2, nc, groups * HEAD, piece), bf16),
            pltpu.VMEM((run, width), bf16),
            pltpu.VMEM((run, width), bf16),
            pltpu.VMEM((groups, length, 3 * HEAD), f32),
            pltpu.VMEM((groups, length, HEAD), bf16),
            pltpu.VMEM((groups, length, HEAD), bf16),
            pltpu.VMEM((groups, length, HEAD), bf16),
            pltpu.VMEM((groups, length, length), f32),
            pltpu.VMEM((length, groups * HEAD), bf16),
            pltpu.VMEM((run, groups * HEAD), bf16),
            pltpu.VMEM((length, groups * HEAD), bf16),
            pltpu.VMEM((run, groups * HEAD), bf16),
            pltpu.VMEM((length, groups * 3 * HEAD), bf16),
            pltpu.VMEM((groups, length, HEAD), f32),
            pltpu.VMEM((groups, length, HEAD), f32),
            pltpu.VMEM((nc, run, piece), bf16),
            pltpu.VMEM((nz, nc, rows, piece), bf16),
            pltpu.VMEM((run, width), bf16),
            pltpu.VMEM((run, width), bf16),
            pltpu.VMEM((run, width), bf16),
            pltpu.VMEM((run, width), bf16),
            pltpu.VMEM((2, run, width), bf16),
            pltpu.VMEM((rows, width), f32),
            dma((5,)),
            dma((2, nz, PARTS)), dma((2, nz, PARTS)),
            dma((2 * nz, PARTS)), dma((2 * nz, PARTS)),
            dma((half, SLABS)), dma((half, SLABS)), dma((half, SLABS)), dma((half, SLABS)),
            dma((5, half)), dma((5, half)), dma((nc,)), dma((nc,)), dma((ns,)), dma((ns,)),
            dma((2, nz, PARTS)), dma((2, nz, PARTS)), dma((2,)), dma((2,)), dma((nz, half)), dma((nz, half)),
            dma((nz, CHUNKS)), dma((nz, CHUNKS)), dma((2, nz, CHUNKS)), dma((2, nz, CHUNKS)),
        ],
        compiler_params=pltpu.CompilerParams(
            collective_id=0, has_side_effects=True, vmem_limit_bytes=66000000
        ),
    )(
        timesteps, positions, mod_weight, latent[0], cotangent[0],
        input_weight,
        output_weight.reshape(groups * HEAD, piece),
    )
    block_out, latent_grad = pl.pallas_call(
        hand_over,
        out_shape=(
            jax.ShapeDtypeStruct((rows, width), bf16),
            jax.ShapeDtypeStruct((rows, width), f32),
        ),
        in_specs=[vmem] * 2,
        out_specs=(vmem, vmem),
    )(block_out, latent_grad)
    return (block_out[None], latent_grad[None])


def solution(mesh):
    placed = (
        P("cand", "seq", None),
        P(),
        P(),
        P("cand", "seq"),
        P("cand", "seq", None),
        P("seq", None, "cand"),
        P("cand", "seq", None),
    )
    return jax.shard_map(
        on_device,
        mesh=mesh,
        in_specs=placed,
        out_specs=(P("cand", "seq", None), P("cand", "seq", None)),
        check_vma=False,
    )
```

```python
import functools
import math

import jax
import jax.numpy as jnp
from jax import lax
from jax.experimental import pallas as pl
from jax.experimental.pallas import tpu as pltpu
from jax.sharding import PartitionSpec as P

HEAD = 128
CHUNKS = 4
PARTS = 3
SLABS = 6
HALVES = 2
MESH = pl.DeviceIdType.MESH


epsilon = 1e-06


def swap_pairs(values):
    lane = lax.broadcasted_iota(jnp.int32, values.shape, 1)
    small = HEAD // 8
    large = (HEAD - small) // 2
    near = jnp.where(
        lane < small // 2,
        pltpu.roll(values, HEAD - small // 2, 1),
        pltpu.roll(values, small // 2, 1),
    )
    upper = ((lane >= small) & (lane < small + large // 2)) | (
        (lane >= small + large) & (lane < small + large + large // 2)
    )
    far = jnp.where(
        upper, pltpu.roll(values, HEAD - large // 2, 1), pltpu.roll(values, large // 2, 1)
    )
    return jnp.where(lane < small, near, far)


def dot_nt(left, right):
    return lax.dot_general(left, right, (((1,), (1,)), ((), ())), preferred_element_type=jnp.float32)


def dot_tn(left, right):
    return lax.dot_general(left, right, (((0,), (0,)), ((), ())), preferred_element_type=jnp.float32)


def inverse_rms(values):
    return lax.rsqrt(jnp.mean(values * values, -1, keepdims=True) + epsilon)


def layer_norm(values):
    centred = values - jnp.mean(values, -1, keepdims=True)
    inverse_std = lax.rsqrt(jnp.mean(centred * centred, -1, keepdims=True) + epsilon)
    return (centred * inverse_std, inverse_std)


def sections():
    first = HEAD // 8
    other = (HEAD - first) // 2
    return ((0, first), (first, other), (first + other, other))


def step_kernel(
    nc, ns,
    time_ref, pos_ref, mod_w_ref, latent_ref, cot_ref, w_in_ref, w_out_ref,
    block_ref, grad_ref,
    w_raw, mod_w, pos8, angle, cos_ref, sin_ref, part, part_in, mine, mod_all, vecs,
    lat_all, x_all, w_in_all, w_out_all, cot_all, x_cot, proj, inverse_all, q_all, k_all, v_all, probs,
    att, att_near, d_att, d_away, d_proj, key_sum, value_sum, mix_out, mix_in,
    dm_away, dm_here, dm_near, dm_sum, chain_in, total,
    own_sem, lat_s, lat_r, laty_s, laty_r, wi_s, wi_r, wif_s, wif_r, wo_s, wo_r, m1_s, m1_r,
    m2_s, m2_r, cot_s, cot_r, ex_s, ex_r, mx_s, mx_r, dmn_s, dmn_r, ch_s, ch_r,
):
    me_c = lax.axis_index("cand")
    me_s = lax.axis_index("seq")
    rows, width = latent_ref.shape
    length = rows * ns
    slab = w_in_ref.shape[0]
    groups = q_all.shape[0]
    cols = mod_w_ref.shape[1]
    piece = w_out_ref.shape[1]
    chunk = width // CHUNKS
    half = nc // 2
    core = lax.rem(me_c, 2)
    mate = me_c + 1 - 2 * core
    nz = ns // 2
    me_y, me_z = lax.rem(me_s, 2), lax.div(me_s, 2)
    near = me_s + 1 - 2 * me_y
    score_scale = HEAD ** (-0.5)
    size = rows // PARTS
    span = slab // SLABS
    run = nz * rows
    f32, bf16 = jnp.float32, jnp.bfloat16

    def place(index):
        return lax.rem(index, 2) * nz + lax.div(index, 2)

    def rows_of(index, count):
        return pl.ds(pl.multiple_of(index * count, count), count)

    def link(src, dst, send, recv, cand, seq):
        return pltpu.make_async_remote_copy(
            src_ref=src, dst_ref=dst, send_sem=send, recv_sem=recv,
            device_id=(cand, seq), device_id_type=MESH,
        )

    def remote(*args):
        copy = link(*args)
        copy.start()
        return copy

    def c_peer(k):
        return lax.rem(me_c + k, nc)

    def c_from(k):
        return lax.rem(me_c - k + nc, nc)

    def z_seq(z):
        return 2 * z + me_y

    barrier = pltpu.get_barrier_semaphore()
    for k in range(1, nc):
        pl.semaphore_signal(barrier, inc=1, device_id=(c_peer(k), me_s), device_id_type=MESH)
    for k in range(1, ns):
        pl.semaphore_signal(
            barrier, inc=1, device_id=(me_c, lax.rem(me_s + k, ns)), device_id_type=MESH
        )

    def w_in_at(index, q):
        return w_in_all.at[pl.ds(pl.multiple_of(index * slab + q * span, span), span)]

    own = [
        pltpu.make_async_copy(mod_w_ref, mod_w, own_sem.at[0]),
        pltpu.make_async_copy(latent_ref, lat_all.at[rows_of(place(me_s), rows)], own_sem.at[1]),
        pltpu.make_async_copy(cot_ref, cot_all.at[rows_of(me_z, rows)], own_sem.at[2]),
        pltpu.make_async_copy(w_in_ref, w_raw, own_sem.at[3]),
        pltpu.make_async_copy(w_out_ref, w_out_all.at[me_y, me_c], own_sem.at[4]),
    ]
    for copy in own:
        copy.start()
    tile = 3 * HEAD

    def flatten(i, _):
        at = pl.ds(pl.multiple_of(me_c * slab + i * 16, 16), 16)
        for h in range(groups):
            w_in_all[at, h * tile : (h + 1) * tile] = w_raw[
                pl.ds(pl.multiple_of(i * 16, 16), 16), h
            ]
        return 0

    pl.semaphore_wait(barrier, nc - 1 + ns - 1)

    def lat_at(z, y, p):
        return lat_all.at[pl.ds(pl.multiple_of((y * nz + z) * rows + p * size, size), size)]

    done = []

    def z_send(dirn, hop, p, src, z):
        to = me_z + 1 - 2 * dirn
        return link(
            src, lat_at(z, me_y, p), lat_s.at[dirn, hop, p], lat_r.at[dirn, hop, p],
            me_c, z_seq(to),
        )

    for p in range(PARTS):
        src = latent_ref.at[pl.ds(p * size, size)]
        for dirn, there in ((0, me_z < nz - 1), (1, me_z > 0)):
            @pl.when(there)
            def _():
                z_send(dirn, 0, p, src, me_z).start()
        done.append(
            remote(src, lat_at(me_z, me_y, p), laty_s.at[0, p], laty_r.at[0, p], me_c, near)
        )

    def slab_part(q):
        src = w_in_at(me_c, q)
        return [
            remote(src, w_in_at(me_c, q), wi_s.at[j, q], wi_r.at[j, q], c_peer(2 * j), me_s)
            for j in range(1, half)
        ]

    def flatten_part(q):
        lax.fori_loop(q * span // 16, (q + 1) * span // 16, flatten, 0)

    own[3].wait()
    flatten_part(0)
    w_in_far = [slab_part(0)]

    count = part.shape[0]
    lead = mod_w_ref.shape[0]
    held_rows = max(16, nc)
    index = me_c * lead + lax.broadcasted_iota(jnp.int32, (held_rows, lead), 1)
    steps = width // 2
    is_cos = index < steps
    order = jnp.where(is_cos, index, index - steps).astype(f32)
    row = lax.broadcasted_iota(jnp.int32, (held_rows, 1), 0)
    times = jnp.zeros((held_rows, 1), f32)
    for c in range(nc):
        times = jnp.where(row == c, time_ref[c].astype(f32), times)
    turns = times * jnp.exp(order * (-math.log(10000.0)) / steps)
    wave = jnp.where(is_cos, jnp.cos(turns), jnp.sin(turns))
    act = (wave / (1.0 + jnp.exp(-wave))).astype(bf16)
    own[0].wait()
    product = jnp.dot(act, mod_w[...], preferred_element_type=f32)
    for c in range(count):
        part[c] = product[c : c + 1]
    m1 = []
    for k in range(1, nc):
        peer = c_peer(k)
        m1.append(remote(part.at[peer], part_in.at[me_c], m1_s.at[k], m1_r.at[k], peer, me_s))
    for q in range(1, SLABS):
        flatten_part(q)
        w_in_far.append(slab_part(q))
    w_in_mate = remote(
        w_in_all.at[rows_of(me_c, slab)], w_in_all.at[rows_of(me_c, slab)], wif_s.at[0, 0],
        wif_r.at[0, 0], mate, me_s
    )

    part_rows = w_out_ref.shape[0] // HALVES

    def w_out_at(y, c, q):
        return w_out_all.at[y, c, pl.ds(q * part_rows, part_rows)]

    def w_out_send(kind, j, q, src, y, c, cand, seq):
        return remote(
            src, w_out_at(y, c, q), wo_s.at[kind, j, q], wo_r.at[kind, j, q], cand, seq
        )

    def w_out_own(q):
        return w_out_ref.at[pl.ds(q * part_rows, part_rows)]

    w_out_far = [
        [
            w_out_send(0, j, q, w_out_own(q), me_y, me_c, c_peer(2 * j), me_s)
            for j in range(1, half)
        ]
        for q in range(HALVES)
    ]
    w_out_mate = [
        w_out_send(0, 0, q, w_out_own(q), me_y, me_c, mate, me_s) for q in range(HALVES)
    ]

    pos8[...] = jnp.zeros_like(pos8)
    pos8[0 : pos_ref.shape[0]] = pos_ref[...].astype(f32)
    lane = lax.broadcasted_iota(jnp.int32, (8, HEAD), 1)
    axis = lax.broadcasted_iota(jnp.int32, (8, HEAD), 0)
    rate = jnp.zeros((8, HEAD), f32)
    sign = jnp.ones((8, HEAD), f32)
    for a, (start, extent) in enumerate(sections()):
        inside = (lane >= start) & (lane < start + extent)
        late = inside & (lane >= start + extent // 2)
        pair = jnp.where(late, lane - start - extent // 2, lane - start).astype(f32)
        value = jnp.exp(pair * (-math.log(256.0) * 2.0 / extent))
        rate = jnp.where(inside & (axis == a), value, rate)
        sign = jnp.where(inside & ~late, -1.0, sign)
    angle[...] = lax.dot_general(
        pos8[...], rate, (((0,), (0,)), ((), ())), preferred_element_type=f32,
        precision=lax.Precision.HIGHEST,
    )

    def turn_rows(s, _):
        turned = angle[rows_of(s, rows)]
        at = rows_of(place(s), rows)
        cos_ref[at] = jnp.cos(turned)
        sin_ref[at] = jnp.sin(turned) * sign[0:1]
        return 0

    lax.fori_loop(0, ns, turn_rows, 0)

    def exists(dirn, hop):
        return me_z >= hop if dirn == 0 else me_z <= nz - 1 - hop

    def beyond(dirn):
        return me_z < nz - 1 if dirn == 0 else me_z > 0

    def source(dirn, hop):
        return me_z - hop if dirn == 0 else me_z + hop

    def y_slot(dirn, hop):
        return hop if dirn == 0 else nz - 1 + hop

    def y_link(dirn, hop, p):
        held = lat_at(source(dirn, hop), me_y, p)
        slot = y_slot(dirn, hop)
        return link(held, held, laty_s.at[slot, p], laty_r.at[slot, p], me_c, near)

    def relay(hop):
        for p in range(PARTS):
            for dirn in range(2):
                @pl.when(exists(dirn, hop))
                def _():
                    z = source(dirn, hop)
                    held = lat_at(z, me_y, p)
                    z_send(dirn, hop - 1, p, held, z).wait_recv()
                    if hop < nz - 1:
                        @pl.when(beyond(dirn))
                        def _():
                            z_send(dirn, hop, p, held, z).start()
                    y_link(dirn, hop, p).start()

    relay(1)
    for copy in m1:
        copy.wait_recv()
    summed_mod = part[me_c]
    for k in range(1, nc):
        summed_mod = summed_mod + part_in[c_from(k)]
    mine[...] = summed_mod
    mod_all[me_s] = summed_mod
    m2 = [
        remote(
            mine, mod_all.at[me_s], m2_s.at[k], m2_r.at[k], me_c, lax.rem(me_s + k, ns)
        )
        for k in range(1, ns)
    ]
    for hop in range(2, nz - 1):
        relay(hop)

    def cot_at(z, p):
        return cot_all.at[pl.ds(pl.multiple_of(z * rows + p * size, size), size)]

    def cot_send(dirn, hop, p, src, z):
        return link(
            src, cot_at(z, p), cot_s.at[dirn, hop, p], cot_r.at[dirn, hop, p],
            me_c, z_seq(me_z + 1 - 2 * dirn),
        )

    for p in range(PARTS):
        for dirn in range(2):
            @pl.when(beyond(dirn))
            def _():
                cot_send(dirn, 0, p, cot_ref.at[pl.ds(p * size, size)], me_z).start()

    def cot_relay(hop):
        for p in range(PARTS):
            for dirn in range(2):
                @pl.when(exists(dirn, hop))
                def _():
                    z = source(dirn, hop)
                    cot_send(dirn, hop - 1, p, cot_at(z, p), z).wait_recv()
                    if hop < nz - 1:
                        @pl.when(beyond(dirn))
                        def _():
                            cot_send(dirn, hop, p, cot_at(z, p), z).start()

    def gate_rows(z):
        def body(index, _):
            at = pl.ds(pl.multiple_of(z * rows + index * 16, 16), 16)
            gated = (cot_all[at].astype(f32) * vecs[2]).astype(bf16)
            for c in range(nc):
                x_cot[c, at] = gated[:, c * piece : (c + 1) * piece]
            return 0

        lax.fori_loop(0, rows // 16, body, 0)

    def gate_hop(hop):
        for dirn in range(2):
            @pl.when(exists(dirn, hop))
            def _():
                gate_rows(source(dirn, hop))

    for copy in m2:
        copy.wait_recv()
    for s in range(ns):
        at = s * cols
        while at < (s + 1) * cols:
            kind = at // width
            stop = min((s + 1) * cols, (kind + 1) * width)
            vecs[kind, :, at - kind * width : stop - kind * width] = mod_all[
                s, :, at - s * cols : stop - s * cols
            ]
            at = stop

    def norm_rows(at):
        normed, _inverse = layer_norm(lat_all[at].astype(f32))
        x_all[at] = (normed * (1.0 + vecs[1]) + vecs[0]).astype(bf16)

    def norm_run(start, count):
        def body(i, _):
            norm_rows(pl.ds(pl.multiple_of(start + i * 16, 16), 16))
            return 0

        lax.fori_loop(0, count // 16, body, 0)

    own[1].wait()
    norm_run(place(me_s) * rows, rows)
    for dirn in range(2):
        for hop in range(1, nz - 1):
            @pl.when(exists(dirn, hop))
            def _():
                norm_run((me_y * nz + source(dirn, hop)) * rows, rows)

    if nz > 1:
        relay(nz - 1)
        for dirn in range(2):
            @pl.when(exists(dirn, nz - 1))
            def _():
                norm_run((me_y * nz + source(dirn, nz - 1)) * rows, rows)

    w_out_near = [
        w_out_send(1, 0, q, w_out_own(q), me_y, me_c, me_c, near) for q in range(HALVES)
    ]

    w_in_second = []

    def slab_forward(q):
        for j in range(1, half):
            w_in_far[q][j - 1].wait_recv()
            held = w_in_at(c_from(2 * j), q)
            w_in_second.append(
                remote(held, held, wif_s.at[j, q], wif_r.at[j, q], mate, me_s)
            )

    for q in range(SLABS - 1):
        slab_forward(q)
    for copy in done:
        copy.wait_recv()
    norm_run(((1 - me_y) * nz + me_z) * rows, rows)
    for hop in range(1, nz):
        if hop == nz - 1:
            if nz > 2:
                cot_relay(1)
            slab_forward(SLABS - 1)
        for dirn in range(2):
            @pl.when(exists(dirn, hop))
            def _():
                for p in range(PARTS):
                    y_link(dirn, hop, p).wait_recv()
                norm_run(((1 - me_y) * nz + source(dirn, hop)) * rows, rows)
    w_in_mate.wait_recv()
    for copy in w_in_second:
        copy.wait_recv()

    def project(index, _):
        at = pl.ds(pl.multiple_of(index * tile, tile), tile)
        proj[index] = jnp.dot(x_all[...], w_in_all[:, at], preferred_element_type=f32)
        return 0

    lax.fori_loop(0, groups, project, 0)
    for hop in range(2, nz - 1):
        cot_relay(hop)

    def head_at(h):
        return pl.ds(h * HEAD, HEAD)

    def head_forward(h, _):
        query = proj[h, :, 0:HEAD]
        key = proj[h, :, HEAD : 2 * HEAD]
        query_inverse = inverse_rms(query)
        key_inverse = inverse_rms(key)
        query_n = query * query_inverse
        key_n = key * key_inverse
        proj[h, :, 0:HEAD] = query_n
        proj[h, :, HEAD : 2 * HEAD] = key_n
        inverse_all[2 * h] = jnp.broadcast_to(query_inverse, query.shape)
        inverse_all[2 * h + 1] = jnp.broadcast_to(key_inverse, key.shape)
        q_rot = (query_n * cos_ref[...] + swap_pairs(query_n) * sin_ref[...]).astype(bf16)
        k_rot = (key_n * cos_ref[...] + swap_pairs(key_n) * sin_ref[...]).astype(bf16)
        values = proj[h, :, 2 * HEAD :].astype(bf16)
        q_all[h] = q_rot
        k_all[h] = k_rot
        v_all[h] = values
        weights = jnp.exp(dot_nt(q_rot, k_rot) * score_scale - HEAD**0.5)
        share = weights * (1.0 / jnp.sum(weights, -1, keepdims=True))
        probs[h] = share
        att[:, head_at(h)] = jnp.dot(
            share.astype(bf16), values, preferred_element_type=f32
        ).astype(bf16)
        return 0

    for h in range(groups):
        head_forward(h, 0)
    att_move = remote(
        att.at[rows_of(1 - me_y, run)], att_near, ex_s.at[0], ex_r.at[0], me_c, near
    )

    def att_rows(which):
        return att[rows_of(me_y, run)] if which == 0 else att_near[...]

    mixed = []

    def mix_chip(j):
        first = 2 * lax.rem(lax.div(me_c, 2) + j, half)
        for b in range(2):
            mix_out[first + b] = (
                jnp.dot(att_rows(0), w_out_all[me_y, first + b], preferred_element_type=f32)
                + jnp.dot(att_rows(1), w_out_all[1 - me_y, first + b], preferred_element_type=f32)
            ).astype(bf16)
        for k in range(1, nz):
            peer = lax.rem(me_z + k, nz)
            mixed.append(
                remote(
                    mix_out.at[pl.ds(first, 2), rows_of(peer, rows)],
                    mix_in.at[me_z, pl.ds(first, 2)],
                    mx_s.at[k, j], mx_r.at[k, j], me_c, z_seq(peer),
                )
            )

    w_out_second = []
    w_out_cross = []
    w_out_near_mate = []
    for q in range(HALVES):
        w_out_near[q].wait_recv()
        w_out_near_mate.append(
            w_out_send(2, 0, q, w_out_at(1 - me_y, me_c, q), 1 - me_y, me_c, mate, me_s)
        )
        for j in range(1, half):
            w_out_far[q][j - 1].wait_recv()
            from_y = jnp.where(core == 0, me_y, 1 - me_y)
            from_c = jnp.where(core == 0, c_from(2 * j), me_c)
            w_out_cross.append(
                w_out_send(
                    3, j, q, w_out_at(from_y, from_c, q), from_y, from_c,
                    jnp.where(core == 0, me_c, c_peer(2 * j)), jnp.where(core == 0, near, me_s),
                )
            )
            w_out_second.append(
                w_out_send(
                    2, j, q, w_out_at(me_y, c_from(2 * j), q), me_y, c_from(2 * j), mate, me_s
                )
            )

    own[4].wait()
    for copy in w_out_mate + [att_move] + w_out_near_mate:
        copy.wait_recv()
    mix_chip(0)

    own[2].wait()
    gate_rows(me_z)
    for hop in range(1, nz - 1):
        gate_hop(hop)
    cot_relay(nz - 1)
    gate_hop(nz - 1)

    def d_attended(y, first, count):
        block = jnp.zeros((run, groups * HEAD), f32)
        for i in range(count):
            c = first + i
            block = block + dot_nt(x_cot[c], w_out_all[y, c])
        return block

    chip = 2 * lax.div(me_c, 2)
    away_sum = d_attended(1 - me_y, chip, 2)
    for q in range(HALVES):
        for j in range(1, half):
            held = w_out_at(1 - me_y, c_from(2 * j), q)
            link(held, held, wo_s.at[3, j, q], wo_r.at[3, j, q], me_c, near).wait_recv()
            w_out_second.append(
                w_out_send(4, j, q, held, 1 - me_y, c_from(2 * j), mate, me_s)
            )
    for copy in w_out_second:
        copy.wait_recv()
    for j in range(1, half):
        away_sum = away_sum + d_attended(1 - me_y, 2 * lax.rem(lax.div(me_c, 2) + j, half), 2)
    d_away[...] = away_sum.astype(bf16)
    d_move = remote(
        d_away, d_att.at[rows_of(me_y, run)], ex_s.at[1], ex_r.at[1], me_c, near
    )
    d_att[rows_of(me_y, run)] = d_attended(me_y, 0, nc).astype(bf16)
    for j in range(1, half):
        mix_chip(j)

    def back_norm(d_rot, normed, inverse, cos, sin):
        d_normed = d_rot * cos - swap_pairs(d_rot) * sin
        return inverse * (d_normed - normed * jnp.mean(d_normed * normed, -1, keepdims=True))

    def query_part(h, y):
        at = rows_of(y, run)
        d_heads = d_att[at, head_at(h)]
        share = probs[h, at]
        d_values = dot_tn(share.astype(bf16), d_heads)
        d_probs = dot_nt(d_heads, v_all[h])
        d_scores = (share * (d_probs - jnp.sum(share * d_probs, -1, keepdims=True))).astype(bf16)
        d_qrot = jnp.dot(d_scores, k_all[h], preferred_element_type=f32) * score_scale
        d_krot = dot_tn(d_scores, q_all[h, at])
        d_query = back_norm(
            d_qrot, proj[h, at, 0:HEAD], inverse_all[2 * h, at], cos_ref[at], sin_ref[at]
        )
        d_proj[at, head_at(3 * h)] = d_query.astype(bf16)
        return d_values, d_krot

    def first_half(h, _):
        d_values, d_krot = query_part(h, me_y)
        value_sum[h] = d_values
        key_sum[h] = d_krot
        return 0

    for h in range(groups):
        first_half(h, 0)
    d_move.wait_recv()

    def second_half(h, _):
        d_values, d_krot = query_part(h, 1 - me_y)
        d_key = back_norm(
            (key_sum[h] + d_krot) * score_scale, proj[h, :, HEAD : 2 * HEAD],
            inverse_all[2 * h + 1], cos_ref[...], sin_ref[...],
        )
        d_proj[:, head_at(3 * h + 1)] = d_key.astype(bf16)
        d_proj[:, head_at(3 * h + 2)] = (value_sum[h] + d_values).astype(bf16)
        return 0

    for h in range(groups):
        second_half(h, 0)

    order = []
    low, high = 0, nz - 1
    for i in range(nz):
        take = (me_z - low >= high - me_z).astype(jnp.int32)
        order.append(take * low + (1 - take) * high)
        low, high = low + take, high - (1 - take)

    d_near = [[None] * CHUNKS for _ in range(nz)]

    def away(i, j):
        at = (rows_of(order[i], rows), pl.ds(j * chunk, chunk))
        d_near[i][j] = remote(
            dm_away.at[at], dm_near.at[at], dmn_s.at[i, j], dmn_r.at[i, j], me_c, near
        )

    for j in range(CHUNKS):
        part_cols = slice(j * chunk, (j + 1) * chunk)
        dm_away[:, part_cols] = dot_nt(
            d_proj[rows_of(1 - me_y, run)], w_in_all[part_cols]
        ).astype(bf16)
        away(0, j)
    for i in range(1, nz):
        for j in range(CHUNKS):
            away(i, j)
    for j in range(CHUNKS):
        part_cols = slice(j * chunk, (j + 1) * chunk)
        dm_here[:, part_cols] = dot_nt(
            d_proj[rows_of(me_y, run)], w_in_all[part_cols]
        ).astype(bf16)

    chain = []
    for i in range(nz - 1):
        to = order[i]
        up = to > me_z
        dirn = 1 - up.astype(jnp.int32)
        fed = (up & (me_z > 0)) | (~up & (me_z < nz - 1))
        beside = z_seq(me_z + 1 - 2 * dirn)
        for j in range(CHUNKS):
            at = (rows_of(to, rows), pl.ds(j * chunk, chunk))
            d_near[i][j].wait_recv()
            hop = link(
                dm_sum.at[at], chain_in.at[(dirn,) + at], ch_s.at[dirn, to, j],
                ch_r.at[dirn, to, j], me_c, beside,
            )
            value = dm_here[at].astype(f32) + dm_near[at].astype(f32)

            @pl.when(fed)
            def _():
                hop.wait_recv()
                dm_sum[at] = (value + chain_in[(dirn,) + at].astype(f32)).astype(bf16)

            @pl.when(~fed)
            def _():
                dm_sum[at] = value.astype(bf16)

            hop.start()
            chain.append(hop)

    for copy in mixed:
        copy.wait_recv()
    for start in range(0, rows, 16):
        mine_at = pl.ds(pl.multiple_of(me_z * rows + start, 16), 16)
        lat_rows = pl.ds(pl.multiple_of(place(me_s) * rows + start, 16), 16)
        for c in range(nc):
            value = mix_out[c, mine_at].astype(f32)
            for k in range(1, nz):
                value = value + mix_in[lax.rem(me_z + k, nz), c, start : start + 16].astype(f32)
            part_cols = slice(c * piece, (c + 1) * piece)
            block_ref[start : start + 16, part_cols] = (
                lat_all[lat_rows, part_cols].astype(f32) + vecs[2, :, part_cols] * value
            ).astype(bf16)

    for j in range(CHUNKS):
        part_cols = pl.ds(j * chunk, chunk)
        at = (rows_of(me_z, rows), part_cols)
        d_near[nz - 1][j].wait_recv()
        total[:, part_cols] = dm_here[at].astype(f32) + dm_near[at].astype(f32)
        for dirn, fed in ((0, me_z > 0), (1, me_z < nz - 1)):
            @pl.when(fed)
            def _():
                landed = chain_in.at[(dirn,) + at]
                link(
                    landed, landed, ch_s.at[dirn, me_z, j], ch_r.at[dirn, me_z, j], me_c, near
                ).wait_recv()
                total[:, part_cols] += landed[...].astype(f32)

    for start in range(0, rows, 16):
        lat_rows = pl.ds(pl.multiple_of(place(me_s) * rows + start, 16), 16)
        cot_rows = pl.ds(pl.multiple_of(me_z * rows + start, 16), 16)
        normed, inverse_std = layer_norm(lat_all[lat_rows].astype(f32))
        d_normed = total[start : start + 16] * (1.0 + vecs[1])
        grad_ref[start : start + 16] = cot_all[cot_rows].astype(f32) + inverse_std * (
            d_normed
            - jnp.mean(d_normed, -1, keepdims=True)
            - normed * jnp.mean(d_normed * normed, -1, keepdims=True)
        )

    for p in range(PARTS):
        for dirn in range(2):
            for hop in range(nz - 1):
                @pl.when(exists(dirn, hop) & beyond(dirn))
                def _():
                    held = lat_at(source(dirn, hop), me_y, p)
                    z_send(dirn, hop, p, held, source(dirn, hop)).wait_send()
                    held = cot_at(source(dirn, hop), p)
                    cot_send(dirn, hop, p, held, source(dirn, hop)).wait_send()
            for hop in range(1, nz):
                @pl.when(exists(dirn, hop))
                def _():
                    y_link(dirn, hop, p).wait_send()
    for copy in (
        done + m1 + m2 + sum(w_in_far, []) + [w_in_mate] + w_in_second + sum(w_out_far, [])
        + w_out_mate + w_out_near + w_out_near_mate + w_out_second + w_out_cross
        + [att_move, d_move] + mixed + sum(d_near, []) + chain
    ):
        copy.wait_send()


def hand_over(block_ref, grad_ref, block_out, grad_out):
    block_out[...] = block_ref[...]
    grad_out[...] = grad_ref[...]


def on_device(latent, timesteps, positions, mod_weight, input_weight, output_weight, cotangent):
    nc = lax.axis_size("cand")
    ns = lax.axis_size("seq")
    rows, width = latent.shape[1:]
    length = rows * ns
    slab = input_weight.shape[0]
    groups = input_weight.shape[1]
    cols = mod_weight.shape[1]
    piece = output_weight.shape[2]
    half = nc // 2
    nz = ns // 2
    run = nz * rows
    vmem = pl.BlockSpec(memory_space=pltpu.VMEM)
    smem = pl.BlockSpec(memory_space=pltpu.SMEM)
    anywhere = pl.BlockSpec(memory_space=pl.ANY)
    f32, bf16 = jnp.float32, jnp.bfloat16
    dma = pltpu.SemaphoreType.DMA
    block_out, latent_grad = pl.pallas_call(
        functools.partial(step_kernel, nc, ns),
        out_shape=(
            jax.ShapeDtypeStruct((rows, width), bf16),
            jax.ShapeDtypeStruct((rows, width), f32),
        ),
        in_specs=[smem, vmem] + [anywhere] * 5,
        out_specs=(vmem, vmem),
        scratch_shapes=[
            pltpu.VMEM(input_weight.shape, bf16),
            pltpu.VMEM(mod_weight.shape, bf16),
            pltpu.VMEM((8, length), f32),
            pltpu.VMEM((length, HEAD), f32),
            pltpu.VMEM((length, HEAD), f32),
            pltpu.VMEM((length, HEAD), f32),
            pltpu.VMEM((nc, 1, cols), f32),
            pltpu.VMEM((nc, 1, cols), f32),
            pltpu.VMEM((1, cols), f32),
            pltpu.VMEM((ns, 1, cols), f32),
            pltpu.VMEM((3, 1, width), f32),
            pltpu.VMEM((length, width), bf16),
            pltpu.VMEM((length, width), bf16),
            pltpu.VMEM((slab * nc, groups * 3 * HEAD), bf16),
            pltpu.VMEM((2, nc, groups * HEAD, piece), bf16),
            pltpu.VMEM((run, width), bf16),
            pltpu.VMEM((nc, run, piece), bf16),
            pltpu.VMEM((groups, length, 3 * HEAD), f32),
            pltpu.VMEM((2 * groups, length, HEAD), f32),
            pltpu.VMEM((groups, length, HEAD), bf16),
            pltpu.VMEM((groups, length, HEAD), bf16),
            pltpu.VMEM((groups, length, HEAD), bf16),
            pltpu.VMEM((groups, length, length), f32),
            pltpu.VMEM((length, groups * HEAD), bf16),
            pltpu.VMEM((run, groups * HEAD), bf16),
            pltpu.VMEM((length, groups * HEAD), bf16),
            pltpu.VMEM((run, groups * HEAD), bf16),
            pltpu.VMEM((length, groups * 3 * HEAD), bf16),
            pltpu.VMEM((groups, length, HEAD), f32),
            pltpu.VMEM((groups, length, HEAD), f32),
            pltpu.VMEM((nc, run, piece), bf16),
            pltpu.VMEM((nz, nc, rows, piece), bf16),
            pltpu.VMEM((run, width), bf16),
            pltpu.VMEM((run, width), bf16),
            pltpu.VMEM((run, width), bf16),
            pltpu.VMEM((run, width), bf16),
            pltpu.VMEM((2, run, width), bf16),
            pltpu.VMEM((rows, width), f32),
            dma((5,)),
            dma((2, nz, PARTS)), dma((2, nz, PARTS)),
            dma((2 * nz, PARTS)), dma((2 * nz, PARTS)),
            dma((half, SLABS)), dma((half, SLABS)), dma((half, SLABS)), dma((half, SLABS)),
            dma((5, half, HALVES)), dma((5, half, HALVES)), dma((nc,)), dma((nc,)), dma((ns,)), dma((ns,)),
            dma((2, nz, PARTS)), dma((2, nz, PARTS)), dma((2,)), dma((2,)), dma((nz, half)), dma((nz, half)),
            dma((nz, CHUNKS)), dma((nz, CHUNKS)), dma((2, nz, CHUNKS)), dma((2, nz, CHUNKS)),
        ],
        compiler_params=pltpu.CompilerParams(
            collective_id=0, has_side_effects=True, vmem_limit_bytes=66000000
        ),
    )(
        timesteps, positions, mod_weight, latent[0], cotangent[0],
        input_weight,
        output_weight.reshape(groups * HEAD, piece),
    )
    block_out, latent_grad = pl.pallas_call(
        hand_over,
        out_shape=(
            jax.ShapeDtypeStruct((rows, width), bf16),
            jax.ShapeDtypeStruct((rows, width), f32),
        ),
        in_specs=[vmem] * 2,
        out_specs=(vmem, vmem),
    )(block_out, latent_grad)
    return (block_out[None], latent_grad[None])


def solution(mesh):
    placed = (
        P("cand", "seq", None),
        P(),
        P(),
        P("cand", "seq"),
        P("cand", "seq", None),
        P("seq", None, "cand"),
        P("cand", "seq", None),
    )
    return jax.shard_map(
        on_device,
        mesh=mesh,
        in_specs=placed,
        out_specs=(P("cand", "seq", None), P("cand", "seq", None)),
        check_vma=False,
    )
```

```python
import functools
import math

import jax
import jax.numpy as jnp
from jax import lax
from jax.experimental import pallas as pl
from jax.experimental.pallas import tpu as pltpu
from jax.sharding import PartitionSpec as P

HEAD = 128
CHUNKS = 4
PARTS = 3
SLABS = 6
HALVES = 2
MESH = pl.DeviceIdType.MESH


epsilon = 1e-06


def swap_pairs(values):
    lane = lax.broadcasted_iota(jnp.int32, values.shape, 1)
    small = HEAD // 8
    large = (HEAD - small) // 2
    near = jnp.where(
        lane < small // 2,
        pltpu.roll(values, HEAD - small // 2, 1),
        pltpu.roll(values, small // 2, 1),
    )
    upper = ((lane >= small) & (lane < small + large // 2)) | (
        (lane >= small + large) & (lane < small + large + large // 2)
    )
    far = jnp.where(
        upper, pltpu.roll(values, HEAD - large // 2, 1), pltpu.roll(values, large // 2, 1)
    )
    return jnp.where(lane < small, near, far)


def dot_nt(left, right):
    return lax.dot_general(left, right, (((1,), (1,)), ((), ())), preferred_element_type=jnp.float32)


def dot_tn(left, right):
    return lax.dot_general(left, right, (((0,), (0,)), ((), ())), preferred_element_type=jnp.float32)


def inverse_rms(values):
    return lax.rsqrt(jnp.mean(values * values, -1, keepdims=True) + epsilon)


def layer_norm(values):
    centred = values - jnp.mean(values, -1, keepdims=True)
    inverse_std = lax.rsqrt(jnp.mean(centred * centred, -1, keepdims=True) + epsilon)
    return (centred * inverse_std, inverse_std)


def sections():
    first = HEAD // 8
    other = (HEAD - first) // 2
    return ((0, first), (first, other), (first + other, other))


def step_kernel(
    nc, ns,
    time_ref, pos_ref, mod_w_ref, latent_ref, cot_ref, w_in_ref, w_out_ref,
    block_ref, grad_ref,
    w_raw, mod_w, pos8, angle, cos_ref, sin_ref, part, part_in, mine, mod_all, vecs,
    lat_all, x_all, w_in_all, w_out_all, cot_all, x_cot, proj, inverse_all, q_all, k_all, v_all, probs,
    att, att_near, d_att, d_away, d_proj, key_sum, value_sum, mix_out, mix_in,
    dm_away, dm_here, dm_near, dm_sum, chain_in, total, normed_own, inverse_own, block_own, grad_own,
    out_sem, own_sem, lat_s, lat_r, laty_s, laty_r, wi_s, wi_r, wif_s, wif_r, wo_s, wo_r, m1_s, m1_r,
    m2_s, m2_r, cot_s, cot_r, ex_s, ex_r, mx_s, mx_r, dmn_s, dmn_r, ch_s, ch_r,
):
    me_c = lax.axis_index("cand")
    me_s = lax.axis_index("seq")
    rows, width = latent_ref.shape
    length = rows * ns
    slab = w_in_ref.shape[0]
    groups = q_all.shape[0]
    cols = mod_w_ref.shape[1]
    piece = w_out_ref.shape[1]
    chunk = width // CHUNKS
    half = nc // 2
    core = lax.rem(me_c, 2)
    mate = me_c + 1 - 2 * core
    nz = ns // 2
    me_y, me_z = lax.rem(me_s, 2), lax.div(me_s, 2)
    near = me_s + 1 - 2 * me_y
    score_scale = HEAD ** (-0.5)
    size = rows // PARTS
    span = slab // SLABS
    run = nz * rows
    f32, bf16 = jnp.float32, jnp.bfloat16

    def place(index):
        return lax.rem(index, 2) * nz + lax.div(index, 2)

    def rows_of(index, count):
        return pl.ds(pl.multiple_of(index * count, count), count)

    def link(src, dst, send, recv, cand, seq):
        return pltpu.make_async_remote_copy(
            src_ref=src, dst_ref=dst, send_sem=send, recv_sem=recv,
            device_id=(cand, seq), device_id_type=MESH,
        )

    def remote(*args):
        copy = link(*args)
        copy.start()
        return copy

    def c_peer(k):
        return lax.rem(me_c + k, nc)

    def c_from(k):
        return lax.rem(me_c - k + nc, nc)

    def z_seq(z):
        return 2 * z + me_y

    barrier = pltpu.get_barrier_semaphore()
    for k in range(1, nc):
        pl.semaphore_signal(barrier, inc=1, device_id=(c_peer(k), me_s), device_id_type=MESH)
    for k in range(1, ns):
        pl.semaphore_signal(
            barrier, inc=1, device_id=(me_c, lax.rem(me_s + k, ns)), device_id_type=MESH
        )

    def w_in_at(index, q):
        return w_in_all.at[pl.ds(pl.multiple_of(index * slab + q * span, span), span)]

    own = [
        pltpu.make_async_copy(mod_w_ref, mod_w, own_sem.at[0]),
        pltpu.make_async_copy(latent_ref, lat_all.at[rows_of(place(me_s), rows)], own_sem.at[1]),
        pltpu.make_async_copy(cot_ref, cot_all.at[rows_of(me_z, rows)], own_sem.at[2]),
        pltpu.make_async_copy(w_in_ref, w_raw, own_sem.at[3]),
        pltpu.make_async_copy(w_out_ref, w_out_all.at[me_y, me_c], own_sem.at[4]),
    ]
    for copy in own:
        copy.start()
    tile = 3 * HEAD

    def flatten(i, _):
        at = pl.ds(pl.multiple_of(me_c * slab + i * 16, 16), 16)
        for h in range(groups):
            w_in_all[at, h * tile : (h + 1) * tile] = w_raw[
                pl.ds(pl.multiple_of(i * 16, 16), 16), h
            ]
        return 0

    pl.semaphore_wait(barrier, nc - 1 + ns - 1)

    def lat_at(z, y, p):
        return lat_all.at[pl.ds(pl.multiple_of((y * nz + z) * rows + p * size, size), size)]

    done = []

    def z_send(dirn, hop, p, src, z):
        to = me_z + 1 - 2 * dirn
        return link(
            src, lat_at(z, me_y, p), lat_s.at[dirn, hop, p], lat_r.at[dirn, hop, p],
            me_c, z_seq(to),
        )

    for p in range(PARTS):
        src = latent_ref.at[pl.ds(p * size, size)]
        for dirn, there in ((0, me_z < nz - 1), (1, me_z > 0)):
            @pl.when(there)
            def _():
                z_send(dirn, 0, p, src, me_z).start()
        done.append(
            remote(src, lat_at(me_z, me_y, p), laty_s.at[0, p], laty_r.at[0, p], me_c, near)
        )

    def slab_part(q):
        src = w_in_at(me_c, q)
        return [
            remote(src, w_in_at(me_c, q), wi_s.at[j, q], wi_r.at[j, q], c_peer(2 * j), me_s)
            for j in range(1, half)
        ]

    def flatten_part(q):
        lax.fori_loop(q * span // 16, (q + 1) * span // 16, flatten, 0)

    own[3].wait()
    flatten_part(0)
    w_in_far = [slab_part(0)]

    count = part.shape[0]
    lead = mod_w_ref.shape[0]
    held_rows = max(16, nc)
    index = me_c * lead + lax.broadcasted_iota(jnp.int32, (held_rows, lead), 1)
    steps = width // 2
    is_cos = index < steps
    order = jnp.where(is_cos, index, index - steps).astype(f32)
    row = lax.broadcasted_iota(jnp.int32, (held_rows, 1), 0)
    times = jnp.zeros((held_rows, 1), f32)
    for c in range(nc):
        times = jnp.where(row == c, time_ref[c].astype(f32), times)
    turns = times * jnp.exp(order * (-math.log(10000.0)) / steps)
    wave = jnp.where(is_cos, jnp.cos(turns), jnp.sin(turns))
    act = (wave / (1.0 + jnp.exp(-wave))).astype(bf16)
    own[0].wait()
    product = jnp.dot(act, mod_w[...], preferred_element_type=f32)
    for c in range(count):
        part[c] = product[c : c + 1]
    m1 = []
    for k in range(1, nc):
        peer = c_peer(k)
        m1.append(remote(part.at[peer], part_in.at[me_c], m1_s.at[k], m1_r.at[k], peer, me_s))
    for q in range(1, SLABS):
        flatten_part(q)
        w_in_far.append(slab_part(q))
    w_in_mate = remote(
        w_in_all.at[rows_of(me_c, slab)], w_in_all.at[rows_of(me_c, slab)], wif_s.at[0, 0],
        wif_r.at[0, 0], mate, me_s
    )

    part_rows = w_out_ref.shape[0] // HALVES

    def w_out_at(y, c, q):
        return w_out_all.at[y, c, pl.ds(q * part_rows, part_rows)]

    def w_out_send(kind, j, q, src, y, c, cand, seq):
        return remote(
            src, w_out_at(y, c, q), wo_s.at[kind, j, q], wo_r.at[kind, j, q], cand, seq
        )

    def w_out_own(q):
        return w_out_ref.at[pl.ds(q * part_rows, part_rows)]

    w_out_far = [
        [
            w_out_send(0, j, q, w_out_own(q), me_y, me_c, c_peer(2 * j), me_s)
            for j in range(1, half)
        ]
        for q in range(HALVES)
    ]
    w_out_mate = [
        w_out_send(0, 0, q, w_out_own(q), me_y, me_c, mate, me_s) for q in range(HALVES)
    ]

    pos8[...] = jnp.zeros_like(pos8)
    pos8[0 : pos_ref.shape[0]] = pos_ref[...].astype(f32)
    lane = lax.broadcasted_iota(jnp.int32, (8, HEAD), 1)
    axis = lax.broadcasted_iota(jnp.int32, (8, HEAD), 0)
    rate = jnp.zeros((8, HEAD), f32)
    sign = jnp.ones((8, HEAD), f32)
    for a, (start, extent) in enumerate(sections()):
        inside = (lane >= start) & (lane < start + extent)
        late = inside & (lane >= start + extent // 2)
        pair = jnp.where(late, lane - start - extent // 2, lane - start).astype(f32)
        value = jnp.exp(pair * (-math.log(256.0) * 2.0 / extent))
        rate = jnp.where(inside & (axis == a), value, rate)
        sign = jnp.where(inside & ~late, -1.0, sign)
    angle[...] = lax.dot_general(
        pos8[...], rate, (((0,), (0,)), ((), ())), preferred_element_type=f32,
        precision=lax.Precision.HIGHEST,
    )

    def turn_rows(s, _):
        turned = angle[rows_of(s, rows)]
        at = rows_of(place(s), rows)
        cos_ref[at] = jnp.cos(turned)
        sin_ref[at] = jnp.sin(turned) * sign[0:1]
        return 0

    lax.fori_loop(0, ns, turn_rows, 0)

    def exists(dirn, hop):
        return me_z >= hop if dirn == 0 else me_z <= nz - 1 - hop

    def beyond(dirn):
        return me_z < nz - 1 if dirn == 0 else me_z > 0

    def source(dirn, hop):
        return me_z - hop if dirn == 0 else me_z + hop

    def y_slot(dirn, hop):
        return hop if dirn == 0 else nz - 1 + hop

    def y_link(dirn, hop, p):
        held = lat_at(source(dirn, hop), me_y, p)
        slot = y_slot(dirn, hop)
        return link(held, held, laty_s.at[slot, p], laty_r.at[slot, p], me_c, near)

    def relay(hop):
        for p in range(PARTS):
            for dirn in range(2):
                @pl.when(exists(dirn, hop))
                def _():
                    z = source(dirn, hop)
                    held = lat_at(z, me_y, p)
                    z_send(dirn, hop - 1, p, held, z).wait_recv()
                    if hop < nz - 1:
                        @pl.when(beyond(dirn))
                        def _():
                            z_send(dirn, hop, p, held, z).start()
                    y_link(dirn, hop, p).start()

    relay(1)
    for copy in m1:
        copy.wait_recv()
    summed_mod = part[me_c]
    for k in range(1, nc):
        summed_mod = summed_mod + part_in[c_from(k)]
    mine[...] = summed_mod
    mod_all[me_s] = summed_mod
    m2 = [
        remote(
            mine, mod_all.at[me_s], m2_s.at[k], m2_r.at[k], me_c, lax.rem(me_s + k, ns)
        )
        for k in range(1, ns)
    ]
    for hop in range(2, nz - 1):
        relay(hop)

    def cot_at(z, p):
        return cot_all.at[pl.ds(pl.multiple_of(z * rows + p * size, size), size)]

    def cot_send(dirn, hop, p, src, z):
        return link(
            src, cot_at(z, p), cot_s.at[dirn, hop, p], cot_r.at[dirn, hop, p],
            me_c, z_seq(me_z + 1 - 2 * dirn),
        )

    for p in range(PARTS):
        for dirn in range(2):
            @pl.when(beyond(dirn))
            def _():
                cot_send(dirn, 0, p, cot_ref.at[pl.ds(p * size, size)], me_z).start()

    def cot_relay(hop):
        for p in range(PARTS):
            for dirn in range(2):
                @pl.when(exists(dirn, hop))
                def _():
                    z = source(dirn, hop)
                    cot_send(dirn, hop - 1, p, cot_at(z, p), z).wait_recv()
                    if hop < nz - 1:
                        @pl.when(beyond(dirn))
                        def _():
                            cot_send(dirn, hop, p, cot_at(z, p), z).start()

    def gate_rows(z):
        def body(index, _):
            at = pl.ds(pl.multiple_of(z * rows + index * 16, 16), 16)
            gated = (cot_all[at].astype(f32) * vecs[2]).astype(bf16)
            for c in range(nc):
                x_cot[c, at] = gated[:, c * piece : (c + 1) * piece]
            return 0

        lax.fori_loop(0, rows // 16, body, 0)

    def gate_hop(hop):
        for dirn in range(2):
            @pl.when(exists(dirn, hop))
            def _():
                gate_rows(source(dirn, hop))

    for copy in m2:
        copy.wait_recv()
    for s in range(ns):
        at = s * cols
        while at < (s + 1) * cols:
            kind = at // width
            stop = min((s + 1) * cols, (kind + 1) * width)
            vecs[kind, :, at - kind * width : stop - kind * width] = mod_all[
                s, :, at - s * cols : stop - s * cols
            ]
            at = stop

    def norm_rows(at):
        normed, _inverse = layer_norm(lat_all[at].astype(f32))
        x_all[at] = (normed * (1.0 + vecs[1]) + vecs[0]).astype(bf16)

    def norm_run(start, count):
        def body(i, _):
            norm_rows(pl.ds(pl.multiple_of(start + i * 16, 16), 16))
            return 0

        lax.fori_loop(0, count // 16, body, 0)

    own[1].wait()
    norm_run(place(me_s) * rows, rows)
    for dirn in range(2):
        for hop in range(1, nz - 1):
            @pl.when(exists(dirn, hop))
            def _():
                norm_run((me_y * nz + source(dirn, hop)) * rows, rows)

    if nz > 1:
        relay(nz - 1)
        for dirn in range(2):
            @pl.when(exists(dirn, nz - 1))
            def _():
                norm_run((me_y * nz + source(dirn, nz - 1)) * rows, rows)

    w_out_near = [
        w_out_send(1, 0, q, w_out_own(q), me_y, me_c, me_c, near) for q in range(HALVES)
    ]

    w_in_second = []

    def slab_forward(q):
        for j in range(1, half):
            w_in_far[q][j - 1].wait_recv()
            held = w_in_at(c_from(2 * j), q)
            w_in_second.append(
                remote(held, held, wif_s.at[j, q], wif_r.at[j, q], mate, me_s)
            )

    for q in range(SLABS - 1):
        slab_forward(q)
    for copy in done:
        copy.wait_recv()
    norm_run(((1 - me_y) * nz + me_z) * rows, rows)
    for hop in range(1, nz):
        if hop == nz - 1:
            if nz > 2:
                cot_relay(1)
            slab_forward(SLABS - 1)
        for dirn in range(2):
            @pl.when(exists(dirn, hop))
            def _():
                for p in range(PARTS):
                    y_link(dirn, hop, p).wait_recv()
                norm_run(((1 - me_y) * nz + source(dirn, hop)) * rows, rows)
    w_in_mate.wait_recv()
    for copy in w_in_second:
        copy.wait_recv()

    def project(index, _):
        at = pl.ds(pl.multiple_of(index * tile, tile), tile)
        proj[index] = jnp.dot(x_all[...], w_in_all[:, at], preferred_element_type=f32)
        return 0

    lax.fori_loop(0, groups, project, 0)
    for hop in range(2, nz - 1):
        cot_relay(hop)

    def head_at(h):
        return pl.ds(h * HEAD, HEAD)

    def head_forward(h, _):
        query = proj[h, :, 0:HEAD]
        key = proj[h, :, HEAD : 2 * HEAD]
        query_inverse = inverse_rms(query)
        key_inverse = inverse_rms(key)
        query_n = query * query_inverse
        key_n = key * key_inverse
        proj[h, :, 0:HEAD] = query_n
        proj[h, :, HEAD : 2 * HEAD] = key_n
        inverse_all[2 * h] = jnp.broadcast_to(query_inverse, query.shape)
        inverse_all[2 * h + 1] = jnp.broadcast_to(key_inverse, key.shape)
        q_rot = (query_n * cos_ref[...] + swap_pairs(query_n) * sin_ref[...]).astype(bf16)
        k_rot = (key_n * cos_ref[...] + swap_pairs(key_n) * sin_ref[...]).astype(bf16)
        values = proj[h, :, 2 * HEAD :].astype(bf16)
        q_all[h] = q_rot
        k_all[h] = k_rot
        v_all[h] = values
        weights = jnp.exp(dot_nt(q_rot, k_rot) * score_scale - HEAD**0.5)
        share = weights * (1.0 / jnp.sum(weights, -1, keepdims=True))
        probs[h] = share
        att[:, head_at(h)] = jnp.dot(
            share.astype(bf16), values, preferred_element_type=f32
        ).astype(bf16)
        return 0

    for h in range(groups):
        head_forward(h, 0)
    att_move = remote(
        att.at[rows_of(1 - me_y, run)], att_near, ex_s.at[0], ex_r.at[0], me_c, near
    )

    def att_rows(which):
        return att[rows_of(me_y, run)] if which == 0 else att_near[...]

    mixed = []

    def mix_chip(j):
        first = 2 * lax.rem(lax.div(me_c, 2) + j, half)
        for b in range(2):
            mix_out[first + b] = (
                jnp.dot(att_rows(0), w_out_all[me_y, first + b], preferred_element_type=f32)
                + jnp.dot(att_rows(1), w_out_all[1 - me_y, first + b], preferred_element_type=f32)
            ).astype(bf16)
        for k in range(1, nz):
            peer = lax.rem(me_z + k, nz)
            mixed.append(
                remote(
                    mix_out.at[pl.ds(first, 2), rows_of(peer, rows)],
                    mix_in.at[me_z, pl.ds(first, 2)],
                    mx_s.at[k, j], mx_r.at[k, j], me_c, z_seq(peer),
                )
            )

    w_out_second = []
    w_out_cross = []
    w_out_near_mate = []
    for q in range(HALVES):
        w_out_near[q].wait_recv()
        w_out_near_mate.append(
            w_out_send(2, 0, q, w_out_at(1 - me_y, me_c, q), 1 - me_y, me_c, mate, me_s)
        )
        for j in range(1, half):
            w_out_far[q][j - 1].wait_recv()
            from_y = jnp.where(core == 0, me_y, 1 - me_y)
            from_c = jnp.where(core == 0, c_from(2 * j), me_c)
            w_out_cross.append(
                w_out_send(
                    3, j, q, w_out_at(from_y, from_c, q), from_y, from_c,
                    jnp.where(core == 0, me_c, c_peer(2 * j)), jnp.where(core == 0, near, me_s),
                )
            )
            w_out_second.append(
                w_out_send(
                    2, j, q, w_out_at(me_y, c_from(2 * j), q), me_y, c_from(2 * j), mate, me_s
                )
            )

    own[4].wait()
    for copy in w_out_mate + [att_move] + w_out_near_mate:
        copy.wait_recv()
    mix_chip(0)

    own[2].wait()
    gate_rows(me_z)
    for hop in range(1, nz - 1):
        gate_hop(hop)
    cot_relay(nz - 1)
    gate_hop(nz - 1)

    def d_attended(y, first, count):
        block = jnp.zeros((run, groups * HEAD), f32)
        for i in range(count):
            c = first + i
            block = block + dot_nt(x_cot[c], w_out_all[y, c])
        return block

    chip = 2 * lax.div(me_c, 2)
    away_sum = d_attended(1 - me_y, chip, 2)
    for q in range(HALVES):
        for j in range(1, half):
            held = w_out_at(1 - me_y, c_from(2 * j), q)
            link(held, held, wo_s.at[3, j, q], wo_r.at[3, j, q], me_c, near).wait_recv()
            w_out_second.append(
                w_out_send(4, j, q, held, 1 - me_y, c_from(2 * j), mate, me_s)
            )
    for copy in w_out_second:
        copy.wait_recv()
    for j in range(1, half):
        away_sum = away_sum + d_attended(1 - me_y, 2 * lax.rem(lax.div(me_c, 2) + j, half), 2)
    d_away[...] = away_sum.astype(bf16)
    d_move = [
        remote(
            d_away.at[:, head_at(h)], d_att.at[rows_of(me_y, run), head_at(h)],
            ex_s.at[1 + h], ex_r.at[1 + h], me_c, near,
        )
        for h in range(groups)
    ]
    d_att[rows_of(me_y, run)] = d_attended(me_y, 0, nc).astype(bf16)
    for j in range(1, half):
        mix_chip(j)

    def back_norm(d_rot, normed, inverse, cos, sin):
        d_normed = d_rot * cos - swap_pairs(d_rot) * sin
        return inverse * (d_normed - normed * jnp.mean(d_normed * normed, -1, keepdims=True))

    def query_part(h, y):
        at = rows_of(y, run)
        d_heads = d_att[at, head_at(h)]
        share = probs[h, at]
        d_values = dot_tn(share.astype(bf16), d_heads)
        d_probs = dot_nt(d_heads, v_all[h])
        d_scores = (share * (d_probs - jnp.sum(share * d_probs, -1, keepdims=True))).astype(bf16)
        d_qrot = jnp.dot(d_scores, k_all[h], preferred_element_type=f32) * score_scale
        d_krot = dot_tn(d_scores, q_all[h, at])
        d_query = back_norm(
            d_qrot, proj[h, at, 0:HEAD], inverse_all[2 * h, at], cos_ref[at], sin_ref[at]
        )
        d_proj[at, head_at(3 * h)] = d_query.astype(bf16)
        return d_values, d_krot

    def first_half(h, _):
        d_values, d_krot = query_part(h, me_y)
        value_sum[h] = d_values
        key_sum[h] = d_krot
        return 0

    for h in range(groups):
        first_half(h, 0)

    def second_half(h, _):
        d_values, d_krot = query_part(h, 1 - me_y)
        d_key = back_norm(
            (key_sum[h] + d_krot) * score_scale, proj[h, :, HEAD : 2 * HEAD],
            inverse_all[2 * h + 1], cos_ref[...], sin_ref[...],
        )
        d_proj[:, head_at(3 * h + 1)] = d_key.astype(bf16)
        d_proj[:, head_at(3 * h + 2)] = (value_sum[h] + d_values).astype(bf16)
        return 0

    for h in range(groups):
        d_move[h].wait_recv()
        second_half(h, 0)

    order = []
    low, high = 0, nz - 1
    for i in range(nz):
        take = (me_z - low >= high - me_z).astype(jnp.int32)
        order.append(take * low + (1 - take) * high)
        low, high = low + take, high - (1 - take)

    d_near = [[] for _ in range(nz)]

    def away(i, j):
        if i < nz - 1:
            at = (rows_of(order[i], rows), pl.ds(j * chunk, chunk))
        else:
            at = pl.ds(pl.multiple_of(me_z * rows + j * 16, 16), 16)
        d_near[i].append(
            remote(dm_away.at[at], dm_near.at[at], dmn_s.at[i, j], dmn_r.at[i, j], me_c, near)
        )

    for j in range(CHUNKS):
        part_cols = slice(j * chunk, (j + 1) * chunk)
        dm_away[:, part_cols] = dot_nt(
            d_proj[rows_of(1 - me_y, run)], w_in_all[part_cols]
        ).astype(bf16)
        away(0, j)
    for i in range(1, nz):
        for j in range(CHUNKS if i < nz - 1 else rows // 16):
            away(i, j)
    for j in range(CHUNKS):
        part_cols = slice(j * chunk, (j + 1) * chunk)
        dm_here[:, part_cols] = dot_nt(
            d_proj[rows_of(me_y, run)], w_in_all[part_cols]
        ).astype(bf16)

    def lat_rows(start):
        return lat_all[pl.ds(pl.multiple_of(place(me_s) * rows + start, 16), 16)].astype(f32)

    for start in range(0, rows, 16):
        normed, inverse_std = layer_norm(lat_rows(start))
        normed_own[start : start + 16] = normed
        inverse_own[start : start + 16] = jnp.broadcast_to(inverse_std, (16, HEAD))

    chain = []
    for i in range(nz - 1):
        to = order[i]
        up = to > me_z
        dirn = 1 - up.astype(jnp.int32)
        fed = (up & (me_z > 0)) | (~up & (me_z < nz - 1))
        beside = z_seq(me_z + 1 - 2 * dirn)
        for j in range(CHUNKS):
            at = (rows_of(to, rows), pl.ds(j * chunk, chunk))
            d_near[i][j].wait_recv()
            hop = link(
                dm_sum.at[at], chain_in.at[(dirn,) + at], ch_s.at[dirn, to, j],
                ch_r.at[dirn, to, j], me_c, beside,
            )
            value = dm_here[at].astype(f32) + dm_near[at].astype(f32)

            @pl.when(fed)
            def _():
                hop.wait_recv()
                dm_sum[at] = (value + chain_in[(dirn,) + at].astype(f32)).astype(bf16)

            @pl.when(~fed)
            def _():
                dm_sum[at] = value.astype(bf16)

            hop.start()
            chain.append(hop)

    for copy in mixed:
        copy.wait_recv()
    leave = []
    for start in range(0, rows, 16):
        mine_at = pl.ds(pl.multiple_of(me_z * rows + start, 16), 16)
        latent_rows = lat_rows(start)
        for c in range(nc):
            value = mix_out[c, mine_at].astype(f32)
            for k in range(1, nz):
                value = value + mix_in[lax.rem(me_z + k, nz), c, start : start + 16].astype(f32)
            part_cols = slice(c * piece, (c + 1) * piece)
            block_own[start : start + 16, part_cols] = (
                latent_rows[:, part_cols] + vecs[2, :, part_cols] * value
            ).astype(bf16)
    leave.append(pltpu.make_async_copy(block_own, block_ref, out_sem.at[0]))
    leave[0].start()

    total[...] = dm_here[rows_of(me_z, rows)].astype(f32)
    for dirn, fed in ((0, me_z > 0), (1, me_z < nz - 1)):
        @pl.when(fed)
        def _():
            for j in range(CHUNKS):
                part_cols = pl.ds(j * chunk, chunk)
                landed = chain_in.at[dirn, rows_of(me_z, rows), part_cols]
                link(
                    landed, landed, ch_s.at[dirn, me_z, j], ch_r.at[dirn, me_z, j], me_c, near
                ).wait_recv()
                total[:, part_cols] += landed[...].astype(f32)

    for j in range(rows // 16):
        at = slice(16 * j, 16 * j + 16)
        mine_at = pl.ds(pl.multiple_of(me_z * rows + 16 * j, 16), 16)
        d_near[nz - 1][j].wait_recv()
        d_normed = (total[at] + dm_near[mine_at].astype(f32)) * (1.0 + vecs[1])
        normed = normed_own[at]
        grad_own[at] = cot_all[mine_at].astype(f32) + inverse_own[at, 0:1] * (
            d_normed
            - jnp.mean(d_normed, -1, keepdims=True)
            - normed * jnp.mean(d_normed * normed, -1, keepdims=True)
        )
        leave.append(
            pltpu.make_async_copy(grad_own.at[at], grad_ref.at[at], out_sem.at[1 + j])
        )
        leave[-1].start()

    for p in range(PARTS):
        for dirn in range(2):
            for hop in range(nz - 1):
                @pl.when(exists(dirn, hop) & beyond(dirn))
                def _():
                    held = lat_at(source(dirn, hop), me_y, p)
                    z_send(dirn, hop, p, held, source(dirn, hop)).wait_send()
                    held = cot_at(source(dirn, hop), p)
                    cot_send(dirn, hop, p, held, source(dirn, hop)).wait_send()
            for hop in range(1, nz):
                @pl.when(exists(dirn, hop))
                def _():
                    y_link(dirn, hop, p).wait_send()
    for copy in (
        done + m1 + m2 + sum(w_in_far, []) + [w_in_mate] + w_in_second + sum(w_out_far, [])
        + w_out_mate + w_out_near + w_out_near_mate + w_out_second + w_out_cross
        + [att_move] + d_move + mixed + sum(d_near, []) + chain
    ):
        copy.wait_send()
    for copy in leave:
        copy.wait()


def hand_over(block_ref, grad_ref, block_out, grad_out):
    block_out[...] = block_ref[...]
    grad_out[...] = grad_ref[...]


def on_device(latent, timesteps, positions, mod_weight, input_weight, output_weight, cotangent):
    nc = lax.axis_size("cand")
    ns = lax.axis_size("seq")
    rows, width = latent.shape[1:]
    length = rows * ns
    slab = input_weight.shape[0]
    groups = input_weight.shape[1]
    cols = mod_weight.shape[1]
    piece = output_weight.shape[2]
    half = nc // 2
    nz = ns // 2
    run = nz * rows
    vmem = pl.BlockSpec(memory_space=pltpu.VMEM)
    smem = pl.BlockSpec(memory_space=pltpu.SMEM)
    anywhere = pl.BlockSpec(memory_space=pl.ANY)
    f32, bf16 = jnp.float32, jnp.bfloat16
    dma = pltpu.SemaphoreType.DMA
    block_out, latent_grad = pl.pallas_call(
        functools.partial(step_kernel, nc, ns),
        out_shape=(
            jax.ShapeDtypeStruct((rows, width), bf16),
            jax.ShapeDtypeStruct((rows, width), f32),
        ),
        in_specs=[smem, vmem] + [anywhere] * 5,
        out_specs=(anywhere, anywhere),
        scratch_shapes=[
            pltpu.VMEM(input_weight.shape, bf16),
            pltpu.VMEM(mod_weight.shape, bf16),
            pltpu.VMEM((8, length), f32),
            pltpu.VMEM((length, HEAD), f32),
            pltpu.VMEM((length, HEAD), f32),
            pltpu.VMEM((length, HEAD), f32),
            pltpu.VMEM((nc, 1, cols), f32),
            pltpu.VMEM((nc, 1, cols), f32),
            pltpu.VMEM((1, cols), f32),
            pltpu.VMEM((ns, 1, cols), f32),
            pltpu.VMEM((3, 1, width), f32),
            pltpu.VMEM((length, width), bf16),
            pltpu.VMEM((length, width), bf16),
            pltpu.VMEM((slab * nc, groups * 3 * HEAD), bf16),
            pltpu.VMEM((2, nc, groups * HEAD, piece), bf16),
            pltpu.VMEM((run, width), bf16),
            pltpu.VMEM((nc, run, piece), bf16),
            pltpu.VMEM((groups, length, 3 * HEAD), f32),
            pltpu.VMEM((2 * groups, length, HEAD), f32),
            pltpu.VMEM((groups, length, HEAD), bf16),
            pltpu.VMEM((groups, length, HEAD), bf16),
            pltpu.VMEM((groups, length, HEAD), bf16),
            pltpu.VMEM((groups, length, length), f32),
            pltpu.VMEM((length, groups * HEAD), bf16),
            pltpu.VMEM((run, groups * HEAD), bf16),
            pltpu.VMEM((length, groups * HEAD), bf16),
            pltpu.VMEM((run, groups * HEAD), bf16),
            pltpu.VMEM((length, groups * 3 * HEAD), bf16),
            pltpu.VMEM((groups, length, HEAD), f32),
            pltpu.VMEM((groups, length, HEAD), f32),
            pltpu.VMEM((nc, run, piece), bf16),
            pltpu.VMEM((nz, nc, rows, piece), bf16),
            pltpu.VMEM((run, width), bf16),
            pltpu.VMEM((run, width), bf16),
            pltpu.VMEM((run, width), bf16),
            pltpu.VMEM((run, width), bf16),
            pltpu.VMEM((2, run, width), bf16),
            pltpu.VMEM((rows, width), f32),
            pltpu.VMEM((rows, width), f32),
            pltpu.VMEM((rows, HEAD), f32),
            pltpu.VMEM((rows, width), bf16),
            pltpu.VMEM((rows, width), f32),
            dma((1 + rows // 16,)),
            dma((5,)),
            dma((2, nz, PARTS)), dma((2, nz, PARTS)),
            dma((2 * nz, PARTS)), dma((2 * nz, PARTS)),
            dma((half, SLABS)), dma((half, SLABS)), dma((half, SLABS)), dma((half, SLABS)),
            dma((5, half, HALVES)), dma((5, half, HALVES)), dma((nc,)), dma((nc,)), dma((ns,)), dma((ns,)),
            dma((2, nz, PARTS)), dma((2, nz, PARTS)), dma((1 + groups,)), dma((1 + groups,)), dma((nz, half)), dma((nz, half)),
            dma((nz, max(CHUNKS, rows // 16))), dma((nz, max(CHUNKS, rows // 16))), dma((2, nz, CHUNKS)), dma((2, nz, CHUNKS)),
        ],
        compiler_params=pltpu.CompilerParams(
            collective_id=0, has_side_effects=True, vmem_limit_bytes=66000000
        ),
    )(
        timesteps, positions, mod_weight, latent[0], cotangent[0],
        input_weight,
        output_weight.reshape(groups * HEAD, piece),
    )
    block_out, latent_grad = pl.pallas_call(
        hand_over,
        out_shape=(
            jax.ShapeDtypeStruct((rows, width), bf16),
            jax.ShapeDtypeStruct((rows, width), f32),
        ),
        in_specs=[vmem] * 2,
        out_specs=(vmem, vmem),
    )(block_out, latent_grad)
    return (block_out[None], latent_grad[None])


def solution(mesh):
    placed = (
        P("cand", "seq", None),
        P(),
        P(),
        P("cand", "seq"),
        P("cand", "seq", None),
        P("seq", None, "cand"),
        P("cand", "seq", None),
    )
    return jax.shard_map(
        on_device,
        mesh=mesh,
        in_specs=placed,
        out_specs=(P("cand", "seq", None), P("cand", "seq", None)),
        check_vma=False,
    )
```

```python
import functools
import math

import jax
import jax.numpy as jnp
from jax import lax
from jax.experimental import pallas as pl
from jax.experimental.pallas import tpu as pltpu
from jax.sharding import PartitionSpec as P

HEAD = 128
CHUNKS = 4
PARTS = 3
SLABS = 6
HALVES = 2
MESH = pl.DeviceIdType.MESH


epsilon = 1e-06


def swap_pairs(values):
    lane = lax.broadcasted_iota(jnp.int32, values.shape, 1)
    small = HEAD // 8
    large = (HEAD - small) // 2
    near = jnp.where(
        lane < small // 2,
        pltpu.roll(values, HEAD - small // 2, 1),
        pltpu.roll(values, small // 2, 1),
    )
    upper = ((lane >= small) & (lane < small + large // 2)) | (
        (lane >= small + large) & (lane < small + large + large // 2)
    )
    far = jnp.where(
        upper, pltpu.roll(values, HEAD - large // 2, 1), pltpu.roll(values, large // 2, 1)
    )
    return jnp.where(lane < small, near, far)


def dot_nt(left, right):
    return lax.dot_general(left, right, (((1,), (1,)), ((), ())), preferred_element_type=jnp.float32)


def dot_tn(left, right):
    return lax.dot_general(left, right, (((0,), (0,)), ((), ())), preferred_element_type=jnp.float32)


def inverse_rms(values):
    return lax.rsqrt(jnp.mean(values * values, -1, keepdims=True) + epsilon)


def layer_norm(values):
    centred = values - jnp.mean(values, -1, keepdims=True)
    inverse_std = lax.rsqrt(jnp.mean(centred * centred, -1, keepdims=True) + epsilon)
    return (centred * inverse_std, inverse_std)


def sections():
    first = HEAD // 8
    other = (HEAD - first) // 2
    return ((0, first), (first, other), (first + other, other))


def step_kernel(
    nc, ns,
    time_ref, pos_ref, mod_w_ref, latent_ref, cot_ref, w_in_ref, w_out_ref,
    block_ref, grad_ref,
    w_raw, mod_w, pos8, angle, cos_ref, sin_ref, part, part_in, mine, mod_all, vecs,
    lat_all, x_all, w_in_all, w_out_all, cot_all, x_cot, proj, inverse_all, q_all, k_all, v_all, probs,
    att, att_near, d_att, d_away, d_proj, key_sum, value_sum, mix_out, mix_in,
    dm_away, dm_here, dm_near, dm_sum, chain_in, total, normed_own, inverse_own, block_own, grad_own,
    out_sem, own_sem, lat_s, lat_r, laty_s, laty_r, wi_s, wi_r, wif_s, wif_r, wo_s, wo_r, m1_s, m1_r,
    m2_s, m2_r, cot_s, cot_r, ex_s, ex_r, mx_s, mx_r, dmn_s, dmn_r, ch_s, ch_r,
):
    me_c = lax.axis_index("cand")
    me_s = lax.axis_index("seq")
    rows, width = latent_ref.shape
    length = rows * ns
    slab = w_in_ref.shape[0]
    groups = q_all.shape[0]
    cols = mod_w_ref.shape[1]
    piece = w_out_ref.shape[1]
    chunk = width // CHUNKS
    half = nc // 2
    core = lax.rem(me_c, 2)
    mate = me_c + 1 - 2 * core
    nz = ns // 2
    me_y, me_z = lax.rem(me_s, 2), lax.div(me_s, 2)
    near = me_s + 1 - 2 * me_y
    score_scale = HEAD ** (-0.5)
    size = rows // PARTS
    span = slab // SLABS
    run = nz * rows
    f32, bf16 = jnp.float32, jnp.bfloat16

    def place(index):
        return lax.rem(index, 2) * nz + lax.div(index, 2)

    def rows_of(index, count):
        return pl.ds(pl.multiple_of(index * count, count), count)

    def link(src, dst, send, recv, cand, seq):
        return pltpu.make_async_remote_copy(
            src_ref=src, dst_ref=dst, send_sem=send, recv_sem=recv,
            device_id=(cand, seq), device_id_type=MESH,
        )

    def remote(*args):
        copy = link(*args)
        copy.start()
        return copy

    def c_peer(k):
        return lax.rem(me_c + k, nc)

    def c_from(k):
        return lax.rem(me_c - k + nc, nc)

    def z_seq(z):
        return 2 * z + me_y

    barrier = pltpu.get_barrier_semaphore()
    for k in range(1, nc):
        pl.semaphore_signal(barrier, inc=1, device_id=(c_peer(k), me_s), device_id_type=MESH)
    for k in range(1, ns):
        pl.semaphore_signal(
            barrier, inc=1, device_id=(me_c, lax.rem(me_s + k, ns)), device_id_type=MESH
        )

    def w_in_at(index, q):
        return w_in_all.at[pl.ds(pl.multiple_of(index * slab + q * span, span), span)]

    own = [
        pltpu.make_async_copy(mod_w_ref, mod_w, own_sem.at[0]),
        pltpu.make_async_copy(latent_ref, lat_all.at[rows_of(place(me_s), rows)], own_sem.at[1]),
        pltpu.make_async_copy(cot_ref, cot_all.at[rows_of(me_z, rows)], own_sem.at[2]),
        pltpu.make_async_copy(w_in_ref, w_raw, own_sem.at[3]),
        pltpu.make_async_copy(w_out_ref, w_out_all.at[me_y, me_c], own_sem.at[4]),
    ]
    for copy in own:
        copy.start()
    tile = 3 * HEAD

    def flatten(i, _):
        at = pl.ds(pl.multiple_of(me_c * slab + i * 16, 16), 16)
        for h in range(groups):
            w_in_all[at, h * tile : (h + 1) * tile] = w_raw[
                pl.ds(pl.multiple_of(i * 16, 16), 16), h
            ]
        return 0

    pl.semaphore_wait(barrier, nc - 1 + ns - 1)

    def lat_at(z, y, p):
        return lat_all.at[pl.ds(pl.multiple_of((y * nz + z) * rows + p * size, size), size)]

    done = []

    def z_send(dirn, hop, p, src, z):
        to = me_z + 1 - 2 * dirn
        return link(
            src, lat_at(z, me_y, p), lat_s.at[dirn, hop, p], lat_r.at[dirn, hop, p],
            me_c, z_seq(to),
        )

    for p in range(PARTS):
        src = latent_ref.at[pl.ds(p * size, size)]
        for dirn, there in ((0, me_z < nz - 1), (1, me_z > 0)):
            @pl.when(there)
            def _():
                z_send(dirn, 0, p, src, me_z).start()
        done.append(
            remote(src, lat_at(me_z, me_y, p), laty_s.at[0, p], laty_r.at[0, p], me_c, near)
        )

    def slab_part(q):
        src = w_in_at(me_c, q)
        return [
            remote(src, w_in_at(me_c, q), wi_s.at[j, q], wi_r.at[j, q], c_peer(2 * j), me_s)
            for j in range(1, half)
        ]

    def flatten_part(q):
        lax.fori_loop(q * span // 16, (q + 1) * span // 16, flatten, 0)

    own[3].wait()
    flatten_part(0)
    w_in_far = [slab_part(0)]

    count = part.shape[0]
    lead = mod_w_ref.shape[0]
    held_rows = max(16, nc)
    index = me_c * lead + lax.broadcasted_iota(jnp.int32, (held_rows, lead), 1)
    steps = width // 2
    is_cos = index < steps
    order = jnp.where(is_cos, index, index - steps).astype(f32)
    row = lax.broadcasted_iota(jnp.int32, (held_rows, 1), 0)
    times = jnp.zeros((held_rows, 1), f32)
    for c in range(nc):
        times = jnp.where(row == c, time_ref[c].astype(f32), times)
    turns = times * jnp.exp(order * (-math.log(10000.0)) / steps)
    wave = jnp.where(is_cos, jnp.cos(turns), jnp.sin(turns))
    act = (wave / (1.0 + jnp.exp(-wave))).astype(bf16)
    own[0].wait()
    product = jnp.dot(act, mod_w[...], preferred_element_type=f32)
    for c in range(count):
        part[c] = product[c : c + 1]
    m1 = []
    for k in range(1, nc):
        peer = c_peer(k)
        m1.append(remote(part.at[peer], part_in.at[me_c], m1_s.at[k], m1_r.at[k], peer, me_s))
    for q in range(1, SLABS):
        flatten_part(q)
        w_in_far.append(slab_part(q))
    w_in_mate = remote(
        w_in_all.at[rows_of(me_c, slab)], w_in_all.at[rows_of(me_c, slab)], wif_s.at[0, 0],
        wif_r.at[0, 0], mate, me_s
    )

    part_rows = w_out_ref.shape[0] // HALVES

    def w_out_at(y, c, q):
        return w_out_all.at[y, c, pl.ds(q * part_rows, part_rows)]

    def w_out_send(kind, j, q, src, y, c, cand, seq):
        return remote(
            src, w_out_at(y, c, q), wo_s.at[kind, j, q], wo_r.at[kind, j, q], cand, seq
        )

    def w_out_own(q):
        return w_out_ref.at[pl.ds(q * part_rows, part_rows)]

    w_out_far = [
        [
            w_out_send(0, j, q, w_out_own(q), me_y, me_c, c_peer(2 * j), me_s)
            for j in range(1, half)
        ]
        for q in range(HALVES)
    ]
    w_out_mate = [
        w_out_send(0, 0, q, w_out_own(q), me_y, me_c, mate, me_s) for q in range(HALVES)
    ]

    pos8[...] = jnp.zeros_like(pos8)
    pos8[0 : pos_ref.shape[0]] = pos_ref[...].astype(f32)
    lane = lax.broadcasted_iota(jnp.int32, (8, HEAD), 1)
    axis = lax.broadcasted_iota(jnp.int32, (8, HEAD), 0)
    rate = jnp.zeros((8, HEAD), f32)
    sign = jnp.ones((8, HEAD), f32)
    for a, (start, extent) in enumerate(sections()):
        inside = (lane >= start) & (lane < start + extent)
        late = inside & (lane >= start + extent // 2)
        pair = jnp.where(late, lane - start - extent // 2, lane - start).astype(f32)
        value = jnp.exp(pair * (-math.log(256.0) * 2.0 / extent))
        rate = jnp.where(inside & (axis == a), value, rate)
        sign = jnp.where(inside & ~late, -1.0, sign)
    angle[...] = lax.dot_general(
        pos8[...], rate, (((0,), (0,)), ((), ())), preferred_element_type=f32,
        precision=lax.Precision.HIGHEST,
    )

    def turn_rows(s, _):
        turned = angle[rows_of(s, rows)]
        at = rows_of(place(s), rows)
        cos_ref[at] = jnp.cos(turned)
        sin_ref[at] = jnp.sin(turned) * sign[0:1]
        return 0

    lax.fori_loop(0, ns, turn_rows, 0)

    def exists(dirn, hop):
        return me_z >= hop if dirn == 0 else me_z <= nz - 1 - hop

    def beyond(dirn):
        return me_z < nz - 1 if dirn == 0 else me_z > 0

    def source(dirn, hop):
        return me_z - hop if dirn == 0 else me_z + hop

    def y_slot(dirn, hop):
        return hop if dirn == 0 else nz - 1 + hop

    def y_link(dirn, hop, p):
        held = lat_at(source(dirn, hop), me_y, p)
        slot = y_slot(dirn, hop)
        return link(held, held, laty_s.at[slot, p], laty_r.at[slot, p], me_c, near)

    def relay(hop):
        for p in range(PARTS):
            for dirn in range(2):
                @pl.when(exists(dirn, hop))
                def _():
                    z = source(dirn, hop)
                    held = lat_at(z, me_y, p)
                    z_send(dirn, hop - 1, p, held, z).wait_recv()
                    if hop < nz - 1:
                        @pl.when(beyond(dirn))
                        def _():
                            z_send(dirn, hop, p, held, z).start()
                    y_link(dirn, hop, p).start()

    relay(1)
    for copy in m1:
        copy.wait_recv()
    summed_mod = part[me_c]
    for k in range(1, nc):
        summed_mod = summed_mod + part_in[c_from(k)]
    mine[...] = summed_mod
    mod_all[me_s] = summed_mod
    m2 = [
        remote(
            mine, mod_all.at[me_s], m2_s.at[k], m2_r.at[k], me_c, lax.rem(me_s + k, ns)
        )
        for k in range(1, ns)
    ]
    for hop in range(2, nz - 1):
        relay(hop)

    def cot_at(z, p):
        return cot_all.at[pl.ds(pl.multiple_of(z * rows + p * size, size), size)]

    def cot_send(dirn, hop, p, src, z):
        return link(
            src, cot_at(z, p), cot_s.at[dirn, hop, p], cot_r.at[dirn, hop, p],
            me_c, z_seq(me_z + 1 - 2 * dirn),
        )

    for p in range(PARTS):
        for dirn in range(2):
            @pl.when(beyond(dirn))
            def _():
                cot_send(dirn, 0, p, cot_ref.at[pl.ds(p * size, size)], me_z).start()

    def cot_relay(hop):
        for p in range(PARTS):
            for dirn in range(2):
                @pl.when(exists(dirn, hop))
                def _():
                    z = source(dirn, hop)
                    cot_send(dirn, hop - 1, p, cot_at(z, p), z).wait_recv()
                    if hop < nz - 1:
                        @pl.when(beyond(dirn))
                        def _():
                            cot_send(dirn, hop, p, cot_at(z, p), z).start()

    def gate_rows(z):
        def body(index, _):
            at = pl.ds(pl.multiple_of(z * rows + index * 16, 16), 16)
            gated = (cot_all[at].astype(f32) * vecs[2]).astype(bf16)
            for c in range(nc):
                x_cot[c, at] = gated[:, c * piece : (c + 1) * piece]
            return 0

        lax.fori_loop(0, rows // 16, body, 0)

    def gate_hop(hop):
        for dirn in range(2):
            @pl.when(exists(dirn, hop))
            def _():
                gate_rows(source(dirn, hop))

    for copy in m2:
        copy.wait_recv()
    for s in range(ns):
        at = s * cols
        while at < (s + 1) * cols:
            kind = at // width
            stop = min((s + 1) * cols, (kind + 1) * width)
            vecs[kind, :, at - kind * width : stop - kind * width] = mod_all[
                s, :, at - s * cols : stop - s * cols
            ]
            at = stop

    def norm_rows(at):
        normed, _inverse = layer_norm(lat_all[at].astype(f32))
        x_all[at] = (normed * (1.0 + vecs[1]) + vecs[0]).astype(bf16)

    def norm_run(start, count):
        def body(i, _):
            norm_rows(pl.ds(pl.multiple_of(start + i * 16, 16), 16))
            return 0

        lax.fori_loop(0, count // 16, body, 0)

    own[1].wait()
    norm_run(place(me_s) * rows, rows)
    for dirn in range(2):
        for hop in range(1, nz - 1):
            @pl.when(exists(dirn, hop))
            def _():
                norm_run((me_y * nz + source(dirn, hop)) * rows, rows)

    if nz > 1:
        relay(nz - 1)
        for dirn in range(2):
            @pl.when(exists(dirn, nz - 1))
            def _():
                norm_run((me_y * nz + source(dirn, nz - 1)) * rows, rows)

    w_out_near = [
        w_out_send(1, 0, q, w_out_own(q), me_y, me_c, me_c, near) for q in range(HALVES)
    ]

    w_in_second = []

    def slab_forward(q):
        for j in range(1, half):
            w_in_far[q][j - 1].wait_recv()
            held = w_in_at(c_from(2 * j), q)
            w_in_second.append(
                remote(held, held, wif_s.at[j, q], wif_r.at[j, q], mate, me_s)
            )

    for q in range(SLABS - 1):
        slab_forward(q)
    for copy in done:
        copy.wait_recv()
    norm_run(((1 - me_y) * nz + me_z) * rows, rows)
    for hop in range(1, nz):
        if hop == nz - 1:
            if nz > 2:
                cot_relay(1)
            slab_forward(SLABS - 1)
        for dirn in range(2):
            @pl.when(exists(dirn, hop))
            def _():
                for p in range(PARTS):
                    y_link(dirn, hop, p).wait_recv()
                norm_run(((1 - me_y) * nz + source(dirn, hop)) * rows, rows)
    w_in_mate.wait_recv()
    for copy in w_in_second:
        copy.wait_recv()

    def project(index, _):
        at = pl.ds(pl.multiple_of(index * tile, tile), tile)
        proj[index] = jnp.dot(x_all[...], w_in_all[:, at], preferred_element_type=f32)
        return 0

    lax.fori_loop(0, groups, project, 0)
    for hop in range(2, nz - 1):
        cot_relay(hop)

    def head_at(h):
        return pl.ds(h * HEAD, HEAD)

    def head_forward(h, _):
        query = proj[h, :, 0:HEAD]
        key = proj[h, :, HEAD : 2 * HEAD]
        query_inverse = inverse_rms(query)
        key_inverse = inverse_rms(key)
        query_n = query * query_inverse
        key_n = key * key_inverse
        proj[h, :, 0:HEAD] = query_n
        proj[h, :, HEAD : 2 * HEAD] = key_n
        inverse_all[2 * h] = jnp.broadcast_to(query_inverse, query.shape)
        inverse_all[2 * h + 1] = jnp.broadcast_to(key_inverse, key.shape)
        q_rot = (query_n * cos_ref[...] + swap_pairs(query_n) * sin_ref[...]).astype(bf16)
        k_rot = (key_n * cos_ref[...] + swap_pairs(key_n) * sin_ref[...]).astype(bf16)
        values = proj[h, :, 2 * HEAD :].astype(bf16)
        q_all[h] = q_rot
        k_all[h] = k_rot
        v_all[h] = values
        weights = jnp.exp(dot_nt(q_rot, k_rot) * score_scale - HEAD**0.5)
        share = weights * (1.0 / jnp.sum(weights, -1, keepdims=True))
        probs[h] = share
        att[:, head_at(h)] = jnp.dot(
            share.astype(bf16), values, preferred_element_type=f32
        ).astype(bf16)
        return 0

    for h in range(groups):
        head_forward(h, 0)
    att_move = remote(
        att.at[rows_of(1 - me_y, run)], att_near, ex_s.at[0], ex_r.at[0], me_c, near
    )

    def att_rows(which):
        return att[rows_of(me_y, run)] if which == 0 else att_near[...]

    mixed = []

    def mix_chip(j):
        first = 2 * lax.rem(lax.div(me_c, 2) + j, half)
        for b in range(2):
            mix_out[first + b] = (
                jnp.dot(att_rows(0), w_out_all[me_y, first + b], preferred_element_type=f32)
                + jnp.dot(att_rows(1), w_out_all[1 - me_y, first + b], preferred_element_type=f32)
            ).astype(bf16)
        for k in range(1, nz):
            peer = lax.rem(me_z + k, nz)
            mixed.append(
                remote(
                    mix_out.at[pl.ds(first, 2), rows_of(peer, rows)],
                    mix_in.at[me_z, pl.ds(first, 2)],
                    mx_s.at[k, j], mx_r.at[k, j], me_c, z_seq(peer),
                )
            )

    w_out_second = []
    w_out_cross = []
    w_out_near_mate = []
    for q in range(HALVES):
        w_out_near[q].wait_recv()
        w_out_near_mate.append(
            w_out_send(2, 0, q, w_out_at(1 - me_y, me_c, q), 1 - me_y, me_c, mate, me_s)
        )
        for j in range(1, half):
            w_out_far[q][j - 1].wait_recv()
            from_y = jnp.where(core == 0, me_y, 1 - me_y)
            from_c = jnp.where(core == 0, c_from(2 * j), me_c)
            w_out_cross.append(
                w_out_send(
                    3, j, q, w_out_at(from_y, from_c, q), from_y, from_c,
                    jnp.where(core == 0, me_c, c_peer(2 * j)), jnp.where(core == 0, near, me_s),
                )
            )
            w_out_second.append(
                w_out_send(
                    2, j, q, w_out_at(me_y, c_from(2 * j), q), me_y, c_from(2 * j), mate, me_s
                )
            )

    own[4].wait()
    for copy in w_out_mate + [att_move] + w_out_near_mate:
        copy.wait_recv()
    mix_chip(0)

    own[2].wait()
    gate_rows(me_z)
    for hop in range(1, nz - 1):
        gate_hop(hop)
    cot_relay(nz - 1)
    gate_hop(nz - 1)

    def d_attended(y, first, count):
        block = jnp.zeros((run, groups * HEAD), f32)
        for i in range(count):
            c = first + i
            block = block + dot_nt(x_cot[c], w_out_all[y, c])
        return block

    chip = 2 * lax.div(me_c, 2)
    away_sum = d_attended(1 - me_y, chip, 2)
    for q in range(HALVES):
        for j in range(1, half):
            held = w_out_at(1 - me_y, c_from(2 * j), q)
            link(held, held, wo_s.at[3, j, q], wo_r.at[3, j, q], me_c, near).wait_recv()
            w_out_second.append(
                w_out_send(4, j, q, held, 1 - me_y, c_from(2 * j), mate, me_s)
            )
    for copy in w_out_second:
        copy.wait_recv()
    for j in range(1, half):
        away_sum = away_sum + d_attended(1 - me_y, 2 * lax.rem(lax.div(me_c, 2) + j, half), 2)
    d_away[...] = away_sum.astype(bf16)
    d_move = [
        remote(
            d_away.at[:, head_at(h)], d_att.at[rows_of(me_y, run), head_at(h)],
            ex_s.at[1 + h], ex_r.at[1 + h], me_c, near,
        )
        for h in range(groups)
    ]
    d_att[rows_of(me_y, run)] = d_attended(me_y, 0, nc).astype(bf16)
    for j in range(1, half):
        mix_chip(j)

    def back_norm(d_rot, normed, inverse, cos, sin):
        d_normed = d_rot * cos - swap_pairs(d_rot) * sin
        return inverse * (d_normed - normed * jnp.mean(d_normed * normed, -1, keepdims=True))

    def query_part(h, y):
        at = rows_of(y, run)
        d_heads = d_att[at, head_at(h)]
        share = probs[h, at]
        d_values = dot_tn(share.astype(bf16), d_heads)
        d_probs = dot_nt(d_heads, v_all[h])
        d_scores = (share * (d_probs - jnp.sum(share * d_probs, -1, keepdims=True))).astype(bf16)
        d_qrot = jnp.dot(d_scores, k_all[h], preferred_element_type=f32) * score_scale
        d_krot = dot_tn(d_scores, q_all[h, at])
        d_query = back_norm(
            d_qrot, proj[h, at, 0:HEAD], inverse_all[2 * h, at], cos_ref[at], sin_ref[at]
        )
        d_proj[at, head_at(3 * h)] = d_query.astype(bf16)
        return d_values, d_krot

    def first_half(h, _):
        d_values, d_krot = query_part(h, me_y)
        value_sum[h] = d_values
        key_sum[h] = d_krot
        return 0

    for h in range(groups):
        first_half(h, 0)

    def second_half(h, _):
        d_values, d_krot = query_part(h, 1 - me_y)
        d_key = back_norm(
            (key_sum[h] + d_krot) * score_scale, proj[h, :, HEAD : 2 * HEAD],
            inverse_all[2 * h + 1], cos_ref[...], sin_ref[...],
        )
        d_proj[:, head_at(3 * h + 1)] = d_key.astype(bf16)
        d_proj[:, head_at(3 * h + 2)] = (value_sum[h] + d_values).astype(bf16)
        return 0

    for h in range(groups):
        d_move[h].wait_recv()
        second_half(h, 0)

    order = []
    low, high = 0, nz - 1
    for i in range(nz):
        take = (me_z - low >= high - me_z).astype(jnp.int32)
        order.append(take * low + (1 - take) * high)
        low, high = low + take, high - (1 - take)

    d_near = [[] for _ in range(nz)]

    def away(i, j):
        if i < nz - 1:
            at = (rows_of(order[i], rows), pl.ds(j * chunk, chunk))
        else:
            at = pl.ds(pl.multiple_of(me_z * rows + j * 16, 16), 16)
        d_near[i].append(
            remote(dm_away.at[at], dm_near.at[at], dmn_s.at[i, j], dmn_r.at[i, j], me_c, near)
        )

    for j in range(CHUNKS):
        part_cols = slice(j * chunk, (j + 1) * chunk)
        dm_away[:, part_cols] = dot_nt(
            d_proj[rows_of(1 - me_y, run)], w_in_all[part_cols]
        ).astype(bf16)
        away(0, j)
    for i in range(1, nz):
        for j in range(CHUNKS if i < nz - 1 else rows // 16):
            away(i, j)
    for j in range(CHUNKS):
        part_cols = slice(j * chunk, (j + 1) * chunk)
        dm_here[:, part_cols] = dot_nt(
            d_proj[rows_of(me_y, run)], w_in_all[part_cols]
        ).astype(bf16)

    def lat_rows(start):
        return lat_all[pl.ds(pl.multiple_of(place(me_s) * rows + start, 16), 16)].astype(f32)

    for start in range(0, rows, 16):
        normed, inverse_std = layer_norm(lat_rows(start))
        normed_own[start : start + 16] = normed
        inverse_own[start : start + 16] = jnp.broadcast_to(inverse_std, (16, HEAD))

    chain = []
    for i in range(nz - 1):
        to = order[i]
        up = to > me_z
        dirn = 1 - up.astype(jnp.int32)
        fed = (up & (me_z > 0)) | (~up & (me_z < nz - 1))
        beside = z_seq(me_z + 1 - 2 * dirn)
        for j in range(CHUNKS):
            at = (rows_of(to, rows), pl.ds(j * chunk, chunk))
            d_near[i][j].wait_recv()
            hop = link(
                dm_sum.at[at], chain_in.at[(dirn,) + at], ch_s.at[dirn, to, j],
                ch_r.at[dirn, to, j], me_c, beside,
            )
            value = dm_here[at].astype(f32) + dm_near[at].astype(f32)

            @pl.when(fed)
            def _():
                hop.wait_recv()
                dm_sum[at] = (value + chain_in[(dirn,) + at].astype(f32)).astype(bf16)

            @pl.when(~fed)
            def _():
                dm_sum[at] = value.astype(bf16)

            hop.start()
            chain.append(hop)

    for copy in mixed:
        copy.wait_recv()
    leave = []
    for start in range(0, rows, 16):
        mine_at = pl.ds(pl.multiple_of(me_z * rows + start, 16), 16)
        latent_rows = lat_rows(start)
        for c in range(nc):
            value = mix_out[c, mine_at].astype(f32)
            for k in range(1, nz):
                value = value + mix_in[lax.rem(me_z + k, nz), c, start : start + 16].astype(f32)
            part_cols = slice(c * piece, (c + 1) * piece)
            block_own[start : start + 16, part_cols] = (
                latent_rows[:, part_cols] + vecs[2, :, part_cols] * value
            ).astype(bf16)
    leave.append(pltpu.make_async_copy(block_own, block_ref, out_sem.at[0]))
    leave[0].start()

    total[...] = dm_here[rows_of(me_z, rows)].astype(f32)
    for dirn, fed in ((0, me_z > 0), (1, me_z < nz - 1)):
        @pl.when(fed)
        def _():
            for j in range(CHUNKS):
                part_cols = pl.ds(j * chunk, chunk)
                landed = chain_in.at[dirn, rows_of(me_z, rows), part_cols]
                link(
                    landed, landed, ch_s.at[dirn, me_z, j], ch_r.at[dirn, me_z, j], me_c, near
                ).wait_recv()
                total[:, part_cols] += landed[...].astype(f32)

    for j in range(rows // 16):
        at = slice(16 * j, 16 * j + 16)
        mine_at = pl.ds(pl.multiple_of(me_z * rows + 16 * j, 16), 16)
        d_near[nz - 1][j].wait_recv()
        d_normed = (total[at] + dm_near[mine_at].astype(f32)) * (1.0 + vecs[1])
        normed = normed_own[at]
        grad_own[at] = cot_all[mine_at].astype(f32) + inverse_own[at, 0:1] * (
            d_normed
            - jnp.mean(d_normed, -1, keepdims=True)
            - normed * jnp.mean(d_normed * normed, -1, keepdims=True)
        )
        leave.append(
            pltpu.make_async_copy(grad_own.at[at], grad_ref.at[at], out_sem.at[1 + j])
        )
        leave[-1].start()

    for p in range(PARTS):
        for dirn in range(2):
            for hop in range(nz - 1):
                @pl.when(exists(dirn, hop) & beyond(dirn))
                def _():
                    held = lat_at(source(dirn, hop), me_y, p)
                    z_send(dirn, hop, p, held, source(dirn, hop)).wait_send()
                    held = cot_at(source(dirn, hop), p)
                    cot_send(dirn, hop, p, held, source(dirn, hop)).wait_send()
            for hop in range(1, nz):
                @pl.when(exists(dirn, hop))
                def _():
                    y_link(dirn, hop, p).wait_send()
    for copy in (
        done + m1 + m2 + sum(w_in_far, []) + [w_in_mate] + w_in_second + sum(w_out_far, [])
        + w_out_mate + w_out_near + w_out_near_mate + w_out_second + w_out_cross
        + [att_move] + d_move + mixed + sum(d_near, []) + chain
    ):
        copy.wait_send()
    for copy in leave:
        copy.wait()


def hand_over(block_ref, grad_ref, block_out, grad_out, sems):
    copies = [
        pltpu.make_async_copy(block_ref, block_out, sems.at[0]),
        pltpu.make_async_copy(grad_ref, grad_out, sems.at[1]),
    ]
    for copy in copies:
        copy.start()
    for copy in copies:
        copy.wait()


def on_device(latent, timesteps, positions, mod_weight, input_weight, output_weight, cotangent):
    nc = lax.axis_size("cand")
    ns = lax.axis_size("seq")
    rows, width = latent.shape[1:]
    length = rows * ns
    slab = input_weight.shape[0]
    groups = input_weight.shape[1]
    cols = mod_weight.shape[1]
    piece = output_weight.shape[2]
    half = nc // 2
    nz = ns // 2
    run = nz * rows
    vmem = pl.BlockSpec(memory_space=pltpu.VMEM)
    smem = pl.BlockSpec(memory_space=pltpu.SMEM)
    anywhere = pl.BlockSpec(memory_space=pl.ANY)
    f32, bf16 = jnp.float32, jnp.bfloat16
    dma = pltpu.SemaphoreType.DMA
    block_out, latent_grad = pl.pallas_call(
        functools.partial(step_kernel, nc, ns),
        out_shape=(pltpu.VMEM((rows, width), bf16), pltpu.VMEM((rows, width), f32)),
        in_specs=[smem, vmem] + [anywhere] * 5,
        out_specs=(anywhere, anywhere),
        scratch_shapes=[
            pltpu.VMEM(input_weight.shape, bf16),
            pltpu.VMEM(mod_weight.shape, bf16),
            pltpu.VMEM((8, length), f32),
            pltpu.VMEM((length, HEAD), f32),
            pltpu.VMEM((length, HEAD), f32),
            pltpu.VMEM((length, HEAD), f32),
            pltpu.VMEM((nc, 1, cols), f32),
            pltpu.VMEM((nc, 1, cols), f32),
            pltpu.VMEM((1, cols), f32),
            pltpu.VMEM((ns, 1, cols), f32),
            pltpu.VMEM((3, 1, width), f32),
            pltpu.VMEM((length, width), bf16),
            pltpu.VMEM((length, width), bf16),
            pltpu.VMEM((slab * nc, groups * 3 * HEAD), bf16),
            pltpu.VMEM((2, nc, groups * HEAD, piece), bf16),
            pltpu.VMEM((run, width), bf16),
            pltpu.VMEM((nc, run, piece), bf16),
            pltpu.VMEM((groups, length, 3 * HEAD), f32),
            pltpu.VMEM((2 * groups, length, HEAD), f32),
            pltpu.VMEM((groups, length, HEAD), bf16),
            pltpu.VMEM((groups, length, HEAD), bf16),
            pltpu.VMEM((groups, length, HEAD), bf16),
            pltpu.VMEM((groups, length, length), f32),
            pltpu.VMEM((length, groups * HEAD), bf16),
            pltpu.VMEM((run, groups * HEAD), bf16),
            pltpu.VMEM((length, groups * HEAD), bf16),
            pltpu.VMEM((run, groups * HEAD), bf16),
            pltpu.VMEM((length, groups * 3 * HEAD), bf16),
            pltpu.VMEM((groups, length, HEAD), f32),
            pltpu.VMEM((groups, length, HEAD), f32),
            pltpu.VMEM((nc, run, piece), bf16),
            pltpu.VMEM((nz, nc, rows, piece), bf16),
            pltpu.VMEM((run, width), bf16),
            pltpu.VMEM((run, width), bf16),
            pltpu.VMEM((run, width), bf16),
            pltpu.VMEM((run, width), bf16),
            pltpu.VMEM((2, run, width), bf16),
            pltpu.VMEM((rows, width), f32),
            pltpu.VMEM((rows, width), f32),
            pltpu.VMEM((rows, HEAD), f32),
            pltpu.VMEM((rows, width), bf16),
            pltpu.VMEM((rows, width), f32),
            dma((1 + rows // 16,)),
            dma((5,)),
            dma((2, nz, PARTS)), dma((2, nz, PARTS)),
            dma((2 * nz, PARTS)), dma((2 * nz, PARTS)),
            dma((half, SLABS)), dma((half, SLABS)), dma((half, SLABS)), dma((half, SLABS)),
            dma((5, half, HALVES)), dma((5, half, HALVES)), dma((nc,)), dma((nc,)), dma((ns,)), dma((ns,)),
            dma((2, nz, PARTS)), dma((2, nz, PARTS)), dma((1 + groups,)), dma((1 + groups,)), dma((nz, half)), dma((nz, half)),
            dma((nz, max(CHUNKS, rows // 16))), dma((nz, max(CHUNKS, rows // 16))), dma((2, nz, CHUNKS)), dma((2, nz, CHUNKS)),
        ],
        compiler_params=pltpu.CompilerParams(
            collective_id=0, has_side_effects=True, vmem_limit_bytes=60000000
        ),
    )(
        timesteps, positions, mod_weight, latent[0], cotangent[0],
        input_weight,
        output_weight.reshape(groups * HEAD, piece),
    )
    block_out, latent_grad = pl.pallas_call(
        hand_over,
        out_shape=(
            jax.ShapeDtypeStruct((rows, width), bf16),
            jax.ShapeDtypeStruct((rows, width), f32),
        ),
        in_specs=[anywhere] * 2,
        out_specs=(anywhere, anywhere),
        scratch_shapes=[dma((2,))],
        compiler_params=pltpu.CompilerParams(vmem_limit_bytes=1000000),
    )(block_out, latent_grad)
    return (block_out[None], latent_grad[None])


def solution(mesh):
    placed = (
        P("cand", "seq", None),
        P(),
        P(),
        P("cand", "seq"),
        P("cand", "seq", None),
        P("seq", None, "cand"),
        P("cand", "seq", None),
    )
    return jax.shard_map(
        on_device,
        mesh=mesh,
        in_specs=placed,
        out_specs=(P("cand", "seq", None), P("cand", "seq", None)),
        check_vma=False,
    )
```

```python
import functools
import math

import jax
import jax.numpy as jnp
from jax import lax
from jax.experimental import pallas as pl
from jax.experimental.pallas import tpu as pltpu
from jax.sharding import PartitionSpec as P

HEAD = 128
CHUNKS = 4
PARTS = 3
SLABS = 6
HALVES = 2
MESH = pl.DeviceIdType.MESH


epsilon = 1e-06


def swap_pairs(values):
    lane = lax.broadcasted_iota(jnp.int32, values.shape, 1)
    small = HEAD // 8
    large = (HEAD - small) // 2
    near = jnp.where(
        lane < small // 2,
        pltpu.roll(values, HEAD - small // 2, 1),
        pltpu.roll(values, small // 2, 1),
    )
    upper = ((lane >= small) & (lane < small + large // 2)) | (
        (lane >= small + large) & (lane < small + large + large // 2)
    )
    far = jnp.where(
        upper, pltpu.roll(values, HEAD - large // 2, 1), pltpu.roll(values, large // 2, 1)
    )
    return jnp.where(lane < small, near, far)


def dot_nt(left, right):
    return lax.dot_general(left, right, (((1,), (1,)), ((), ())), preferred_element_type=jnp.float32)


def dot_tn(left, right):
    return lax.dot_general(left, right, (((0,), (0,)), ((), ())), preferred_element_type=jnp.float32)


def inverse_rms(values):
    return lax.rsqrt(jnp.mean(values * values, -1, keepdims=True) + epsilon)


def layer_norm(values):
    centred = values - jnp.mean(values, -1, keepdims=True)
    inverse_std = lax.rsqrt(jnp.mean(centred * centred, -1, keepdims=True) + epsilon)
    return (centred * inverse_std, inverse_std)


def sections():
    first = HEAD // 8
    other = (HEAD - first) // 2
    return ((0, first), (first, other), (first + other, other))


def step_kernel(
    nc, ns,
    time_ref, pos_ref, mod_w_ref, latent_ref, cot_ref, w_in_ref, w_out_ref,
    block_ref, grad_ref,
    w_raw, mod_w, pos8, angle, cos_ref, sin_ref, part, part_in, mine, mod_all, vecs,
    lat_all, x_all, w_in_all, w_out_all, cot_all, x_cot, proj, inverse_all, q_all, k_all, v_all, probs,
    att, att_near, d_att, d_away, d_proj, key_sum, value_sum, mix_out, mix_in,
    dm_away, dm_here, dm_near, dm_sum, chain_in, total, normed_own, inverse_own, block_own, grad_own,
    out_sem, own_sem, lat_s, lat_r, laty_s, laty_r, wi_s, wi_r, wif_s, wif_r, wo_s, wo_r, m1_s, m1_r,
    m2_s, m2_r, cot_s, cot_r, ex_s, ex_r, mx_s, mx_r, dmn_s, dmn_r, ch_s, ch_r,
):
    me_c = lax.axis_index("cand")
    me_s = lax.axis_index("seq")
    rows, width = latent_ref.shape
    length = rows * ns
    slab = w_in_ref.shape[0]
    groups = q_all.shape[0]
    cols = mod_w_ref.shape[1]
    piece = w_out_ref.shape[1]
    chunk = width // CHUNKS
    half = nc // 2
    core = lax.rem(me_c, 2)
    mate = me_c + 1 - 2 * core
    nz = ns // 2
    me_y, me_z = lax.rem(me_s, 2), lax.div(me_s, 2)
    near = me_s + 1 - 2 * me_y
    score_scale = HEAD ** (-0.5)
    size = rows // PARTS
    span = slab // SLABS
    run = nz * rows
    f32, bf16 = jnp.float32, jnp.bfloat16

    def place(index):
        return lax.rem(index, 2) * nz + lax.div(index, 2)

    def rows_of(index, count):
        return pl.ds(pl.multiple_of(index * count, count), count)

    def link(src, dst, send, recv, cand, seq):
        return pltpu.make_async_remote_copy(
            src_ref=src, dst_ref=dst, send_sem=send, recv_sem=recv,
            device_id=(cand, seq), device_id_type=MESH,
        )

    def remote(*args):
        copy = link(*args)
        copy.start()
        return copy

    def c_peer(k):
        return lax.rem(me_c + k, nc)

    def c_from(k):
        return lax.rem(me_c - k + nc, nc)

    def z_seq(z):
        return 2 * z + me_y

    barrier = pltpu.get_barrier_semaphore()
    for k in range(1, nc):
        pl.semaphore_signal(barrier, inc=1, device_id=(c_peer(k), me_s), device_id_type=MESH)
    for k in range(1, ns):
        pl.semaphore_signal(
            barrier, inc=1, device_id=(me_c, lax.rem(me_s + k, ns)), device_id_type=MESH
        )

    def w_in_at(index, q):
        return w_in_all.at[pl.ds(pl.multiple_of(index * slab + q * span, span), span)]

    own = [
        pltpu.make_async_copy(mod_w_ref, mod_w, own_sem.at[0]),
        pltpu.make_async_copy(latent_ref, lat_all.at[rows_of(place(me_s), rows)], own_sem.at[1]),
        pltpu.make_async_copy(cot_ref, cot_all.at[rows_of(me_z, rows)], own_sem.at[2]),
        pltpu.make_async_copy(w_in_ref, w_raw, own_sem.at[3]),
        pltpu.make_async_copy(w_out_ref, w_out_all.at[me_y, me_c], own_sem.at[4]),
    ]
    for copy in own:
        copy.start()
    tile = 3 * HEAD

    def flatten(i, _):
        at = pl.ds(pl.multiple_of(me_c * slab + i * 16, 16), 16)
        for h in range(groups):
            w_in_all[at, h * tile : (h + 1) * tile] = w_raw[
                pl.ds(pl.multiple_of(i * 16, 16), 16), h
            ]
        return 0

    def flatten_part(q):
        lax.fori_loop(q * span // 16, (q + 1) * span // 16, flatten, 0)

    own[3].wait()
    flatten_part(0)
    pl.semaphore_wait(barrier, nc - 1 + ns - 1)

    def lat_at(z, y, p):
        return lat_all.at[pl.ds(pl.multiple_of((y * nz + z) * rows + p * size, size), size)]

    done = []

    def z_send(dirn, hop, p, src, z):
        to = me_z + 1 - 2 * dirn
        return link(
            src, lat_at(z, me_y, p), lat_s.at[dirn, hop, p], lat_r.at[dirn, hop, p],
            me_c, z_seq(to),
        )

    for p in range(PARTS):
        src = latent_ref.at[pl.ds(p * size, size)]
        for dirn, there in ((0, me_z < nz - 1), (1, me_z > 0)):
            @pl.when(there)
            def _():
                z_send(dirn, 0, p, src, me_z).start()
        done.append(
            remote(src, lat_at(me_z, me_y, p), laty_s.at[0, p], laty_r.at[0, p], me_c, near)
        )

    def slab_part(q):
        src = w_in_at(me_c, q)
        return [
            remote(src, w_in_at(me_c, q), wi_s.at[j, q], wi_r.at[j, q], c_peer(2 * j), me_s)
            for j in range(1, half)
        ]

    w_in_far = [slab_part(0)]

    count = part.shape[0]
    lead = mod_w_ref.shape[0]
    held_rows = max(16, nc)
    index = me_c * lead + lax.broadcasted_iota(jnp.int32, (held_rows, lead), 1)
    steps = width // 2
    is_cos = index < steps
    order = jnp.where(is_cos, index, index - steps).astype(f32)
    row = lax.broadcasted_iota(jnp.int32, (held_rows, 1), 0)
    times = jnp.zeros((held_rows, 1), f32)
    for c in range(nc):
        times = jnp.where(row == c, time_ref[c].astype(f32), times)
    turns = times * jnp.exp(order * (-math.log(10000.0)) / steps)
    wave = jnp.where(is_cos, jnp.cos(turns), jnp.sin(turns))
    act = (wave / (1.0 + jnp.exp(-wave))).astype(bf16)
    own[0].wait()
    product = jnp.dot(act, mod_w[...], preferred_element_type=f32)
    for c in range(count):
        part[c] = product[c : c + 1]
    m1 = []
    for k in range(1, nc):
        peer = c_peer(k)
        m1.append(remote(part.at[peer], part_in.at[me_c], m1_s.at[k], m1_r.at[k], peer, me_s))
    for q in range(1, SLABS):
        flatten_part(q)
        w_in_far.append(slab_part(q))
    w_in_mate = remote(
        w_in_all.at[rows_of(me_c, slab)], w_in_all.at[rows_of(me_c, slab)], wif_s.at[0, 0],
        wif_r.at[0, 0], mate, me_s
    )

    part_rows = w_out_ref.shape[0] // HALVES

    def w_out_at(y, c, q):
        return w_out_all.at[y, c, pl.ds(q * part_rows, part_rows)]

    def w_out_send(kind, j, q, src, y, c, cand, seq):
        return remote(
            src, w_out_at(y, c, q), wo_s.at[kind, j, q], wo_r.at[kind, j, q], cand, seq
        )

    def w_out_own(q):
        return w_out_ref.at[pl.ds(q * part_rows, part_rows)]

    w_out_far = [
        [
            w_out_send(0, j, q, w_out_own(q), me_y, me_c, c_peer(2 * j), me_s)
            for j in range(1, half)
        ]
        for q in range(HALVES)
    ]
    w_out_mate = [
        w_out_send(0, 0, q, w_out_own(q), me_y, me_c, mate, me_s) for q in range(HALVES)
    ]

    pos8[...] = jnp.zeros_like(pos8)
    pos8[0 : pos_ref.shape[0]] = pos_ref[...].astype(f32)
    lane = lax.broadcasted_iota(jnp.int32, (8, HEAD), 1)
    axis = lax.broadcasted_iota(jnp.int32, (8, HEAD), 0)
    rate = jnp.zeros((8, HEAD), f32)
    sign = jnp.ones((8, HEAD), f32)
    for a, (start, extent) in enumerate(sections()):
        inside = (lane >= start) & (lane < start + extent)
        late = inside & (lane >= start + extent // 2)
        pair = jnp.where(late, lane - start - extent // 2, lane - start).astype(f32)
        value = jnp.exp(pair * (-math.log(256.0) * 2.0 / extent))
        rate = jnp.where(inside & (axis == a), value, rate)
        sign = jnp.where(inside & ~late, -1.0, sign)
    angle[...] = lax.dot_general(
        pos8[...], rate, (((0,), (0,)), ((), ())), preferred_element_type=f32,
        precision=lax.Precision.HIGHEST,
    )

    def turn_rows(s, _):
        turned = angle[rows_of(s, rows)]
        at = rows_of(place(s), rows)
        cos_ref[at] = jnp.cos(turned)
        sin_ref[at] = jnp.sin(turned) * sign[0:1]
        return 0

    lax.fori_loop(0, ns, turn_rows, 0)

    def exists(dirn, hop):
        return me_z >= hop if dirn == 0 else me_z <= nz - 1 - hop

    def beyond(dirn):
        return me_z < nz - 1 if dirn == 0 else me_z > 0

    def source(dirn, hop):
        return me_z - hop if dirn == 0 else me_z + hop

    def y_slot(dirn, hop):
        return hop if dirn == 0 else nz - 1 + hop

    def y_link(dirn, hop, p):
        held = lat_at(source(dirn, hop), me_y, p)
        slot = y_slot(dirn, hop)
        return link(held, held, laty_s.at[slot, p], laty_r.at[slot, p], me_c, near)

    def relay(hop):
        for p in range(PARTS):
            for dirn in range(2):
                @pl.when(exists(dirn, hop))
                def _():
                    z = source(dirn, hop)
                    held = lat_at(z, me_y, p)
                    z_send(dirn, hop - 1, p, held, z).wait_recv()
                    if hop < nz - 1:
                        @pl.when(beyond(dirn))
                        def _():
                            z_send(dirn, hop, p, held, z).start()
                    y_link(dirn, hop, p).start()

    relay(1)
    for copy in m1:
        copy.wait_recv()
    summed_mod = part[me_c]
    for k in range(1, nc):
        summed_mod = summed_mod + part_in[c_from(k)]
    mine[...] = summed_mod
    mod_all[me_s] = summed_mod
    m2 = [
        remote(
            mine, mod_all.at[me_s], m2_s.at[k], m2_r.at[k], me_c, lax.rem(me_s + k, ns)
        )
        for k in range(1, ns)
    ]
    for hop in range(2, nz - 1):
        relay(hop)

    def cot_at(z, p):
        return cot_all.at[pl.ds(pl.multiple_of(z * rows + p * size, size), size)]

    def cot_send(dirn, hop, p, src, z):
        return link(
            src, cot_at(z, p), cot_s.at[dirn, hop, p], cot_r.at[dirn, hop, p],
            me_c, z_seq(me_z + 1 - 2 * dirn),
        )

    for p in range(PARTS):
        for dirn in range(2):
            @pl.when(beyond(dirn))
            def _():
                cot_send(dirn, 0, p, cot_ref.at[pl.ds(p * size, size)], me_z).start()

    def cot_relay(hop):
        for p in range(PARTS):
            for dirn in range(2):
                @pl.when(exists(dirn, hop))
                def _():
                    z = source(dirn, hop)
                    cot_send(dirn, hop - 1, p, cot_at(z, p), z).wait_recv()
                    if hop < nz - 1:
                        @pl.when(beyond(dirn))
                        def _():
                            cot_send(dirn, hop, p, cot_at(z, p), z).start()

    def gate_rows(z):
        def body(index, _):
            at = pl.ds(pl.multiple_of(z * rows + index * 16, 16), 16)
            gated = (cot_all[at].astype(f32) * vecs[2]).astype(bf16)
            for c in range(nc):
                x_cot[c, at] = gated[:, c * piece : (c + 1) * piece]
            return 0

        lax.fori_loop(0, rows // 16, body, 0)

    def gate_hop(hop):
        for dirn in range(2):
            @pl.when(exists(dirn, hop))
            def _():
                gate_rows(source(dirn, hop))

    for copy in m2:
        copy.wait_recv()
    for s in range(ns):
        at = s * cols
        while at < (s + 1) * cols:
            kind = at // width
            stop = min((s + 1) * cols, (kind + 1) * width)
            vecs[kind, :, at - kind * width : stop - kind * width] = mod_all[
                s, :, at - s * cols : stop - s * cols
            ]
            at = stop

    def norm_rows(at):
        normed, _inverse = layer_norm(lat_all[at].astype(f32))
        x_all[at] = (normed * (1.0 + vecs[1]) + vecs[0]).astype(bf16)

    def norm_run(start, count):
        def body(i, _):
            norm_rows(pl.ds(pl.multiple_of(start + i * 16, 16), 16))
            return 0

        lax.fori_loop(0, count // 16, body, 0)

    own[1].wait()
    norm_run(place(me_s) * rows, rows)
    for dirn in range(2):
        for hop in range(1, nz - 1):
            @pl.when(exists(dirn, hop))
            def _():
                norm_run((me_y * nz + source(dirn, hop)) * rows, rows)

    if nz > 1:
        relay(nz - 1)
        for dirn in range(2):
            @pl.when(exists(dirn, nz - 1))
            def _():
                norm_run((me_y * nz + source(dirn, nz - 1)) * rows, rows)

    w_out_near = [
        w_out_send(1, 0, q, w_out_own(q), me_y, me_c, me_c, near) for q in range(HALVES)
    ]

    w_in_second = []

    def slab_forward(q):
        for j in range(1, half):
            w_in_far[q][j - 1].wait_recv()
            held = w_in_at(c_from(2 * j), q)
            w_in_second.append(
                remote(held, held, wif_s.at[j, q], wif_r.at[j, q], mate, me_s)
            )

    for q in range(SLABS - 1):
        slab_forward(q)
    for copy in done:
        copy.wait_recv()
    norm_run(((1 - me_y) * nz + me_z) * rows, rows)
    for hop in range(1, nz):
        if hop == nz - 1:
            if nz > 2:
                cot_relay(1)
            slab_forward(SLABS - 1)
        for dirn in range(2):
            @pl.when(exists(dirn, hop))
            def _():
                for p in range(PARTS):
                    y_link(dirn, hop, p).wait_recv()
                norm_run(((1 - me_y) * nz + source(dirn, hop)) * rows, rows)
    w_in_mate.wait_recv()
    for copy in w_in_second:
        copy.wait_recv()

    def project(index, _):
        at = pl.ds(pl.multiple_of(index * tile, tile), tile)
        proj[index] = jnp.dot(x_all[...], w_in_all[:, at], preferred_element_type=f32)
        return 0

    lax.fori_loop(0, groups, project, 0)
    for hop in range(2, nz - 1):
        cot_relay(hop)

    def head_at(h):
        return pl.ds(h * HEAD, HEAD)

    def head_forward(h, _):
        query = proj[h, :, 0:HEAD]
        key = proj[h, :, HEAD : 2 * HEAD]
        query_inverse = inverse_rms(query)
        key_inverse = inverse_rms(key)
        query_n = query * query_inverse
        key_n = key * key_inverse
        proj[h, :, 0:HEAD] = query_n
        proj[h, :, HEAD : 2 * HEAD] = key_n
        inverse_all[2 * h] = jnp.broadcast_to(query_inverse, query.shape)
        inverse_all[2 * h + 1] = jnp.broadcast_to(key_inverse, key.shape)
        q_rot = (query_n * cos_ref[...] + swap_pairs(query_n) * sin_ref[...]).astype(bf16)
        k_rot = (key_n * cos_ref[...] + swap_pairs(key_n) * sin_ref[...]).astype(bf16)
        values = proj[h, :, 2 * HEAD :].astype(bf16)
        q_all[h] = q_rot
        k_all[h] = k_rot
        v_all[h] = values
        weights = jnp.exp(dot_nt(q_rot, k_rot) * score_scale - HEAD**0.5)
        share = weights * (1.0 / jnp.sum(weights, -1, keepdims=True))
        probs[h] = share
        att[:, head_at(h)] = jnp.dot(
            share.astype(bf16), values, preferred_element_type=f32
        ).astype(bf16)
        return 0

    for h in range(groups):
        head_forward(h, 0)
    att_move = remote(
        att.at[rows_of(1 - me_y, run)], att_near, ex_s.at[0], ex_r.at[0], me_c, near
    )

    def att_rows(which):
        return att[rows_of(me_y, run)] if which == 0 else att_near[...]

    mixed = []

    def mix_chip(j):
        first = 2 * lax.rem(lax.div(me_c, 2) + j, half)
        for b in range(2):
            mix_out[first + b] = (
                jnp.dot(att_rows(0), w_out_all[me_y, first + b], preferred_element_type=f32)
                + jnp.dot(att_rows(1), w_out_all[1 - me_y, first + b], preferred_element_type=f32)
            ).astype(bf16)
        for k in range(1, nz):
            peer = lax.rem(me_z + k, nz)
            mixed.append(
                remote(
                    mix_out.at[pl.ds(first, 2), rows_of(peer, rows)],
                    mix_in.at[me_z, pl.ds(first, 2)],
                    mx_s.at[k, j], mx_r.at[k, j], me_c, z_seq(peer),
                )
            )

    w_out_second = []
    w_out_cross = []
    w_out_near_mate = []
    for q in range(HALVES):
        w_out_near[q].wait_recv()
        w_out_near_mate.append(
            w_out_send(2, 0, q, w_out_at(1 - me_y, me_c, q), 1 - me_y, me_c, mate, me_s)
        )
        for j in range(1, half):
            w_out_far[q][j - 1].wait_recv()
            from_y = jnp.where(core == 0, me_y, 1 - me_y)
            from_c = jnp.where(core == 0, c_from(2 * j), me_c)
            w_out_cross.append(
                w_out_send(
                    3, j, q, w_out_at(from_y, from_c, q), from_y, from_c,
                    jnp.where(core == 0, me_c, c_peer(2 * j)), jnp.where(core == 0, near, me_s),
                )
            )
            w_out_second.append(
                w_out_send(
                    2, j, q, w_out_at(me_y, c_from(2 * j), q), me_y, c_from(2 * j), mate, me_s
                )
            )

    own[4].wait()
    for copy in w_out_mate + [att_move] + w_out_near_mate:
        copy.wait_recv()
    mix_chip(0)

    own[2].wait()
    gate_rows(me_z)
    for hop in range(1, nz - 1):
        gate_hop(hop)
    cot_relay(nz - 1)
    gate_hop(nz - 1)

    def d_attended(y, first, count):
        block = jnp.zeros((run, groups * HEAD), f32)
        for i in range(count):
            c = first + i
            block = block + dot_nt(x_cot[c], w_out_all[y, c])
        return block

    chip = 2 * lax.div(me_c, 2)
    away_sum = d_attended(1 - me_y, chip, 2)
    for q in range(HALVES):
        for j in range(1, half):
            held = w_out_at(1 - me_y, c_from(2 * j), q)
            link(held, held, wo_s.at[3, j, q], wo_r.at[3, j, q], me_c, near).wait_recv()
            w_out_second.append(
                w_out_send(4, j, q, held, 1 - me_y, c_from(2 * j), mate, me_s)
            )
    for copy in w_out_second:
        copy.wait_recv()
    for j in range(1, half):
        away_sum = away_sum + d_attended(1 - me_y, 2 * lax.rem(lax.div(me_c, 2) + j, half), 2)
    d_away[...] = away_sum.astype(bf16)
    d_move = [
        remote(
            d_away.at[:, head_at(h)], d_att.at[rows_of(me_y, run), head_at(h)],
            ex_s.at[1 + h], ex_r.at[1 + h], me_c, near,
        )
        for h in range(groups)
    ]
    d_att[rows_of(me_y, run)] = d_attended(me_y, 0, nc).astype(bf16)
    for j in range(1, half):
        mix_chip(j)

    def back_norm(d_rot, normed, inverse, cos, sin):
        d_normed = d_rot * cos - swap_pairs(d_rot) * sin
        return inverse * (d_normed - normed * jnp.mean(d_normed * normed, -1, keepdims=True))

    def query_part(h, y):
        at = rows_of(y, run)
        d_heads = d_att[at, head_at(h)]
        share = probs[h, at]
        d_values = dot_tn(share.astype(bf16), d_heads)
        d_probs = dot_nt(d_heads, v_all[h])
        d_scores = (share * (d_probs - jnp.sum(share * d_probs, -1, keepdims=True))).astype(bf16)
        d_qrot = jnp.dot(d_scores, k_all[h], preferred_element_type=f32) * score_scale
        d_krot = dot_tn(d_scores, q_all[h, at])
        d_query = back_norm(
            d_qrot, proj[h, at, 0:HEAD], inverse_all[2 * h, at], cos_ref[at], sin_ref[at]
        )
        d_proj[at, head_at(3 * h)] = d_query.astype(bf16)
        return d_values, d_krot

    def first_half(h, _):
        d_values, d_krot = query_part(h, me_y)
        value_sum[h] = d_values
        key_sum[h] = d_krot
        return 0

    for h in range(groups):
        first_half(h, 0)

    def key_rows(h, y):
        at = rows_of(y, run)
        d_key = back_norm(
            key_sum[h, at] * score_scale, proj[h, at, HEAD : 2 * HEAD],
            inverse_all[2 * h + 1, at], cos_ref[at], sin_ref[at],
        )
        d_proj[at, head_at(3 * h + 1)] = d_key.astype(bf16)

    def second_half(h, _):
        d_values, d_krot = query_part(h, 1 - me_y)
        key_sum[h] += d_krot
        d_proj[:, head_at(3 * h + 2)] = (value_sum[h] + d_values).astype(bf16)
        key_rows(h, 1 - me_y)
        return 0

    for h in range(groups):
        d_move[h].wait_recv()
        second_half(h, 0)

    order = []
    low, high = 0, nz - 1
    for i in range(nz):
        take = (me_z - low >= high - me_z).astype(jnp.int32)
        order.append(take * low + (1 - take) * high)
        low, high = low + take, high - (1 - take)

    d_near = [[] for _ in range(nz)]

    def away(i, j):
        if i < nz - 1:
            at = (rows_of(order[i], rows), pl.ds(j * chunk, chunk))
        else:
            at = pl.ds(pl.multiple_of(me_z * rows + j * 16, 16), 16)
        d_near[i].append(
            remote(dm_away.at[at], dm_near.at[at], dmn_s.at[i, j], dmn_r.at[i, j], me_c, near)
        )

    for j in range(CHUNKS):
        part_cols = slice(j * chunk, (j + 1) * chunk)
        dm_away[:, part_cols] = dot_nt(
            d_proj[rows_of(1 - me_y, run)], w_in_all[part_cols]
        ).astype(bf16)
        away(0, j)
    for i in range(1, nz):
        for j in range(CHUNKS if i < nz - 1 else rows // 16):
            away(i, j)
    for h in range(groups):
        key_rows(h, me_y)
    for j in range(CHUNKS):
        part_cols = slice(j * chunk, (j + 1) * chunk)
        dm_here[:, part_cols] = dot_nt(
            d_proj[rows_of(me_y, run)], w_in_all[part_cols]
        ).astype(bf16)

    def lat_rows(start):
        return lat_all[pl.ds(pl.multiple_of(place(me_s) * rows + start, 16), 16)].astype(f32)

    for start in range(0, rows, 16):
        normed, inverse_std = layer_norm(lat_rows(start))
        normed_own[start : start + 16] = normed
        inverse_own[start : start + 16] = jnp.broadcast_to(inverse_std, (16, HEAD))

    chain = []
    for i in range(nz - 1):
        to = order[i]
        up = to > me_z
        dirn = 1 - up.astype(jnp.int32)
        fed = (up & (me_z > 0)) | (~up & (me_z < nz - 1))
        beside = z_seq(me_z + 1 - 2 * dirn)
        for j in range(CHUNKS):
            at = (rows_of(to, rows), pl.ds(j * chunk, chunk))
            d_near[i][j].wait_recv()
            hop = link(
                dm_sum.at[at], chain_in.at[(dirn,) + at], ch_s.at[dirn, to, j],
                ch_r.at[dirn, to, j], me_c, beside,
            )
            value = dm_here[at].astype(f32) + dm_near[at].astype(f32)

            @pl.when(fed)
            def _():
                hop.wait_recv()
                dm_sum[at] = (value + chain_in[(dirn,) + at].astype(f32)).astype(bf16)

            @pl.when(~fed)
            def _():
                dm_sum[at] = value.astype(bf16)

            hop.start()
            chain.append(hop)

    for copy in mixed:
        copy.wait_recv()
    leave = []
    for start in range(0, rows, 16):
        mine_at = pl.ds(pl.multiple_of(me_z * rows + start, 16), 16)
        latent_rows = lat_rows(start)
        for c in range(nc):
            value = mix_out[c, mine_at].astype(f32)
            for k in range(1, nz):
                value = value + mix_in[lax.rem(me_z + k, nz), c, start : start + 16].astype(f32)
            part_cols = slice(c * piece, (c + 1) * piece)
            block_own[start : start + 16, part_cols] = (
                latent_rows[:, part_cols] + vecs[2, :, part_cols] * value
            ).astype(bf16)
    leave.append(pltpu.make_async_copy(block_own, block_ref, out_sem.at[0]))
    leave[0].start()

    total[...] = dm_here[rows_of(me_z, rows)].astype(f32)
    for dirn, fed in ((0, me_z > 0), (1, me_z < nz - 1)):
        @pl.when(fed)
        def _():
            for j in range(CHUNKS):
                part_cols = pl.ds(j * chunk, chunk)
                landed = chain_in.at[dirn, rows_of(me_z, rows), part_cols]
                link(
                    landed, landed, ch_s.at[dirn, me_z, j], ch_r.at[dirn, me_z, j], me_c, near
                ).wait_recv()
                total[:, part_cols] += landed[...].astype(f32)

    for j in range(rows // 16):
        at = slice(16 * j, 16 * j + 16)
        mine_at = pl.ds(pl.multiple_of(me_z * rows + 16 * j, 16), 16)
        d_near[nz - 1][j].wait_recv()
        d_normed = (total[at] + dm_near[mine_at].astype(f32)) * (1.0 + vecs[1])
        normed = normed_own[at]
        grad_own[at] = cot_all[mine_at].astype(f32) + inverse_own[at, 0:1] * (
            d_normed
            - jnp.mean(d_normed, -1, keepdims=True)
            - normed * jnp.mean(d_normed * normed, -1, keepdims=True)
        )
        leave.append(
            pltpu.make_async_copy(grad_own.at[at], grad_ref.at[at], out_sem.at[1 + j])
        )
        leave[-1].start()

    for p in range(PARTS):
        for dirn in range(2):
            for hop in range(nz - 1):
                @pl.when(exists(dirn, hop) & beyond(dirn))
                def _():
                    held = lat_at(source(dirn, hop), me_y, p)
                    z_send(dirn, hop, p, held, source(dirn, hop)).wait_send()
                    held = cot_at(source(dirn, hop), p)
                    cot_send(dirn, hop, p, held, source(dirn, hop)).wait_send()
            for hop in range(1, nz):
                @pl.when(exists(dirn, hop))
                def _():
                    y_link(dirn, hop, p).wait_send()
    for copy in (
        done + m1 + m2 + sum(w_in_far, []) + [w_in_mate] + w_in_second + sum(w_out_far, [])
        + w_out_mate + w_out_near + w_out_near_mate + w_out_second + w_out_cross
        + [att_move] + d_move + mixed + sum(d_near, []) + chain
    ):
        copy.wait_send()
    for copy in leave:
        copy.wait()


def hand_over(block_ref, grad_ref, block_out, grad_out, sems):
    copies = [
        pltpu.make_async_copy(block_ref, block_out, sems.at[0]),
        pltpu.make_async_copy(grad_ref, grad_out, sems.at[1]),
    ]
    for copy in copies:
        copy.start()
    for copy in copies:
        copy.wait()


def on_device(latent, timesteps, positions, mod_weight, input_weight, output_weight, cotangent):
    nc = lax.axis_size("cand")
    ns = lax.axis_size("seq")
    rows, width = latent.shape[1:]
    length = rows * ns
    slab = input_weight.shape[0]
    groups = input_weight.shape[1]
    cols = mod_weight.shape[1]
    piece = output_weight.shape[2]
    half = nc // 2
    nz = ns // 2
    run = nz * rows
    vmem = pl.BlockSpec(memory_space=pltpu.VMEM)
    smem = pl.BlockSpec(memory_space=pltpu.SMEM)
    anywhere = pl.BlockSpec(memory_space=pl.ANY)
    f32, bf16 = jnp.float32, jnp.bfloat16
    dma = pltpu.SemaphoreType.DMA
    block_out, latent_grad = pl.pallas_call(
        functools.partial(step_kernel, nc, ns),
        out_shape=(pltpu.VMEM((rows, width), bf16), pltpu.VMEM((rows, width), f32)),
        in_specs=[smem, vmem] + [anywhere] * 5,
        out_specs=(anywhere, anywhere),
        scratch_shapes=[
            pltpu.VMEM(input_weight.shape, bf16),
            pltpu.VMEM(mod_weight.shape, bf16),
            pltpu.VMEM((8, length), f32),
            pltpu.VMEM((length, HEAD), f32),
            pltpu.VMEM((length, HEAD), f32),
            pltpu.VMEM((length, HEAD), f32),
            pltpu.VMEM((nc, 1, cols), f32),
            pltpu.VMEM((nc, 1, cols), f32),
            pltpu.VMEM((1, cols), f32),
            pltpu.VMEM((ns, 1, cols), f32),
            pltpu.VMEM((3, 1, width), f32),
            pltpu.VMEM((length, width), bf16),
            pltpu.VMEM((length, width), bf16),
            pltpu.VMEM((slab * nc, groups * 3 * HEAD), bf16),
            pltpu.VMEM((2, nc, groups * HEAD, piece), bf16),
            pltpu.VMEM((run, width), bf16),
            pltpu.VMEM((nc, run, piece), bf16),
            pltpu.VMEM((groups, length, 3 * HEAD), f32),
            pltpu.VMEM((2 * groups, length, HEAD), f32),
            pltpu.VMEM((groups, length, HEAD), bf16),
            pltpu.VMEM((groups, length, HEAD), bf16),
            pltpu.VMEM((groups, length, HEAD), bf16),
            pltpu.VMEM((groups, length, length), f32),
            pltpu.VMEM((length, groups * HEAD), bf16),
            pltpu.VMEM((run, groups * HEAD), bf16),
            pltpu.VMEM((length, groups * HEAD), bf16),
            pltpu.VMEM((run, groups * HEAD), bf16),
            pltpu.VMEM((length, groups * 3 * HEAD), bf16),
            pltpu.VMEM((groups, length, HEAD), f32),
            pltpu.VMEM((groups, length, HEAD), f32),
            pltpu.VMEM((nc, run, piece), bf16),
            pltpu.VMEM((nz, nc, rows, piece), bf16),
            pltpu.VMEM((run, width), bf16),
            pltpu.VMEM((run, width), bf16),
            pltpu.VMEM((run, width), bf16),
            pltpu.VMEM((run, width), bf16),
            pltpu.VMEM((2, run, width), bf16),
            pltpu.VMEM((rows, width), f32),
            pltpu.VMEM((rows, width), f32),
            pltpu.VMEM((rows, HEAD), f32),
            pltpu.VMEM((rows, width), bf16),
            pltpu.VMEM((rows, width), f32),
            dma((1 + rows // 16,)),
            dma((5,)),
            dma((2, nz, PARTS)), dma((2, nz, PARTS)),
            dma((2 * nz, PARTS)), dma((2 * nz, PARTS)),
            dma((half, SLABS)), dma((half, SLABS)), dma((half, SLABS)), dma((half, SLABS)),
            dma((5, half, HALVES)), dma((5, half, HALVES)), dma((nc,)), dma((nc,)), dma((ns,)), dma((ns,)),
            dma((2, nz, PARTS)), dma((2, nz, PARTS)), dma((1 + groups,)), dma((1 + groups,)), dma((nz, half)), dma((nz, half)),
            dma((nz, max(CHUNKS, rows // 16))), dma((nz, max(CHUNKS, rows // 16))), dma((2, nz, CHUNKS)), dma((2, nz, CHUNKS)),
        ],
        compiler_params=pltpu.CompilerParams(
            collective_id=0, has_side_effects=True, vmem_limit_bytes=60000000
        ),
    )(
        timesteps, positions, mod_weight, latent[0], cotangent[0],
        input_weight,
        output_weight.reshape(groups * HEAD, piece),
    )
    block_out, latent_grad = pl.pallas_call(
        hand_over,
        out_shape=(
            jax.ShapeDtypeStruct((rows, width), bf16),
            jax.ShapeDtypeStruct((rows, width), f32),
        ),
        in_specs=[anywhere] * 2,
        out_specs=(anywhere, anywhere),
        scratch_shapes=[dma((2,))],
        compiler_params=pltpu.CompilerParams(vmem_limit_bytes=1000000),
    )(block_out, latent_grad)
    return (block_out[None], latent_grad[None])


def solution(mesh):
    placed = (
        P("cand", "seq", None),
        P(),
        P(),
        P("cand", "seq"),
        P("cand", "seq", None),
        P("seq", None, "cand"),
        P("cand", "seq", None),
    )
    return jax.shard_map(
        on_device,
        mesh=mesh,
        in_specs=placed,
        out_specs=(P("cand", "seq", None), P("cand", "seq", None)),
        check_vma=False,
    )
```

```python
import functools
import math

import jax
import jax.numpy as jnp
from jax import lax
from jax.experimental import pallas as pl
from jax.experimental.pallas import tpu as pltpu
from jax.sharding import PartitionSpec as P

HEAD = 128
CHUNKS = 4
PARTS = 3
SLABS = 6
HALVES = 2
MESH = pl.DeviceIdType.MESH


epsilon = 1e-06


def swap_pairs(values):
    lane = lax.broadcasted_iota(jnp.int32, values.shape, 1)
    small = HEAD // 8
    large = (HEAD - small) // 2
    near = jnp.where(
        lane < small // 2,
        pltpu.roll(values, HEAD - small // 2, 1),
        pltpu.roll(values, small // 2, 1),
    )
    upper = ((lane >= small) & (lane < small + large // 2)) | (
        (lane >= small + large) & (lane < small + large + large // 2)
    )
    far = jnp.where(
        upper, pltpu.roll(values, HEAD - large // 2, 1), pltpu.roll(values, large // 2, 1)
    )
    return jnp.where(lane < small, near, far)


def dot_nt(left, right):
    return lax.dot_general(left, right, (((1,), (1,)), ((), ())), preferred_element_type=jnp.float32)


def dot_tn(left, right):
    return lax.dot_general(left, right, (((0,), (0,)), ((), ())), preferred_element_type=jnp.float32)


def inverse_rms(values):
    return lax.rsqrt(jnp.mean(values * values, -1, keepdims=True) + epsilon)


def layer_norm(values):
    centred = values - jnp.mean(values, -1, keepdims=True)
    inverse_std = lax.rsqrt(jnp.mean(centred * centred, -1, keepdims=True) + epsilon)
    return (centred * inverse_std, inverse_std)


def sections():
    first = HEAD // 8
    other = (HEAD - first) // 2
    return ((0, first), (first, other), (first + other, other))


def step_kernel(
    nc, ns,
    time_ref, pos_ref, mod_w_ref, latent_ref, cot_ref, w_in_ref, w_out_ref,
    block_ref, grad_ref,
    w_raw, mod_w, pos8, angle, cos_ref, sin_ref, part, part_in, mine, mod_all, vecs,
    lat_all, x_all, w_in_all, w_out_all, cot_all, x_cot, proj, inverse_all, q_all, k_all, v_all, probs,
    att, att_near, d_att, d_away, d_proj, key_sum, value_sum, mix_out, mix_in,
    dm_away, dm_here, dm_near, dm_sum, chain_in, total, normed_own, inverse_own, block_own, grad_own,
    out_sem, own_sem, lat_s, lat_r, laty_s, laty_r, wi_s, wi_r, wif_s, wif_r, wo_s, wo_r, m1_s, m1_r,
    m2_s, m2_r, cot_s, cot_r, ex_s, ex_r, mx_s, mx_r, dmn_s, dmn_r, ch_s, ch_r,
):
    me_c = lax.axis_index("cand")
    me_s = lax.axis_index("seq")
    rows, width = latent_ref.shape
    length = rows * ns
    slab = w_in_ref.shape[0]
    groups = q_all.shape[0]
    cols = mod_w_ref.shape[1]
    piece = w_out_ref.shape[1]
    chunk = width // CHUNKS
    half = nc // 2
    core = lax.rem(me_c, 2)
    mate = me_c + 1 - 2 * core
    nz = ns // 2
    me_y, me_z = lax.rem(me_s, 2), lax.div(me_s, 2)
    near = me_s + 1 - 2 * me_y
    score_scale = HEAD ** (-0.5)
    size = rows // PARTS
    span = slab // SLABS
    run = nz * rows
    f32, bf16 = jnp.float32, jnp.bfloat16

    def place(index):
        return lax.rem(index, 2) * nz + lax.div(index, 2)

    def rows_of(index, count):
        return pl.ds(pl.multiple_of(index * count, count), count)

    def link(src, dst, send, recv, cand, seq):
        return pltpu.make_async_remote_copy(
            src_ref=src, dst_ref=dst, send_sem=send, recv_sem=recv,
            device_id=(cand, seq), device_id_type=MESH,
        )

    def remote(*args):
        copy = link(*args)
        copy.start()
        return copy

    def c_peer(k):
        return lax.rem(me_c + k, nc)

    def c_from(k):
        return lax.rem(me_c - k + nc, nc)

    def z_seq(z):
        return 2 * z + me_y

    barrier = pltpu.get_barrier_semaphore()
    for k in range(1, nc):
        pl.semaphore_signal(barrier, inc=1, device_id=(c_peer(k), me_s), device_id_type=MESH)
    for k in range(1, ns):
        pl.semaphore_signal(
            barrier, inc=1, device_id=(me_c, lax.rem(me_s + k, ns)), device_id_type=MESH
        )

    def w_in_at(index, q):
        return w_in_all.at[pl.ds(pl.multiple_of(index * slab + q * span, span), span)]

    own = [
        pltpu.make_async_copy(mod_w_ref, mod_w, own_sem.at[0]),
        pltpu.make_async_copy(latent_ref, lat_all.at[rows_of(place(me_s), rows)], own_sem.at[1]),
        pltpu.make_async_copy(cot_ref, cot_all.at[rows_of(me_z, rows)], own_sem.at[2]),
        pltpu.make_async_copy(w_in_ref, w_raw, own_sem.at[3]),
        pltpu.make_async_copy(w_out_ref, w_out_all.at[me_y, me_c], own_sem.at[4]),
    ]
    for copy in own:
        copy.start()
    tile = 3 * HEAD

    def flatten(i, _):
        at = pl.ds(pl.multiple_of(me_c * slab + i * 16, 16), 16)
        for h in range(groups):
            w_in_all[at, h * tile : (h + 1) * tile] = w_raw[
                pl.ds(pl.multiple_of(i * 16, 16), 16), h
            ]
        return 0

    def flatten_part(q):
        lax.fori_loop(q * span // 16, (q + 1) * span // 16, flatten, 0)

    own[3].wait()
    flatten_part(0)
    pl.semaphore_wait(barrier, nc - 1 + ns - 1)

    def lat_at(z, y, p):
        return lat_all.at[pl.ds(pl.multiple_of((y * nz + z) * rows + p * size, size), size)]

    done = []

    def z_send(dirn, hop, p, src, z):
        to = me_z + 1 - 2 * dirn
        return link(
            src, lat_at(z, me_y, p), lat_s.at[dirn, hop, p], lat_r.at[dirn, hop, p],
            me_c, z_seq(to),
        )

    for p in range(PARTS):
        src = latent_ref.at[pl.ds(p * size, size)]
        for dirn, there in ((0, me_z < nz - 1), (1, me_z > 0)):
            @pl.when(there)
            def _():
                z_send(dirn, 0, p, src, me_z).start()
        done.append(
            remote(src, lat_at(me_z, me_y, p), laty_s.at[0, p], laty_r.at[0, p], me_c, near)
        )

    def slab_part(q):
        src = w_in_at(me_c, q)
        return [
            remote(src, w_in_at(me_c, q), wi_s.at[j, q], wi_r.at[j, q], c_peer(2 * j), me_s)
            for j in range(1, half)
        ]

    w_in_far = [slab_part(0)]

    count = part.shape[0]
    lead = mod_w_ref.shape[0]
    held_rows = max(16, nc)
    index = me_c * lead + lax.broadcasted_iota(jnp.int32, (held_rows, lead), 1)
    steps = width // 2
    is_cos = index < steps
    order = jnp.where(is_cos, index, index - steps).astype(f32)
    row = lax.broadcasted_iota(jnp.int32, (held_rows, 1), 0)
    times = jnp.zeros((held_rows, 1), f32)
    for c in range(nc):
        times = jnp.where(row == c, time_ref[c].astype(f32), times)
    turns = times * jnp.exp(order * (-math.log(10000.0)) / steps)
    wave = jnp.where(is_cos, jnp.cos(turns), jnp.sin(turns))
    act = (wave / (1.0 + jnp.exp(-wave))).astype(bf16)
    own[0].wait()
    product = jnp.dot(act, mod_w[...], preferred_element_type=f32)
    for c in range(count):
        part[c] = product[c : c + 1]
    m1 = []
    for k in range(1, nc):
        peer = c_peer(k)
        m1.append(remote(part.at[peer], part_in.at[me_c], m1_s.at[k], m1_r.at[k], peer, me_s))
    for q in range(1, SLABS):
        flatten_part(q)
        w_in_far.append(slab_part(q))
    w_in_mate = remote(
        w_in_all.at[rows_of(me_c, slab)], w_in_all.at[rows_of(me_c, slab)], wif_s.at[0, 0],
        wif_r.at[0, 0], mate, me_s
    )

    part_rows = w_out_ref.shape[0] // HALVES

    def w_out_at(y, c, q):
        return w_out_all.at[y, c, pl.ds(q * part_rows, part_rows)]

    def w_out_send(kind, j, q, src, y, c, cand, seq):
        return remote(
            src, w_out_at(y, c, q), wo_s.at[kind, j, q], wo_r.at[kind, j, q], cand, seq
        )

    def w_out_own(q):
        return w_out_ref.at[pl.ds(q * part_rows, part_rows)]

    w_out_far = [
        [
            w_out_send(0, j, q, w_out_own(q), me_y, me_c, c_peer(2 * j), me_s)
            for j in range(1, half)
        ]
        for q in range(HALVES)
    ]
    w_out_mate = [
        w_out_send(0, 0, q, w_out_own(q), me_y, me_c, mate, me_s) for q in range(HALVES)
    ]

    pos8[...] = jnp.zeros_like(pos8)
    pos8[0 : pos_ref.shape[0]] = pos_ref[...].astype(f32)
    lane = lax.broadcasted_iota(jnp.int32, (8, HEAD), 1)
    axis = lax.broadcasted_iota(jnp.int32, (8, HEAD), 0)
    rate = jnp.zeros((8, HEAD), f32)
    sign = jnp.ones((8, HEAD), f32)
    for a, (start, extent) in enumerate(sections()):
        inside = (lane >= start) & (lane < start + extent)
        late = inside & (lane >= start + extent // 2)
        pair = jnp.where(late, lane - start - extent // 2, lane - start).astype(f32)
        value = jnp.exp(pair * (-math.log(256.0) * 2.0 / extent))
        rate = jnp.where(inside & (axis == a), value, rate)
        sign = jnp.where(inside & ~late, -1.0, sign)
    angle[...] = lax.dot_general(
        pos8[...], rate, (((0,), (0,)), ((), ())), preferred_element_type=f32,
        precision=lax.Precision.HIGHEST,
    )

    def turn_rows(s, _):
        turned = angle[rows_of(s, rows)]
        at = rows_of(place(s), rows)
        cos_ref[at] = jnp.cos(turned)
        sin_ref[at] = jnp.sin(turned) * sign[0:1]
        return 0

    lax.fori_loop(0, ns, turn_rows, 0)

    def exists(dirn, hop):
        return me_z >= hop if dirn == 0 else me_z <= nz - 1 - hop

    def beyond(dirn):
        return me_z < nz - 1 if dirn == 0 else me_z > 0

    def source(dirn, hop):
        return me_z - hop if dirn == 0 else me_z + hop

    def y_slot(dirn, hop):
        return hop if dirn == 0 else nz - 1 + hop

    def y_link(dirn, hop, p):
        held = lat_at(source(dirn, hop), me_y, p)
        slot = y_slot(dirn, hop)
        return link(held, held, laty_s.at[slot, p], laty_r.at[slot, p], me_c, near)

    def relay(hop):
        for p in range(PARTS):
            for dirn in range(2):
                @pl.when(exists(dirn, hop))
                def _():
                    z = source(dirn, hop)
                    held = lat_at(z, me_y, p)
                    z_send(dirn, hop - 1, p, held, z).wait_recv()
                    if hop < nz - 1:
                        @pl.when(beyond(dirn))
                        def _():
                            z_send(dirn, hop, p, held, z).start()
                    y_link(dirn, hop, p).start()

    relay(1)
    for copy in m1:
        copy.wait_recv()
    summed_mod = part[me_c]
    for k in range(1, nc):
        summed_mod = summed_mod + part_in[c_from(k)]
    mine[...] = summed_mod
    mod_all[me_s] = summed_mod
    m2 = [
        remote(
            mine, mod_all.at[me_s], m2_s.at[k], m2_r.at[k], me_c, lax.rem(me_s + k, ns)
        )
        for k in range(1, ns)
    ]
    for hop in range(2, nz - 1):
        relay(hop)

    def cot_at(z, p):
        return cot_all.at[pl.ds(pl.multiple_of(z * rows + p * size, size), size)]

    def cot_send(dirn, hop, p, src, z):
        return link(
            src, cot_at(z, p), cot_s.at[dirn, hop, p], cot_r.at[dirn, hop, p],
            me_c, z_seq(me_z + 1 - 2 * dirn),
        )

    for p in range(PARTS):
        for dirn in range(2):
            @pl.when(beyond(dirn))
            def _():
                cot_send(dirn, 0, p, cot_ref.at[pl.ds(p * size, size)], me_z).start()

    def cot_relay(hop):
        for p in range(PARTS):
            for dirn in range(2):
                @pl.when(exists(dirn, hop))
                def _():
                    z = source(dirn, hop)
                    cot_send(dirn, hop - 1, p, cot_at(z, p), z).wait_recv()
                    if hop < nz - 1:
                        @pl.when(beyond(dirn))
                        def _():
                            cot_send(dirn, hop, p, cot_at(z, p), z).start()

    def gate_rows(z):
        def body(index, _):
            at = pl.ds(pl.multiple_of(z * rows + index * 16, 16), 16)
            gated = (cot_all[at].astype(f32) * vecs[2]).astype(bf16)
            for c in range(nc):
                x_cot[c, at] = gated[:, c * piece : (c + 1) * piece]
            return 0

        lax.fori_loop(0, rows // 16, body, 0)

    def gate_hop(hop):
        for dirn in range(2):
            @pl.when(exists(dirn, hop))
            def _():
                gate_rows(source(dirn, hop))

    for copy in m2:
        copy.wait_recv()
    for s in range(ns):
        at = s * cols
        while at < (s + 1) * cols:
            kind = at // width
            stop = min((s + 1) * cols, (kind + 1) * width)
            vecs[kind, :, at - kind * width : stop - kind * width] = mod_all[
                s, :, at - s * cols : stop - s * cols
            ]
            at = stop

    def norm_rows(at):
        normed, _inverse = layer_norm(lat_all[at].astype(f32))
        x_all[at] = (normed * (1.0 + vecs[1]) + vecs[0]).astype(bf16)

    def norm_run(start, count):
        def body(i, _):
            norm_rows(pl.ds(pl.multiple_of(start + i * 16, 16), 16))
            return 0

        lax.fori_loop(0, count // 16, body, 0, unroll=True)

    own[1].wait()
    norm_run(place(me_s) * rows, rows)
    for dirn in range(2):
        for hop in range(1, nz - 1):
            @pl.when(exists(dirn, hop))
            def _():
                norm_run((me_y * nz + source(dirn, hop)) * rows, rows)

    if nz > 1:
        relay(nz - 1)
        for dirn in range(2):
            @pl.when(exists(dirn, nz - 1))
            def _():
                norm_run((me_y * nz + source(dirn, nz - 1)) * rows, rows)

    w_out_near = [
        w_out_send(1, 0, q, w_out_own(q), me_y, me_c, me_c, near) for q in range(HALVES)
    ]

    w_in_second = []

    def slab_forward(q):
        for j in range(1, half):
            w_in_far[q][j - 1].wait_recv()
            held = w_in_at(c_from(2 * j), q)
            w_in_second.append(
                remote(held, held, wif_s.at[j, q], wif_r.at[j, q], mate, me_s)
            )

    for q in range(SLABS - 1):
        slab_forward(q)
    for copy in done:
        copy.wait_recv()
    norm_run(((1 - me_y) * nz + me_z) * rows, rows)
    for hop in range(1, nz):
        if hop == nz - 1:
            if nz > 2:
                cot_relay(1)
            slab_forward(SLABS - 1)
        for dirn in range(2):
            @pl.when(exists(dirn, hop))
            def _():
                for p in range(PARTS):
                    y_link(dirn, hop, p).wait_recv()
                norm_run(((1 - me_y) * nz + source(dirn, hop)) * rows, rows)
    w_in_mate.wait_recv()
    for copy in w_in_second:
        copy.wait_recv()

    def project(index, _):
        at = pl.ds(pl.multiple_of(index * tile, tile), tile)
        proj[index] = jnp.dot(x_all[...], w_in_all[:, at], preferred_element_type=f32)
        return 0

    lax.fori_loop(0, groups, project, 0)
    for hop in range(2, nz - 1):
        cot_relay(hop)

    def head_at(h):
        return pl.ds(h * HEAD, HEAD)

    def head_forward(h, _):
        query = proj[h, :, 0:HEAD]
        key = proj[h, :, HEAD : 2 * HEAD]
        query_inverse = inverse_rms(query)
        key_inverse = inverse_rms(key)
        query_n = query * query_inverse
        key_n = key * key_inverse
        proj[h, :, 0:HEAD] = query_n
        proj[h, :, HEAD : 2 * HEAD] = key_n
        inverse_all[2 * h] = jnp.broadcast_to(query_inverse, query.shape)
        inverse_all[2 * h + 1] = jnp.broadcast_to(key_inverse, key.shape)
        q_rot = (query_n * cos_ref[...] + swap_pairs(query_n) * sin_ref[...]).astype(bf16)
        k_rot = (key_n * cos_ref[...] + swap_pairs(key_n) * sin_ref[...]).astype(bf16)
        values = proj[h, :, 2 * HEAD :].astype(bf16)
        q_all[h] = q_rot
        k_all[h] = k_rot
        v_all[h] = values
        weights = jnp.exp(dot_nt(q_rot, k_rot) * score_scale - HEAD**0.5)
        share = weights * (1.0 / jnp.sum(weights, -1, keepdims=True))
        probs[h] = share
        att[:, head_at(h)] = jnp.dot(
            share.astype(bf16), values, preferred_element_type=f32
        ).astype(bf16)
        return 0

    for h in range(groups):
        head_forward(h, 0)
    att_move = remote(
        att.at[rows_of(1 - me_y, run)], att_near, ex_s.at[0], ex_r.at[0], me_c, near
    )

    def att_rows(which):
        return att[rows_of(me_y, run)] if which == 0 else att_near[...]

    mixed = []

    def mix_chip(j):
        first = 2 * lax.rem(lax.div(me_c, 2) + j, half)
        for b in range(2):
            mix_out[first + b] = (
                jnp.dot(att_rows(0), w_out_all[me_y, first + b], preferred_element_type=f32)
                + jnp.dot(att_rows(1), w_out_all[1 - me_y, first + b], preferred_element_type=f32)
            ).astype(bf16)
        for k in range(1, nz):
            peer = lax.rem(me_z + k, nz)
            mixed.append(
                remote(
                    mix_out.at[pl.ds(first, 2), rows_of(peer, rows)],
                    mix_in.at[me_z, pl.ds(first, 2)],
                    mx_s.at[k, j], mx_r.at[k, j], me_c, z_seq(peer),
                )
            )

    w_out_second = []
    w_out_cross = []
    w_out_near_mate = []
    for q in range(HALVES):
        w_out_near[q].wait_recv()
        w_out_near_mate.append(
            w_out_send(2, 0, q, w_out_at(1 - me_y, me_c, q), 1 - me_y, me_c, mate, me_s)
        )
        for j in range(1, half):
            w_out_far[q][j - 1].wait_recv()
            from_y = jnp.where(core == 0, me_y, 1 - me_y)
            from_c = jnp.where(core == 0, c_from(2 * j), me_c)
            w_out_cross.append(
                w_out_send(
                    3, j, q, w_out_at(from_y, from_c, q), from_y, from_c,
                    jnp.where(core == 0, me_c, c_peer(2 * j)), jnp.where(core == 0, near, me_s),
                )
            )
            w_out_second.append(
                w_out_send(
                    2, j, q, w_out_at(me_y, c_from(2 * j), q), me_y, c_from(2 * j), mate, me_s
                )
            )

    own[4].wait()
    for copy in w_out_mate + [att_move] + w_out_near_mate:
        copy.wait_recv()
    mix_chip(0)

    own[2].wait()
    gate_rows(me_z)
    for hop in range(1, nz - 1):
        gate_hop(hop)
    cot_relay(nz - 1)
    gate_hop(nz - 1)

    def d_attended(y, first, count):
        block = jnp.zeros((run, groups * HEAD), f32)
        for i in range(count):
            c = first + i
            block = block + dot_nt(x_cot[c], w_out_all[y, c])
        return block

    chip = 2 * lax.div(me_c, 2)
    away_sum = d_attended(1 - me_y, chip, 2)
    for q in range(HALVES):
        for j in range(1, half):
            held = w_out_at(1 - me_y, c_from(2 * j), q)
            link(held, held, wo_s.at[3, j, q], wo_r.at[3, j, q], me_c, near).wait_recv()
            w_out_second.append(
                w_out_send(4, j, q, held, 1 - me_y, c_from(2 * j), mate, me_s)
            )
    for copy in w_out_second:
        copy.wait_recv()
    for j in range(1, half):
        away_sum = away_sum + d_attended(1 - me_y, 2 * lax.rem(lax.div(me_c, 2) + j, half), 2)
    d_away[...] = away_sum.astype(bf16)
    d_move = [
        remote(
            d_away.at[:, head_at(h)], d_att.at[rows_of(me_y, run), head_at(h)],
            ex_s.at[1 + h], ex_r.at[1 + h], me_c, near,
        )
        for h in range(groups)
    ]
    d_att[rows_of(me_y, run)] = d_attended(me_y, 0, nc).astype(bf16)
    for j in range(1, half):
        mix_chip(j)

    def back_norm(d_rot, normed, inverse, cos, sin):
        d_normed = d_rot * cos - swap_pairs(d_rot) * sin
        return inverse * (d_normed - normed * jnp.mean(d_normed * normed, -1, keepdims=True))

    def query_part(h, y):
        at = rows_of(y, run)
        d_heads = d_att[at, head_at(h)]
        share = probs[h, at]
        d_values = dot_tn(share.astype(bf16), d_heads)
        d_probs = dot_nt(d_heads, v_all[h])
        d_scores = (share * (d_probs - jnp.sum(share * d_probs, -1, keepdims=True))).astype(bf16)
        d_qrot = jnp.dot(d_scores, k_all[h], preferred_element_type=f32) * score_scale
        d_krot = dot_tn(d_scores, q_all[h, at])
        d_query = back_norm(
            d_qrot, proj[h, at, 0:HEAD], inverse_all[2 * h, at], cos_ref[at], sin_ref[at]
        )
        d_proj[at, head_at(3 * h)] = d_query.astype(bf16)
        return d_values, d_krot

    def first_half(h, _):
        d_values, d_krot = query_part(h, me_y)
        value_sum[h] = d_values
        key_sum[h] = d_krot
        return 0

    for h in range(groups):
        first_half(h, 0)

    def key_rows(h, y):
        at = rows_of(y, run)
        d_key = back_norm(
            key_sum[h, at] * score_scale, proj[h, at, HEAD : 2 * HEAD],
            inverse_all[2 * h + 1, at], cos_ref[at], sin_ref[at],
        )
        d_proj[at, head_at(3 * h + 1)] = d_key.astype(bf16)

    def second_half(h, _):
        d_values, d_krot = query_part(h, 1 - me_y)
        key_sum[h] += d_krot
        d_proj[:, head_at(3 * h + 2)] = (value_sum[h] + d_values).astype(bf16)
        key_rows(h, 1 - me_y)
        return 0

    for h in range(groups):
        d_move[h].wait_recv()
        second_half(h, 0)

    order = []
    low, high = 0, nz - 1
    for i in range(nz):
        take = (me_z - low >= high - me_z).astype(jnp.int32)
        order.append(take * low + (1 - take) * high)
        low, high = low + take, high - (1 - take)

    d_near = [[] for _ in range(nz)]

    def away(i, j):
        if i < nz - 1:
            at = (rows_of(order[i], rows), pl.ds(j * chunk, chunk))
        else:
            at = pl.ds(pl.multiple_of(me_z * rows + j * 16, 16), 16)
        d_near[i].append(
            remote(dm_away.at[at], dm_near.at[at], dmn_s.at[i, j], dmn_r.at[i, j], me_c, near)
        )

    for j in range(CHUNKS):
        part_cols = slice(j * chunk, (j + 1) * chunk)
        dm_away[:, part_cols] = dot_nt(
            d_proj[rows_of(1 - me_y, run)], w_in_all[part_cols]
        ).astype(bf16)
        away(0, j)
    for i in range(1, nz):
        for j in range(CHUNKS if i < nz - 1 else rows // 16):
            away(i, j)
    for h in range(groups):
        key_rows(h, me_y)
    for j in range(CHUNKS):
        part_cols = slice(j * chunk, (j + 1) * chunk)
        dm_here[:, part_cols] = dot_nt(
            d_proj[rows_of(me_y, run)], w_in_all[part_cols]
        ).astype(bf16)

    def lat_rows(start):
        return lat_all[pl.ds(pl.multiple_of(place(me_s) * rows + start, 16), 16)].astype(f32)

    for start in range(0, rows, 16):
        normed, inverse_std = layer_norm(lat_rows(start))
        normed_own[start : start + 16] = normed
        inverse_own[start : start + 16] = jnp.broadcast_to(inverse_std, (16, HEAD))

    chain = []
    for i in range(nz - 1):
        to = order[i]
        up = to > me_z
        dirn = 1 - up.astype(jnp.int32)
        fed = (up & (me_z > 0)) | (~up & (me_z < nz - 1))
        beside = z_seq(me_z + 1 - 2 * dirn)
        for j in range(CHUNKS):
            at = (rows_of(to, rows), pl.ds(j * chunk, chunk))
            d_near[i][j].wait_recv()
            hop = link(
                dm_sum.at[at], chain_in.at[(dirn,) + at], ch_s.at[dirn, to, j],
                ch_r.at[dirn, to, j], me_c, beside,
            )
            value = dm_here[at].astype(f32) + dm_near[at].astype(f32)

            @pl.when(fed)
            def _():
                hop.wait_recv()
                dm_sum[at] = (value + chain_in[(dirn,) + at].astype(f32)).astype(bf16)

            @pl.when(~fed)
            def _():
                dm_sum[at] = value.astype(bf16)

            hop.start()
            chain.append(hop)

    for copy in mixed:
        copy.wait_recv()
    leave = []
    for start in range(0, rows, 16):
        mine_at = pl.ds(pl.multiple_of(me_z * rows + start, 16), 16)
        latent_rows = lat_rows(start)
        for c in range(nc):
            value = mix_out[c, mine_at].astype(f32)
            for k in range(1, nz):
                value = value + mix_in[lax.rem(me_z + k, nz), c, start : start + 16].astype(f32)
            part_cols = slice(c * piece, (c + 1) * piece)
            block_own[start : start + 16, part_cols] = (
                latent_rows[:, part_cols] + vecs[2, :, part_cols] * value
            ).astype(bf16)
    leave.append(pltpu.make_async_copy(block_own, block_ref, out_sem.at[0]))
    leave[0].start()

    total[...] = dm_here[rows_of(me_z, rows)].astype(f32)
    for dirn, fed in ((0, me_z > 0), (1, me_z < nz - 1)):
        @pl.when(fed)
        def _():
            for j in range(CHUNKS):
                part_cols = pl.ds(j * chunk, chunk)
                landed = chain_in.at[dirn, rows_of(me_z, rows), part_cols]
                link(
                    landed, landed, ch_s.at[dirn, me_z, j], ch_r.at[dirn, me_z, j], me_c, near
                ).wait_recv()
                total[:, part_cols] += landed[...].astype(f32)

    for j in range(rows // 16):
        at = slice(16 * j, 16 * j + 16)
        mine_at = pl.ds(pl.multiple_of(me_z * rows + 16 * j, 16), 16)
        d_near[nz - 1][j].wait_recv()
        d_normed = (total[at] + dm_near[mine_at].astype(f32)) * (1.0 + vecs[1])
        normed = normed_own[at]
        grad_own[at] = cot_all[mine_at].astype(f32) + inverse_own[at, 0:1] * (
            d_normed
            - jnp.mean(d_normed, -1, keepdims=True)
            - normed * jnp.mean(d_normed * normed, -1, keepdims=True)
        )
        leave.append(
            pltpu.make_async_copy(grad_own.at[at], grad_ref.at[at], out_sem.at[1 + j])
        )
        leave[-1].start()

    for p in range(PARTS):
        for dirn in range(2):
            for hop in range(nz - 1):
                @pl.when(exists(dirn, hop) & beyond(dirn))
                def _():
                    held = lat_at(source(dirn, hop), me_y, p)
                    z_send(dirn, hop, p, held, source(dirn, hop)).wait_send()
                    held = cot_at(source(dirn, hop), p)
                    cot_send(dirn, hop, p, held, source(dirn, hop)).wait_send()
            for hop in range(1, nz):
                @pl.when(exists(dirn, hop))
                def _():
                    y_link(dirn, hop, p).wait_send()
    for copy in (
        done + m1 + m2 + sum(w_in_far, []) + [w_in_mate] + w_in_second + sum(w_out_far, [])
        + w_out_mate + w_out_near + w_out_near_mate + w_out_second + w_out_cross
        + [att_move] + d_move + mixed + sum(d_near, []) + chain
    ):
        copy.wait_send()
    for copy in leave:
        copy.wait()


def hand_over(block_ref, grad_ref, block_out, grad_out, sems):
    copies = [
        pltpu.make_async_copy(block_ref, block_out, sems.at[0]),
        pltpu.make_async_copy(grad_ref, grad_out, sems.at[1]),
    ]
    for copy in copies:
        copy.start()
    for copy in copies:
        copy.wait()


def on_device(latent, timesteps, positions, mod_weight, input_weight, output_weight, cotangent):
    nc = lax.axis_size("cand")
    ns = lax.axis_size("seq")
    rows, width = latent.shape[1:]
    length = rows * ns
    slab = input_weight.shape[0]
    groups = input_weight.shape[1]
    cols = mod_weight.shape[1]
    piece = output_weight.shape[2]
    half = nc // 2
    nz = ns // 2
    run = nz * rows
    vmem = pl.BlockSpec(memory_space=pltpu.VMEM)
    smem = pl.BlockSpec(memory_space=pltpu.SMEM)
    anywhere = pl.BlockSpec(memory_space=pl.ANY)
    f32, bf16 = jnp.float32, jnp.bfloat16
    dma = pltpu.SemaphoreType.DMA
    block_out, latent_grad = pl.pallas_call(
        functools.partial(step_kernel, nc, ns),
        out_shape=(pltpu.VMEM((rows, width), bf16), pltpu.VMEM((rows, width), f32)),
        in_specs=[smem, vmem] + [anywhere] * 5,
        out_specs=(anywhere, anywhere),
        scratch_shapes=[
            pltpu.VMEM(input_weight.shape, bf16),
            pltpu.VMEM(mod_weight.shape, bf16),
            pltpu.VMEM((8, length), f32),
            pltpu.VMEM((length, HEAD), f32),
            pltpu.VMEM((length, HEAD), f32),
            pltpu.VMEM((length, HEAD), f32),
            pltpu.VMEM((nc, 1, cols), f32),
            pltpu.VMEM((nc, 1, cols), f32),
            pltpu.VMEM((1, cols), f32),
            pltpu.VMEM((ns, 1, cols), f32),
            pltpu.VMEM((3, 1, width), f32),
            pltpu.VMEM((length, width), bf16),
            pltpu.VMEM((length, width), bf16),
            pltpu.VMEM((slab * nc, groups * 3 * HEAD), bf16),
            pltpu.VMEM((2, nc, groups * HEAD, piece), bf16),
            pltpu.VMEM((run, width), bf16),
            pltpu.VMEM((nc, run, piece), bf16),
            pltpu.VMEM((groups, length, 3 * HEAD), f32),
            pltpu.VMEM((2 * groups, length, HEAD), f32),
            pltpu.VMEM((groups, length, HEAD), bf16),
            pltpu.VMEM((groups, length, HEAD), bf16),
            pltpu.VMEM((groups, length, HEAD), bf16),
            pltpu.VMEM((groups, length, length), f32),
            pltpu.VMEM((length, groups * HEAD), bf16),
            pltpu.VMEM((run, groups * HEAD), bf16),
            pltpu.VMEM((length, groups * HEAD), bf16),
            pltpu.VMEM((run, groups * HEAD), bf16),
            pltpu.VMEM((length, groups * 3 * HEAD), bf16),
            pltpu.VMEM((groups, length, HEAD), f32),
            pltpu.VMEM((groups, length, HEAD), f32),
            pltpu.VMEM((nc, run, piece), bf16),
            pltpu.VMEM((nz, nc, rows, piece), bf16),
            pltpu.VMEM((run, width), bf16),
            pltpu.VMEM((run, width), bf16),
            pltpu.VMEM((run, width), bf16),
            pltpu.VMEM((run, width), bf16),
            pltpu.VMEM((2, run, width), bf16),
            pltpu.VMEM((rows, width), f32),
            pltpu.VMEM((rows, width), f32),
            pltpu.VMEM((rows, HEAD), f32),
            pltpu.VMEM((rows, width), bf16),
            pltpu.VMEM((rows, width), f32),
            dma((1 + rows // 16,)),
            dma((5,)),
            dma((2, nz, PARTS)), dma((2, nz, PARTS)),
            dma((2 * nz, PARTS)), dma((2 * nz, PARTS)),
            dma((half, SLABS)), dma((half, SLABS)), dma((half, SLABS)), dma((half, SLABS)),
            dma((5, half, HALVES)), dma((5, half, HALVES)), dma((nc,)), dma((nc,)), dma((ns,)), dma((ns,)),
            dma((2, nz, PARTS)), dma((2, nz, PARTS)), dma((1 + groups,)), dma((1 + groups,)), dma((nz, half)), dma((nz, half)),
            dma((nz, max(CHUNKS, rows // 16))), dma((nz, max(CHUNKS, rows // 16))), dma((2, nz, CHUNKS)), dma((2, nz, CHUNKS)),
        ],
        compiler_params=pltpu.CompilerParams(
            collective_id=0, has_side_effects=True, vmem_limit_bytes=60000000
        ),
    )(
        timesteps, positions, mod_weight, latent[0], cotangent[0],
        input_weight,
        output_weight.reshape(groups * HEAD, piece),
    )
    block_out, latent_grad = pl.pallas_call(
        hand_over,
        out_shape=(
            jax.ShapeDtypeStruct((rows, width), bf16),
            jax.ShapeDtypeStruct((rows, width), f32),
        ),
        in_specs=[anywhere] * 2,
        out_specs=(anywhere, anywhere),
        scratch_shapes=[dma((2,))],
        compiler_params=pltpu.CompilerParams(vmem_limit_bytes=1000000),
    )(block_out, latent_grad)
    return (block_out[None], latent_grad[None])


def solution(mesh):
    placed = (
        P("cand", "seq", None),
        P(),
        P(),
        P("cand", "seq"),
        P("cand", "seq", None),
        P("seq", None, "cand"),
        P("cand", "seq", None),
    )
    return jax.shard_map(
        on_device,
        mesh=mesh,
        in_specs=placed,
        out_specs=(P("cand", "seq", None), P("cand", "seq", None)),
        check_vma=False,
    )
```
